256 devices in a mesh: wide: 128 (over z, y, x_hi, core), narrow: 2 (over x_lo).
Axes of the slice: x: 4 (x_hi: 2, x_lo: 2; x = x_hi * 2 + x_lo), y: 4, z: 8, core: 2. Of those that a mesh axis runs over, the one named last changes fastest.
Arguments:
- key_grads: bfloat16 [128, 2, 2, 2048, 512], P('wide', 'narrow'), may hold values from -1600 to 1600
- router_grads: bfloat16 [128, 2, 2, 64, 2048], P('wide', 'narrow'), may hold values from -1600 to 1600
- gain_grads: bfloat16 [128, 2, 2, 2048], P('wide', 'narrow'), may hold values from -1600 to 1600
- key_master: float32 [2048, 512], P('narrow'), may hold values from -3 to 3
- key_first: float32 [2048, 512], P('narrow'), may hold values from -3 to 3
- key_second: float32 [2048, 512], P('narrow'), may hold values from 0.01 to 1
- router_master: float32 [64, 2048], P(None, 'narrow'), may hold values from -3 to 3
- router_first: float32 [64, 2048], P(None, 'narrow'), may hold values from -3 to 3
- router_second: float32 [64, 2048], P(None, 'narrow'), may hold values from 0.01 to 1
- gain_master: float32 [2048], P('narrow'), may hold values from 0.5 to 1.5
- gain_first: float32 [2048], P('narrow'), may hold values from -3 to 3
- gain_second: float32 [2048], P('narrow'), may hold values from 0.01 to 1
Outputs:
- key_master_new: float32 [2048, 512], P('narrow')
- key_first_new: float32 [2048, 512], P('narrow')
- key_second_new: float32 [2048, 512], P('narrow')
- router_master_new: float32 [64, 2048], P(None, 'narrow')
- router_first_new: float32 [64, 2048], P(None, 'narrow')
- router_second_new: float32 [64, 2048], P(None, 'narrow')
- gain_master_new: float32 [2048], P('narrow')
- gain_first_new: float32 [2048], P('narrow')
- gain_second_new: float32 [2048], P('narrow')
- key_weight: bfloat16 [2048, 512], replicated
- router_weight: bfloat16 [64, 2048], replicated
- gain_weight: bfloat16 [2048], replicated
The draws below stay inside these ranges and needn't reach their ends.
All inputs are finite; a program needn't handle non-finite values.
Results may differ from the reference program's by a relative error of at most 0.002.
Values may be sent and summed in bfloat16 or wider, within the bound.
No kernel may reach another device: no remote copies, remote signals or barrier semaphores. Data moves between devices by JAX's collectives and lax.ppermute only.
A program may use at most 64 MiB of HBM per device.

```python
import math
import jax
import jax.numpy as jnp
from jax import lax

D = 2048
KEY_WIDTH = 512
EXPERTS = 64
MICRO = 2
N_WIDE = 128
N_NARROW = 2


def scaled_grads(key, leading, row_count, col_count, rows_last):
    streams = jax.random.split(key, 3)
    row_place = jnp.arange(row_count, dtype=jnp.float32) / row_count
    row_scale = jnp.exp(jax.random.uniform(streams[1], (row_count,)) * math.log(10.0)) * jnp.exp(row_place * math.log(3.0))
    col_scale = jnp.exp(jax.random.uniform(streams[2], (col_count,)) * math.log(10.0))
    if rows_last:
        trailing = (col_count, row_count)
        surface = col_scale[:, None] * row_scale[None, :]
    else:
        trailing = (row_count, col_count)
        surface = row_scale[:, None] * col_scale[None, :]
    values = jax.random.truncated_normal(streams[0], -4.0, 4.0, leading + trailing)
    return (0.3 * values * surface).astype(jnp.float32)


def draw_key_grads(key, part):
    return scaled_grads(jax.random.fold_in(key, 11), (N_WIDE, N_NARROW, MICRO), D, KEY_WIDTH, False).astype(jnp.bfloat16)


def draw_router_grads(key, part):
    return scaled_grads(jax.random.fold_in(key, 12), (N_WIDE, N_NARROW, MICRO), D, EXPERTS, True).astype(jnp.bfloat16)


def draw_gain_grads(key, part):
    produced = scaled_grads(jax.random.fold_in(key, 13), (N_WIDE, N_NARROW, MICRO), D, 1, False)
    return produced.reshape((N_WIDE, N_NARROW, MICRO, D)).astype(jnp.bfloat16)


def shard_levels(own_key, extent, shards, least, top_value):
    factor_of, own = 1.0, jax.random.fold_in(own_key, 6)
    for axis_at, blocks in shards:
        heights = jnp.exp(jax.random.uniform(jax.random.fold_in(own, axis_at), (blocks,), jnp.float32, least / len(shards), top_value / len(shards)))
        factor_of = factor_of * jnp.repeat(heights, extent[axis_at] // blocks).reshape([-1 if axis == axis_at else 1 for axis in range(len(extent))])
    return factor_of


def noise(rng, extent, scale, most, cuts=(), kind=jnp.bfloat16):
    drawn = jax.random.normal(rng, extent, jnp.float32) * scale
    if len(cuts) > 0:
        drawn = shard_levels(rng, extent, cuts, -0.22, 0.18) * drawn
    return jnp.clip(drawn, min=-most, max=most).astype(kind)


def setup_inputs(seed: int = 0) -> dict:
    key_list = jax.random.split(jax.random.key(seed), 13)
    key_grads = draw_key_grads(jax.random.fold_in(key_list[12], 71), 0)
    router_grads = draw_router_grads(jax.random.fold_in(key_list[12], 71), 0)
    gain_grads = draw_gain_grads(jax.random.fold_in(key_list[12], 71), 0)
    key_master = noise(key_list[3], (D, KEY_WIDTH), 0.5, 3.0, ((0, 2),), jnp.float32)
    key_first = noise(key_list[4], (D, KEY_WIDTH), 0.3, 3.0, ((0, 2),), jnp.float32)
    key_second = jnp.clip(jnp.exp(math.log(1.0) - 4.6051702 * jax.random.uniform(key_list[5], (D, KEY_WIDTH), jnp.float32) ** shard_levels(key_list[5], (D, KEY_WIDTH), ((0, 2),), -0.2, 0.2)), 0.01, 1.0)
    router_master = noise(key_list[6], (EXPERTS, D), 0.5, 3.0, ((1, 2),), jnp.float32)
    router_first = noise(key_list[7], (EXPERTS, D), 0.3, 3.0, ((1, 2),), jnp.float32)
    router_second = jnp.clip(jnp.exp(math.log(1.0) - 4.6051702 * jax.random.uniform(key_list[8], (EXPERTS, D), jnp.float32) ** shard_levels(key_list[8], (EXPERTS, D), ((1, 2),), -0.2, 0.2)), 0.01, 1.0)
    gain_master = jnp.clip(0.5 + 1.0 * jax.random.uniform(key_list[9], (D,), jnp.float32) ** shard_levels(key_list[9], (D,), ((0, 2),), -0.2, 0.2), 0.5, 1.5)
    gain_first = noise(key_list[10], (D,), 0.3, 3.0, ((0, 2),), jnp.float32)
    gain_second = jnp.clip(jnp.exp(math.log(1.0) - 4.6051702 * jax.random.uniform(key_list[11], (D,), jnp.float32) ** shard_levels(key_list[11], (D,), ((0, 2),), -0.2, 0.2)), 0.01, 1.0)
    return dict(key_grads=key_grads, router_grads=router_grads, gain_grads=gain_grads, key_master=key_master, key_first=key_first, key_second=key_second, router_master=router_master, router_first=router_first, router_second=router_second, gain_master=gain_master, gain_first=gain_first, gain_second=gain_second)


beta_one = 0.9
beta_two = 0.95
step_rate = 0.01
epsilon = 1e-08
bias_one = 1.0 - 0.9 ** 10
bias_two = 1.0 - 0.95 ** 10

def reduce_grads(grad_stack):

    def accumulate(summed, blocks):
        locals_sum = lax.optimization_barrier(jnp.sum(blocks.astype(jnp.float32), axis=1)).astype(jnp.bfloat16)
        return (summed + lax.optimization_barrier(jnp.sum(locals_sum.astype(jnp.float32), axis=0)), None)
    start_value = jnp.zeros(grad_stack.shape[3:], jnp.float32)
    summed, unused = lax.scan(accumulate, start_value, grad_stack)
    return summed

def adamw(master, first_moment, second, gradient, factor, decay_rate):
    scaled = factor * gradient
    first_new = beta_one * first_moment + (1.0 - beta_one) * scaled
    second_new = beta_two * second + (1.0 - beta_two) * scaled * scaled
    update = first_new / bias_one / (jnp.sqrt(second_new / bias_two) + epsilon) + decay_rate * master
    master_new = master - step_rate * update
    return (master_new, first_new, second_new)

def reference(key_grads, router_grads, gain_grads, key_master, key_first, key_second, router_master, router_first, router_second, gain_master, gain_first, gain_second):
    grad_key = reduce_grads(key_grads)
    grad_router = reduce_grads(router_grads)
    grad_gain = reduce_grads(gain_grads)
    totals = jnp.sum(grad_key * grad_key) + jnp.sum(grad_router * grad_router) + jnp.sum(grad_gain * grad_gain)
    clip_limit = 0.5 * math.sqrt(D * KEY_WIDTH + EXPERTS * D + D)
    factor = clip_limit / jnp.maximum(jnp.sqrt(totals), clip_limit)
    key_new, key_first_new, key_second_new = adamw(key_master, key_first, key_second, grad_key, factor, 0.1)
    router_new, router_first_new, router_second_new = adamw(router_master, router_first, router_second, grad_router, factor, 0.1)
    gain_new, gain_first_new, gain_second_new = adamw(gain_master, gain_first, gain_second, grad_gain, factor, 0.0)
    return (key_new, key_first_new, key_second_new, router_new, router_first_new, router_second_new, gain_new, gain_first_new, gain_second_new, key_new.astype(jnp.bfloat16), router_new.astype(jnp.bfloat16), gain_new.astype(jnp.bfloat16))
```

```python
import math

import jax
import jax.numpy as jnp
import numpy as np
from jax import lax
from jax.sharding import Mesh
from jax.sharding import PartitionSpec as P

D = 2048
KEY_WIDTH = 512
EXPERTS = 64
LANES = 128

beta_one = 0.9
beta_two = 0.95
step_rate = 0.01
epsilon = 1e-08
bias_one = 1.0 - 0.9**10
bias_two = 1.0 - 0.95**10

SWAP = [(0, 1), (1, 0)]
WIDE = ("z", "y", "xh", "c")


def micro_total(grad_stack):
    summed = jnp.sum(grad_stack.astype(jnp.float32), axis=0)
    return summed.astype(jnp.bfloat16)


def adamw(master, first_moment, second, gradient, factor, decay_rate):
    scaled = factor * gradient
    first_new = beta_one * first_moment + (1.0 - beta_one) * scaled
    second_new = beta_two * second + (1.0 - beta_two) * scaled * scaled
    update = (
        first_new / bias_one / (jnp.sqrt(second_new / bias_two) + epsilon) + decay_rate * master
    )
    master_new = master - step_rate * update
    return (master_new, first_new, second_new)


def pack(key, router, gain):
    key = key.reshape(2, 128, 8, KEY_WIDTH)
    router = router.reshape(16, 4, 2, 8, LANES).transpose(2, 0, 3, 1, 4).reshape(2, 128, 4, LANES)
    gain = jnp.pad(gain.reshape(2, 8, 1, LANES), ((0, 0), (0, 120), (0, 3), (0, 0)))
    return jnp.concatenate([key, jnp.concatenate([router, gain], axis=2)], axis=3)


def unpack(blocks):
    key = blocks[:, :, :KEY_WIDTH].reshape(1024, KEY_WIDTH)
    router = blocks[:, :4, KEY_WIDTH:].reshape(16, 8, 4, LANES)
    router = router.transpose(0, 2, 1, 3).reshape(EXPERTS, 1024)
    gain = blocks[:8, 4, KEY_WIDTH:].reshape(1024)
    return key, router, gain


def on_device(
    key_grads,
    router_grads,
    gain_grads,
    key_master,
    key_first,
    key_second,
    router_master,
    router_first,
    router_second,
    gain_master,
    gain_first,
    gain_second,
):
    core = lax.axis_index("c")
    half = lax.axis_index("xl")
    local = pack(
        micro_total(key_grads[0, 0]), micro_total(router_grads[0, 0]), micro_total(gain_grads[0, 0])
    )
    local = local.reshape(2, 2, 64, 8, 640)
    sent = lax.dynamic_index_in_dim(local, 1 - core, 1, keepdims=False)
    kept = lax.dynamic_index_in_dim(local, core, 1, keepdims=False)
    got = lax.ppermute(sent, "c", SWAP)
    pair = (kept.astype(jnp.float32) + got.astype(jnp.float32)).astype(jnp.bfloat16)
    spread = lax.all_to_all(
        pair.reshape(128, 8, 640), ("xl", "z", "y", "xh"), 0, 0, tiled=True
    )
    own = jnp.sum(spread.astype(jnp.float32), axis=0)
    largest = jnp.maximum(jnp.max(jnp.abs(own)), 1e-30)
    exponent = jnp.floor(jnp.log2(largest)) - 13.0
    scaled_own = own * jnp.exp2(-exponent)
    at = (lax.broadcasted_iota(jnp.int32, own.shape, 0) == 5) & (
        lax.broadcasted_iota(jnp.int32, own.shape, 1) == KEY_WIDTH
    )
    code = jnp.where(at, exponent, scaled_own).astype(jnp.float16)
    parts = lax.all_to_all(
        jnp.broadcast_to(code[None], (64, 8, 640)), ("z", "y", "xh"), 0, 0, tiled=True
    )
    other = lax.ppermute(parts, "c", SWAP)
    blocks = jnp.where(
        core == 0, jnp.concatenate([parts, other]), jnp.concatenate([other, parts])
    )
    blocks = blocks.astype(jnp.float32)
    blocks = blocks * jnp.exp2(blocks[:, 5:6, KEY_WIDTH : KEY_WIDTH + 1])
    key_sum, router_sum, gain_sum = unpack(blocks)
    squares = (
        jnp.sum(key_sum * key_sum) + jnp.sum(router_sum * router_sum) + jnp.sum(gain_sum * gain_sum)
    )
    squares = squares + lax.ppermute(squares, "xl", SWAP)
    clip_limit = 0.5 * math.sqrt(D * KEY_WIDTH + EXPERTS * D + D)
    factor = clip_limit / jnp.maximum(jnp.sqrt(squares), clip_limit)
    key_new, key_first_new, key_second_new = adamw(
        key_master, key_first, key_second, key_sum, factor, 0.1
    )
    router_new, router_first_new, router_second_new = adamw(
        router_master, router_first, router_second, router_sum, factor, 0.1
    )
    gain_new, gain_first_new, gain_second_new = adamw(
        gain_master, gain_first, gain_second, gain_sum, factor, 0.0
    )
    key_low = key_new.astype(jnp.bfloat16)
    router_low = router_new.astype(jnp.bfloat16)
    gain_low = gain_new.astype(jnp.bfloat16)

    def exchange(low):
        mine = lax.dynamic_index_in_dim(low, core, 0, keepdims=False)
        far = lax.ppermute(mine, "xl", SWAP)
        near = lax.ppermute(far, "c", SWAP)
        far = jnp.where(core == 0, jnp.stack([far, near]), jnp.stack([near, far]))
        return jnp.where(half == 0, jnp.stack([low, far]), jnp.stack([far, low]))

    key_weight = exchange(key_low.reshape(2, 512, 512)).reshape(D, KEY_WIDTH)
    router_weight = exchange(router_low.reshape(2, 32, 1024)).reshape(2, EXPERTS, 1024)
    router_weight = jnp.concatenate([router_weight[0], router_weight[1]], axis=1)
    gain_far = lax.ppermute(gain_low, "xl", SWAP)
    gain_weight = jnp.where(
        half == 0, jnp.concatenate([gain_low, gain_far]), jnp.concatenate([gain_far, gain_low])
    )
    return (
        key_new,
        key_first_new,
        key_second_new,
        router_new,
        router_first_new,
        router_second_new,
        gain_new,
        gain_first_new,
        gain_second_new,
        key_weight,
        router_weight,
        gain_weight,
    )


def solution(mesh):
    fine = Mesh(np.asarray(mesh.devices).reshape(8, 4, 2, 2, 2), ("z", "y", "xh", "c", "xl"))
    in_specs = (
        P(WIDE, "xl", None, None, None),
        P(WIDE, "xl", None, None, None),
        P(WIDE, "xl", None, None),
        P("xl", None),
        P("xl", None),
        P("xl", None),
        P(None, "xl"),
        P(None, "xl"),
        P(None, "xl"),
        P("xl"),
        P("xl"),
        P("xl"),
    )
    out_specs = (
        P("xl", None),
        P("xl", None),
        P("xl", None),
        P(None, "xl"),
        P(None, "xl"),
        P(None, "xl"),
        P("xl"),
        P("xl"),
        P("xl"),
        P(),
        P(),
        P(),
    )
    return jax.shard_map(
        on_device, mesh=fine, in_specs=in_specs, out_specs=out_specs, check_vma=False
    )
```

```python
import math

import jax
import jax.numpy as jnp
import numpy as np
from jax import lax
from jax.experimental import pallas as pl
from jax.experimental.pallas import tpu as pltpu
from jax.sharding import Mesh
from jax.sharding import PartitionSpec as P

D = 2048
KEY_WIDTH = 512
EXPERTS = 64
LANES = 128
ROW = KEY_WIDTH + LANES

beta_one = 0.9
beta_two = 0.95
step_rate = 0.01
epsilon = 1e-08
bias_one = 1.0 - 0.9**10
bias_two = 1.0 - 0.95**10

WIDE = ("z", "y", "xh", "c")
ALL = ("z", "y", "xh", "c", "xl")


def place(z, y, x, c):
    return (((z * 4 + y) * 2 + x // 2) * 2 + c) * 2 + x % 2


def permutation(target):
    return [
        (place(z, y, x, c), place(*target(z, y, x, c)))
        for z in range(8)
        for y in range(4)
        for x in range(4)
        for c in range(2)
    ]


def along(stage, shift):
    def target(z, y, x, c):
        if c == stage:
            return z, y, (x + shift) % 4, c
        return z, (y + shift) % 4, x, c

    return permutation(target)


SIBLING = permutation(lambda z, y, x, c: (z, y, x, 1 - c))
PARTNER = permutation(lambda z, y, x, c: (z, y, x ^ 1, c))


def send(x, pairs):
    return lax.ppermute(x, ALL, pairs)


def adamw(master, first_moment, second, gradient, factor, decay_rate):
    scaled = factor * gradient
    first_new = beta_one * first_moment + (1.0 - beta_one) * scaled
    second_new = beta_two * second + (1.0 - beta_two) * scaled * scaled
    update = (
        first_new / bias_one / (jnp.sqrt(second_new / bias_two) + epsilon) + decay_rate * master
    )
    master_new = master - step_rate * update
    return (master_new, first_new, second_new)


def group_of(t, p, q):
    x = jnp.where(t == 0, p, q)
    y = jnp.where(t == 0, q, p)
    return x % 2, t * 8 + (x // 2) * 4 + y


def micro_total(stack):
    return (stack[0].astype(jnp.float32) + stack[1].astype(jnp.float32)).astype(jnp.bfloat16)


def pack_group(key_ref, router_ref, gain_ref, half, group, store):
    key = micro_total(key_ref[...]).astype(jnp.float32)
    router = micro_total(router_ref[...]).astype(jnp.float32)
    gain = micro_total(gain_ref[:, half]).astype(jnp.float32)
    gain = jnp.where(group == 0, gain, 0.0)
    lane = lax.broadcasted_iota(jnp.int32, (8, LANES), 1)
    row = lax.broadcasted_iota(jnp.int32, (8, LANES), 0)
    for z in range(8):
        tile = router[:, (z // 2) * LANES : (z // 2 + 1) * LANES]
        low = lane < 64
        mine = low if z % 2 == 0 else jnp.logical_not(low)
        spare = jnp.where(row // 2 == z // 2, gain, 0.0)
        store(z, key[z * 8 : (z + 1) * 8], jnp.where(mine, tile, spare))


def pack_sent(where_ref, *refs):
    keys, routers, gain_ref, out_ref = refs[:4], refs[4:8], refs[8], refs[9]
    t, p, q = where_ref[0], where_ref[1], pl.program_id(0)
    for k in range(4):
        half, group = group_of(t, (p + k) % 4, q)

        def store(z, key, tile, k=k):
            out_ref[k, 0, z, :, :KEY_WIDTH] = key.astype(jnp.bfloat16)
            out_ref[k, 0, z, :, KEY_WIDTH:] = tile.astype(jnp.bfloat16)

        pack_group(keys[k], routers[k], gain_ref, half, group, store)


def pack_kept(where_ref, *refs):
    keys, routers, gain_ref, got_ref, outs = refs[:4], refs[4:8], refs[8], refs[9], refs[10:]
    t, p, q = where_ref[0], where_ref[1], pl.program_id(0)
    for k in range(4):
        half, group = group_of(t, (p + k) % 4, q)

        def store(z, key, tile, k=k):
            got = got_ref[k, 0, z].astype(jnp.float32)
            outs[k][0, z, :, :KEY_WIDTH] = (key + got[:, :KEY_WIDTH]).astype(jnp.bfloat16)
            outs[k][0, z, :, KEY_WIDTH:] = (tile + got[:, KEY_WIDTH:]).astype(jnp.bfloat16)

        pack_group(keys[k], routers[k], gain_ref, half, group, store)


def pack(t, p, key_grads, router_grads, gain_grads, got=None):
    def key_map(k):
        def index(q, where_ref):
            half, group = group_of(where_ref[0], (where_ref[1] + k) % 4, q)
            return 0, half * 16 + group, 0

        return index

    def router_map(k):
        def index(q, where_ref):
            half, group = group_of(where_ref[0], (where_ref[1] + k) % 4, q)
            return 0, group // 2, half * 2 + group % 2

        return index

    in_specs = [pl.BlockSpec((2, 64, KEY_WIDTH), key_map(k)) for k in range(4)]
    in_specs += [pl.BlockSpec((2, 8, 512), router_map(k)) for k in range(4)]
    in_specs += [pl.BlockSpec((2, 2, 8, LANES), lambda q, where_ref: (0, 0, 0, 0))]
    operands = [key_grads] * 4 + [router_grads] * 4 + [gain_grads]
    whole = pl.BlockSpec((4, 1, 8, 8, ROW), lambda q, where_ref: (0, q, 0, 0, 0))
    if got is None:
        body, out_specs = pack_sent, whole
        out_shape = jax.ShapeDtypeStruct((4, 4, 8, 8, ROW), jnp.bfloat16)
    else:
        body = pack_kept
        in_specs += [whole]
        operands += [got]
        out_specs = [pl.BlockSpec((1, 8, 8, ROW), lambda q, where_ref: (q, 0, 0, 0))] * 4
        out_shape = [jax.ShapeDtypeStruct((4, 8, 8, ROW), jnp.bfloat16)] * 4
    return pl.pallas_call(
        body,
        grid_spec=pltpu.PrefetchScalarGridSpec(
            num_scalar_prefetch=1, grid=(4,), in_specs=in_specs, out_specs=out_specs
        ),
        out_shape=out_shape,
        compiler_params=pltpu.CompilerParams(vmem_limit_bytes=32 * 1024 * 1024),
    )(jnp.stack([t, p]), *operands)


def add_rows(where_ref, *refs):
    terms, outs = refs[:4], refs[4:]
    for k in range(4):
        at = (where_ref[0] + k) % 4
        total = terms[0][at].astype(jnp.float32)
        for term in terms[1:]:
            total = total + term[at].astype(jnp.float32)
        outs[k][...] = total


def sum_rotated(q, terms):
    return pl.pallas_call(
        add_rows,
        in_specs=[pl.BlockSpec(memory_space=pltpu.SMEM)]
        + [pl.BlockSpec(memory_space=pltpu.VMEM)] * 4,
        out_specs=[pl.BlockSpec(memory_space=pltpu.VMEM)] * 4,
        out_shape=[jax.ShapeDtypeStruct((8, 8, ROW), jnp.float32)] * 4,
        compiler_params=pltpu.CompilerParams(vmem_limit_bytes=32 * 1024 * 1024),
    )(q.reshape(1), *terms)


def spare_place(z, shape, block_axis=None):
    row = lax.broadcasted_iota(jnp.int32, shape, len(shape) - 2)
    lane = lax.broadcasted_iota(jnp.int32, shape, len(shape) - 1)
    if block_axis is not None:
        z = lax.broadcasted_iota(jnp.int32, shape, block_axis) % 8
    return (row == (2 * (z // 2) + 2) % 8) & (lane == jnp.where(z % 2 == 0, 64, 0))


def unpack(blocks):
    key = blocks[:, :, :KEY_WIDTH].reshape(1024, KEY_WIDTH)
    tiles = blocks[:, :, KEY_WIDTH:].reshape(8, 2, 4, 2, 8, LANES)
    low = lax.broadcasted_iota(jnp.int32, (8, LANES), 1) < 64
    router = jnp.where(low, tiles[:, :, :, 0], tiles[:, :, :, 1])
    router = router.transpose(0, 3, 1, 2, 4).reshape(EXPERTS, 1024)
    pairs = jnp.where(low, tiles[0, 0, :, 1], tiles[0, 0, :, 0])
    gain = jnp.concatenate([pairs[m, 2 * m : 2 * m + 2] for m in range(4)]).reshape(1024)
    return key, router, gain


def on_device(
    key_grads,
    router_grads,
    gain_grads,
    key_master,
    key_first,
    key_second,
    router_master,
    router_first,
    router_second,
    gain_master,
    gain_first,
    gain_second,
):
    core = lax.axis_index("c")
    half = lax.axis_index("xl")
    x = lax.axis_index("xh") * 2 + half
    y = lax.axis_index("y")
    z = lax.axis_index("z")
    grads = (key_grads[0, 0], router_grads[0, 0], gain_grads.reshape(2, 2, 8, LANES))
    first_place = jnp.where(core == 0, x, y)
    second_place = jnp.where(core == 0, y, x)
    got = send(pack(1 - core, second_place, *grads), SIBLING)
    parts = pack(core, first_place, *grads, got)
    parts = [parts[0]] + [send(parts[k], along(0, k)) for k in (1, 2, 3)]
    parts = sum_rotated(second_place, parts)
    parts = [parts[0]] + [send(parts[k], along(1, k)) for k in (1, 2, 3)]
    partial = (parts[0] + parts[1]) + (parts[2] + parts[3])
    own = jnp.sum(lax.all_to_all(partial, "z", 0, 0, tiled=True), axis=0)
    largest = jnp.maximum(jnp.max(jnp.abs(own)), 1e-30)
    exponent = jnp.floor(jnp.log2(largest)) - 13.0
    tile = jnp.where(spare_place(z, (8, LANES)), exponent, own[:, KEY_WIDTH:] * jnp.exp2(-exponent))
    code = jnp.concatenate([own[:, :KEY_WIDTH] * jnp.exp2(-exponent), tile], axis=1)
    code = code.astype(jnp.float16)
    parts = lax.all_to_all(
        jnp.broadcast_to(code[None], (64, 8, ROW)), ("xh", "y", "z"), 0, 0, tiled=True
    )
    other = send(parts, SIBLING)
    blocks = jnp.where(
        core == 0, jnp.concatenate([parts, other]), jnp.concatenate([other, parts])
    )
    blocks = blocks.astype(jnp.float32)
    held = spare_place(None, (128, 8, LANES), 0)
    exponents = jnp.sum(jnp.where(held, blocks[:, :, KEY_WIDTH:], 0.0), axis=(1, 2), keepdims=True)
    blocks = blocks * jnp.exp2(exponents)
    key_sum, router_sum, gain_sum = unpack(blocks)
    squares = (
        jnp.sum(key_sum * key_sum) + jnp.sum(router_sum * router_sum) + jnp.sum(gain_sum * gain_sum)
    )
    squares = squares + send(squares, PARTNER)
    clip_limit = 0.5 * math.sqrt(D * KEY_WIDTH + EXPERTS * D + D)
    factor = clip_limit / jnp.maximum(jnp.sqrt(squares), clip_limit)
    key_new, key_first_new, key_second_new = adamw(
        key_master, key_first, key_second, key_sum, factor, 0.1
    )
    router_new, router_first_new, router_second_new = adamw(
        router_master, router_first, router_second, router_sum, factor, 0.1
    )
    gain_new, gain_first_new, gain_second_new = adamw(
        gain_master, gain_first, gain_second, gain_sum, factor, 0.0
    )
    key_low = key_new.astype(jnp.bfloat16)
    router_low = router_new.astype(jnp.bfloat16)
    gain_low = gain_new.astype(jnp.bfloat16)

    def exchange(low):
        mine = lax.dynamic_index_in_dim(low, core, 0, keepdims=False)
        far = send(mine, PARTNER)
        near = send(far, SIBLING)
        far = jnp.where(core == 0, jnp.stack([far, near]), jnp.stack([near, far]))
        return jnp.where(half == 0, jnp.stack([low, far]), jnp.stack([far, low]))

    key_weight = exchange(key_low.reshape(2, 512, 512)).reshape(D, KEY_WIDTH)
    router_weight = exchange(router_low.reshape(2, 32, 1024)).reshape(2, EXPERTS, 1024)
    router_weight = jnp.concatenate([router_weight[0], router_weight[1]], axis=1)
    gain_far = send(gain_low, PARTNER)
    gain_weight = jnp.where(
        half == 0, jnp.concatenate([gain_low, gain_far]), jnp.concatenate([gain_far, gain_low])
    )
    return (
        key_new,
        key_first_new,
        key_second_new,
        router_new,
        router_first_new,
        router_second_new,
        gain_new,
        gain_first_new,
        gain_second_new,
        key_weight,
        router_weight,
        gain_weight,
    )


def solution(mesh):
    fine = Mesh(np.asarray(mesh.devices).reshape(8, 4, 2, 2, 2), ("z", "y", "xh", "c", "xl"))
    in_specs = (
        P(WIDE, "xl", None, None, None),
        P(WIDE, "xl", None, None, None),
        P(WIDE, "xl", None, None),
        P("xl", None),
        P("xl", None),
        P("xl", None),
        P(None, "xl"),
        P(None, "xl"),
        P(None, "xl"),
        P("xl"),
        P("xl"),
        P("xl"),
    )
    out_specs = (
        P("xl", None),
        P("xl", None),
        P("xl", None),
        P(None, "xl"),
        P(None, "xl"),
        P(None, "xl"),
        P("xl"),
        P("xl"),
        P("xl"),
        P(),
        P(),
        P(),
    )
    return jax.shard_map(
        on_device, mesh=fine, in_specs=in_specs, out_specs=out_specs, check_vma=False
    )
```

```python
import math

import jax
import jax.numpy as jnp
import numpy as np
from jax import lax
from jax.experimental import pallas as pl
from jax.experimental.pallas import tpu as pltpu
from jax.sharding import Mesh
from jax.sharding import PartitionSpec as P

D = 2048
KEY_WIDTH = 512
EXPERTS = 64
LANES = 128
ROW = KEY_WIDTH + LANES

beta_one = 0.9
beta_two = 0.95
step_rate = 0.01
epsilon = 1e-08
bias_one = 1.0 - 0.9**10
bias_two = 1.0 - 0.95**10

WIDE = ("z", "y", "xh", "c")
ALL = ("z", "y", "xh", "c", "xl")


def place(z, y, x, c):
    return (((z * 4 + y) * 2 + x // 2) * 2 + c) * 2 + x % 2


def permutation(target):
    return [
        (place(z, y, x, c), place(*target(z, y, x, c)))
        for z in range(8)
        for y in range(4)
        for x in range(4)
        for c in range(2)
    ]


def along(stage, shift):
    def target(z, y, x, c):
        if c == stage:
            return z, y, (x + shift) % 4, c
        return z, (y + shift) % 4, x, c

    return permutation(target)


SIBLING = permutation(lambda z, y, x, c: (z, y, x, 1 - c))
PARTNER = permutation(lambda z, y, x, c: (z, y, x ^ 1, c))


def send(x, pairs):
    return lax.ppermute(x, ALL, pairs)


def adamw(master, first_moment, second, gradient, factor, decay_rate):
    scaled = factor * gradient
    first_new = beta_one * first_moment + (1.0 - beta_one) * scaled
    second_new = beta_two * second + (1.0 - beta_two) * scaled * scaled
    update = (
        first_new / bias_one / (jnp.sqrt(second_new / bias_two) + epsilon) + decay_rate * master
    )
    master_new = master - step_rate * update
    return (master_new, first_new, second_new)


def group_of(t, p, q):
    x = jnp.where(t == 0, p, q)
    y = jnp.where(t == 0, q, p)
    return x % 2, t * 8 + (x // 2) * 4 + y


def micro_total(stack):
    return (stack[0].astype(jnp.float32) + stack[1].astype(jnp.float32)).astype(jnp.bfloat16)


def pack_local(where_ref, key_ref, router_ref, gain_ref, out_ref, keys, routers, gains, tiles, sems):
    t, p = where_ref[0], where_ref[1]
    copies = []
    for i in range(16):
        half, group = group_of(t, (p + i // 4) % 4, i % 4)
        rows = pl.ds(pl.multiple_of((half * 16 + group) * 64, 64), 64)
        copies.append(pltpu.make_async_copy(key_ref.at[:, rows], keys.at[i], sems.at[i]))
        rows = pl.ds(pl.multiple_of(group // 2 * 8, 8), 8)
        columns = pl.ds(pl.multiple_of((half * 2 + group % 2) * 512, 512), 512)
        copies.append(
            pltpu.make_async_copy(
                router_ref.at[:, rows, columns], routers.at[i], sems.at[16 + i]
            )
        )
    gain_copy = pltpu.make_async_copy(gain_ref, gains, sems.at[32])
    gain_copy.start()
    for copy in copies:
        copy.start()
    lane = lax.broadcasted_iota(jnp.int32, (8, LANES), 1)
    row = lax.broadcasted_iota(jnp.int32, (8, LANES), 0)
    low = lane < 64
    gain_copy.wait()
    gain = gains[...].astype(jnp.float32)
    gain = (gain[0:1] + gain[1:2]).astype(jnp.bfloat16).astype(jnp.float32)
    for half in range(2):
        tile = jnp.zeros((8, LANES), jnp.float32)
        for r in range(8):
            at = half * 1024 + r * LANES
            tile = jnp.where(row == r, gain[:, at : at + LANES], tile)
        tiles[half] = tile
    for i in range(16):
        half, group = group_of(t, (p + i // 4) % 4, i % 4)
        copies[2 * i].wait()
        copies[2 * i + 1].wait()
        key = keys[i, 0].astype(jnp.float32) + keys[i, 1].astype(jnp.float32)
        out_ref[i // 4, i % 4, :, :, :KEY_WIDTH] = key.astype(jnp.bfloat16).reshape(
            8, 8, KEY_WIDTH
        )
        router = routers[i, 0].astype(jnp.float32) + routers[i, 1].astype(jnp.float32)
        spare = jnp.where(group == 0, tiles[half], 0.0)
        for z in range(8):
            tile = router[:, (z // 2) * LANES : (z // 2 + 1) * LANES]
            mine = low if z % 2 == 0 else jnp.logical_not(low)
            kept = jnp.where(row // 2 == z // 2, spare, 0.0)
            out_ref[i // 4, i % 4, z, :, KEY_WIDTH:] = jnp.where(mine, tile, kept).astype(
                jnp.bfloat16
            )


def pack(t, p, grads):
    return pl.pallas_call(
        pack_local,
        in_specs=[pl.BlockSpec(memory_space=pltpu.SMEM)]
        + [pl.BlockSpec(memory_space=pltpu.HBM)] * 3,
        out_specs=pl.BlockSpec(memory_space=pltpu.VMEM),
        out_shape=jax.ShapeDtypeStruct((4, 4, 8, 8, ROW), jnp.bfloat16),
        scratch_shapes=[
            pltpu.VMEM((16, 2, 64, KEY_WIDTH), jnp.bfloat16),
            pltpu.VMEM((16, 2, 8, 512), jnp.bfloat16),
            pltpu.VMEM((2, D), jnp.bfloat16),
            pltpu.VMEM((2, 8, LANES), jnp.float32),
            pltpu.SemaphoreType.DMA((33,)),
        ],
        compiler_params=pltpu.CompilerParams(vmem_limit_bytes=16 * 1024 * 1024),
    )(jnp.stack([t, p]), *[pltpu.with_memory_space_constraint(g, pltpu.HBM) for g in grads])


def in_vmem(body, operands, shapes, scalars=()):
    scalars = [jnp.stack(scalars)] if scalars else []
    return pl.pallas_call(
        body,
        in_specs=[pl.BlockSpec(memory_space=pltpu.SMEM)] * len(scalars)
        + [pl.BlockSpec(memory_space=pltpu.VMEM)] * len(operands),
        out_specs=[pl.BlockSpec(memory_space=pltpu.VMEM)] * len(shapes),
        out_shape=[jax.ShapeDtypeStruct(*shape) for shape in shapes],
        compiler_params=pltpu.CompilerParams(vmem_limit_bytes=8 * 1024 * 1024),
    )(*scalars, *operands)


def add_pair(kept_ref, got_ref, *outs):
    for k in range(4):
        for q in range(4):
            total = kept_ref[k, q].astype(jnp.float32) + got_ref[k, q].astype(jnp.float32)
            outs[k][q] = total.astype(jnp.bfloat16)


def add_rows(where_ref, *refs):
    terms, outs = refs[:4], refs[4:]
    for k in range(4):
        at = (where_ref[0] + k) % 4
        total = terms[0][at].astype(jnp.float32)
        for term in terms[1:]:
            total = total + term[at].astype(jnp.float32)
        outs[k][...] = total


def add_split(where_ref, *refs):
    terms, (kept_ref, sent_ref) = refs[:-2], refs[-2:]
    bit = where_ref[0]
    for i in range(kept_ref.shape[0]):
        for out_ref, b in ((kept_ref, bit), (sent_ref, 1 - bit)):
            at = 2 * i + b
            total = terms[0][at]
            for term in terms[1:]:
                total = total + term[at]
            out_ref[i] = total


def reduce_along_z(z, terms):
    for step in range(3):
        shape = ((4 >> step, 8, ROW), jnp.float32)
        kept, sent = in_vmem(add_split, terms, [shape] * 2, [(z >> step) & 1])
        pairs = permutation(lambda z, y, x, c, step=step: (z ^ (1 << step), y, x, c))
        terms = [kept, send(sent, pairs)]
    return (terms[0] + terms[1])[0]


def spare_place(z, shape, block_axis=None):
    row = lax.broadcasted_iota(jnp.int32, shape, len(shape) - 2)
    lane = lax.broadcasted_iota(jnp.int32, shape, len(shape) - 1)
    if block_axis is not None:
        z = lax.broadcasted_iota(jnp.int32, shape, block_axis) % 8
    return (row == (2 * (z // 2) + 2) % 8) & (lane == jnp.where(z % 2 == 0, 64, 0))


def unpack(blocks):
    key = blocks[:, :, :KEY_WIDTH].reshape(1024, KEY_WIDTH)
    tiles = blocks[:, :, KEY_WIDTH:].reshape(8, 2, 4, 2, 8, LANES)
    low = lax.broadcasted_iota(jnp.int32, (8, LANES), 1) < 64
    router = jnp.where(low, tiles[:, :, :, 0], tiles[:, :, :, 1])
    router = router.transpose(0, 3, 1, 2, 4).reshape(EXPERTS, 1024)
    pairs = jnp.where(low, tiles[0, 0, :, 1], tiles[0, 0, :, 0])
    gain = jnp.concatenate([pairs[m, 2 * m : 2 * m + 2] for m in range(4)]).reshape(1024)
    return key, router, gain


def on_device(
    key_grads,
    router_grads,
    gain_grads,
    key_master,
    key_first,
    key_second,
    router_master,
    router_first,
    router_second,
    gain_master,
    gain_first,
    gain_second,
):
    core = lax.axis_index("c")
    half = lax.axis_index("xl")
    x = lax.axis_index("xh") * 2 + half
    y = lax.axis_index("y")
    z = lax.axis_index("z")
    grads = (key_grads[0, 0], router_grads[0, 0], gain_grads[0, 0])
    first_place = jnp.where(core == 0, x, y)
    second_place = jnp.where(core == 0, y, x)
    got = send(pack(1 - core, second_place, grads), SIBLING)
    kept = pack(core, first_place, grads)
    parts = in_vmem(add_pair, [kept, got], [((4, 8, 8, ROW), jnp.bfloat16)] * 4)
    parts = [parts[0]] + [send(parts[k], along(0, k)) for k in (1, 2, 3)]
    parts = in_vmem(add_rows, parts, [((8, 8, ROW), jnp.float32)] * 4, [second_place])
    parts = [parts[0]] + [send(parts[k], along(1, k)) for k in (1, 2, 3)]
    own = reduce_along_z(z, parts)
    largest = jnp.maximum(jnp.max(jnp.abs(own)), 1e-30)
    exponent = jnp.floor(jnp.log2(largest)) - 13.0
    tile = jnp.where(spare_place(z, (8, LANES)), exponent, own[:, KEY_WIDTH:] * jnp.exp2(-exponent))
    code = jnp.concatenate([own[:, :KEY_WIDTH] * jnp.exp2(-exponent), tile], axis=1)
    code = code.astype(jnp.float16)
    parts = lax.all_to_all(
        jnp.broadcast_to(code[None], (64, 8, ROW)), ("xh", "y", "z"), 0, 0, tiled=True
    )
    other = send(parts, SIBLING)
    blocks = jnp.where(
        core == 0, jnp.concatenate([parts, other]), jnp.concatenate([other, parts])
    )
    blocks = blocks.astype(jnp.float32)
    held = spare_place(None, (128, 8, LANES), 0)
    exponents = jnp.sum(jnp.where(held, blocks[:, :, KEY_WIDTH:], 0.0), axis=(1, 2), keepdims=True)
    blocks = blocks * jnp.exp2(exponents)
    key_sum, router_sum, gain_sum = unpack(blocks)
    squares = (
        jnp.sum(key_sum * key_sum) + jnp.sum(router_sum * router_sum) + jnp.sum(gain_sum * gain_sum)
    )
    squares = squares + send(squares, PARTNER)
    clip_limit = 0.5 * math.sqrt(D * KEY_WIDTH + EXPERTS * D + D)
    factor = clip_limit / jnp.maximum(jnp.sqrt(squares), clip_limit)
    key_new, key_first_new, key_second_new = adamw(
        key_master, key_first, key_second, key_sum, factor, 0.1
    )
    router_new, router_first_new, router_second_new = adamw(
        router_master, router_first, router_second, router_sum, factor, 0.1
    )
    gain_new, gain_first_new, gain_second_new = adamw(
        gain_master, gain_first, gain_second, gain_sum, factor, 0.0
    )
    key_low = key_new.astype(jnp.bfloat16)
    router_low = router_new.astype(jnp.bfloat16)
    gain_low = gain_new.astype(jnp.bfloat16)

    def exchange(low):
        mine = lax.dynamic_index_in_dim(low, core, 0, keepdims=False)
        far = send(mine, PARTNER)
        near = send(far, SIBLING)
        far = jnp.where(core == 0, jnp.stack([far, near]), jnp.stack([near, far]))
        return jnp.where(half == 0, jnp.stack([low, far]), jnp.stack([far, low]))

    key_weight = exchange(key_low.reshape(2, 512, 512)).reshape(D, KEY_WIDTH)
    router_weight = exchange(router_low.reshape(2, 32, 1024)).reshape(2, EXPERTS, 1024)
    router_weight = jnp.concatenate([router_weight[0], router_weight[1]], axis=1)
    gain_far = send(gain_low, PARTNER)
    gain_weight = jnp.where(
        half == 0, jnp.concatenate([gain_low, gain_far]), jnp.concatenate([gain_far, gain_low])
    )
    return (
        key_new,
        key_first_new,
        key_second_new,
        router_new,
        router_first_new,
        router_second_new,
        gain_new,
        gain_first_new,
        gain_second_new,
        key_weight,
        router_weight,
        gain_weight,
    )


def solution(mesh):
    fine = Mesh(np.asarray(mesh.devices).reshape(8, 4, 2, 2, 2), ("z", "y", "xh", "c", "xl"))
    in_specs = (
        P(WIDE, "xl", None, None, None),
        P(WIDE, "xl", None, None, None),
        P(WIDE, "xl", None, None),
        P("xl", None),
        P("xl", None),
        P("xl", None),
        P(None, "xl"),
        P(None, "xl"),
        P(None, "xl"),
        P("xl"),
        P("xl"),
        P("xl"),
    )
    out_specs = (
        P("xl", None),
        P("xl", None),
        P("xl", None),
        P(None, "xl"),
        P(None, "xl"),
        P(None, "xl"),
        P("xl"),
        P("xl"),
        P("xl"),
        P(),
        P(),
        P(),
    )
    return jax.shard_map(
        on_device, mesh=fine, in_specs=in_specs, out_specs=out_specs, check_vma=False
    )
```

```python
import math

import jax
import jax.numpy as jnp
import numpy as np
from jax import lax
from jax.experimental import pallas as pl
from jax.experimental.pallas import tpu as pltpu
from jax.sharding import Mesh
from jax.sharding import PartitionSpec as P

D = 2048
KEY_WIDTH = 512
EXPERTS = 64
LANES = 128
ROW = KEY_WIDTH + LANES

beta_one = 0.9
beta_two = 0.95
step_rate = 0.01
epsilon = 1e-08
bias_one = 1.0 - 0.9**10
bias_two = 1.0 - 0.95**10

WIDE = ("z", "y", "xh", "c")
ALL = ("z", "y", "xh", "c", "xl")


def place(z, y, x, c):
    return (((z * 4 + y) * 2 + x // 2) * 2 + c) * 2 + x % 2


def permutation(target):
    return [
        (place(z, y, x, c), place(*target(z, y, x, c)))
        for z in range(8)
        for y in range(4)
        for x in range(4)
        for c in range(2)
    ]


def along(stage, shift):
    def target(z, y, x, c):
        if c == stage:
            return z, y, (x + shift) % 4, c
        return z, (y + shift) % 4, x, c

    return permutation(target)


SIBLING = permutation(lambda z, y, x, c: (z, y, x, 1 - c))
PARTNER = permutation(lambda z, y, x, c: (z, y, x ^ 1, c))
OTHER_PARTNER = permutation(lambda z, y, x, c: (z, y, x ^ 3, c))
PARTNER_SIBLING = permutation(lambda z, y, x, c: (z, y, x ^ 1, 1 - c))


def send(x, pairs):
    return lax.ppermute(x, ALL, pairs)


def adamw(master, first_moment, second, scaled, decay_rate):
    first_new = beta_one * first_moment + (1.0 - beta_one) * scaled
    second_new = beta_two * second + (1.0 - beta_two) * scaled * scaled
    update = (
        first_new / bias_one / (jnp.sqrt(second_new / bias_two) + epsilon) + decay_rate * master
    )
    master_new = master - step_rate * update
    return (master_new, first_new, second_new)


def group_of(t, p, q):
    x = jnp.where(t == 0, p, q)
    y = jnp.where(t == 0, q, p)
    return x % 2, t * 8 + (x // 2) * 4 + y


def micro_total(stack):
    return (stack[0].astype(jnp.float32) + stack[1].astype(jnp.float32)).astype(jnp.bfloat16)


def pack_local(where_ref, key_ref, router_ref, gain_ref, out_ref, keys, routers, gains, tiles, sems):
    t, p = where_ref[0], where_ref[1]
    copies = []
    for i in range(16):
        half, group = group_of(t, (p + i // 4) % 4, i % 4)
        rows = pl.ds(pl.multiple_of((half * 16 + group) * 64, 64), 64)
        copies.append(pltpu.make_async_copy(key_ref.at[:, rows], keys.at[i], sems.at[i]))
        rows = pl.ds(pl.multiple_of(group // 2 * 8, 8), 8)
        columns = pl.ds(pl.multiple_of((half * 2 + group % 2) * 512, 512), 512)
        copies.append(
            pltpu.make_async_copy(
                router_ref.at[:, rows, columns], routers.at[i], sems.at[16 + i]
            )
        )
    gain_copy = pltpu.make_async_copy(gain_ref, gains, sems.at[32])
    gain_copy.start()
    for copy in copies:
        copy.start()
    lane = lax.broadcasted_iota(jnp.int32, (8, LANES), 1)
    row = lax.broadcasted_iota(jnp.int32, (8, LANES), 0)
    low = lane < 64
    gain_copy.wait()
    gain = gains[...].astype(jnp.float32)
    gain = (gain[0:1] + gain[1:2]).astype(jnp.bfloat16).astype(jnp.float32)
    for half in range(2):
        for z in range(8):
            at = half * 1024 + z * LANES
            line = gain[:, at : at + LANES]
            turned = jnp.concatenate([line[:, 64:], line[:, :64]], axis=1)
            tiles[half, z] = jnp.where(row == 0, line, jnp.where(row == 1, turned, 0.0))
    for i in range(16):
        half, group = group_of(t, (p + i // 4) % 4, i % 4)
        copies[2 * i].wait()
        copies[2 * i + 1].wait()
        key = keys[i, 0].astype(jnp.float32) + keys[i, 1].astype(jnp.float32)
        out_ref[i // 4, i % 4, :, :, :KEY_WIDTH] = key.astype(jnp.bfloat16).reshape(
            8, 8, KEY_WIDTH
        )
        router = routers[i, 0].astype(jnp.float32) + routers[i, 1].astype(jnp.float32)
        for z in range(8):
            tile = router[:, (z // 2) * LANES : (z // 2 + 1) * LANES]
            mine = low if z % 2 == 0 else jnp.logical_not(low)
            kept = jnp.where(group == 0, tiles[half, z], 0.0)
            out_ref[i // 4, i % 4, z, :, KEY_WIDTH:] = jnp.where(mine, tile, kept).astype(
                jnp.bfloat16
            )


def pack(t, p, grads):
    return pl.pallas_call(
        pack_local,
        in_specs=[pl.BlockSpec(memory_space=pltpu.SMEM)]
        + [pl.BlockSpec(memory_space=pltpu.HBM)] * 3,
        out_specs=pl.BlockSpec(memory_space=pltpu.VMEM),
        out_shape=jax.ShapeDtypeStruct((4, 4, 8, 8, ROW), jnp.bfloat16),
        scratch_shapes=[
            pltpu.VMEM((16, 2, 64, KEY_WIDTH), jnp.bfloat16),
            pltpu.VMEM((16, 2, 8, 512), jnp.bfloat16),
            pltpu.VMEM((2, D), jnp.bfloat16),
            pltpu.VMEM((2, 8, 8, LANES), jnp.float32),
            pltpu.SemaphoreType.DMA((33,)),
        ],
        compiler_params=pltpu.CompilerParams(vmem_limit_bytes=16 * 1024 * 1024),
    )(jnp.stack([t, p]), *[pltpu.with_memory_space_constraint(g, pltpu.HBM) for g in grads])


def in_vmem(body, operands, shapes, scalars=()):
    scalars = [jnp.stack(scalars)] if scalars else []
    return pl.pallas_call(
        body,
        in_specs=[pl.BlockSpec(memory_space=pltpu.SMEM)] * len(scalars)
        + [pl.BlockSpec(memory_space=pltpu.VMEM)] * len(operands),
        out_specs=[pl.BlockSpec(memory_space=pltpu.VMEM)] * len(shapes),
        out_shape=[jax.ShapeDtypeStruct(*shape) for shape in shapes],
        compiler_params=pltpu.CompilerParams(vmem_limit_bytes=8 * 1024 * 1024),
    )(*scalars, *operands)


def add_pair(kept_ref, got_ref, *outs):
    for k in range(4):
        for q in range(4):
            total = kept_ref[k, q].astype(jnp.float32) + got_ref[k, q].astype(jnp.float32)
            outs[k][q] = total.astype(jnp.bfloat16)


def add_rows(where_ref, *refs):
    terms, outs = refs[:4], refs[4:]
    for k in range(4):
        at = (where_ref[0] + k) % 4
        total = terms[0][at].astype(jnp.float32)
        for term in terms[1:]:
            total = total + term[at].astype(jnp.float32)
        outs[k][...] = total


def add_split(where_ref, *refs):
    terms, (kept_ref, sent_ref) = refs[:-2], refs[-2:]
    bit = where_ref[0]
    for i in range(kept_ref.shape[0]):
        for out_ref, b in ((kept_ref, bit), (sent_ref, 1 - bit)):
            at = 2 * i + b
            total = terms[0][at]
            for term in terms[1:]:
                total = total + term[at]
            out_ref[i] = total


def reduce_along_z(z, terms):
    for step in range(3):
        shape = ((4 >> step, 8, ROW), jnp.float32)
        kept, sent = in_vmem(add_split, terms, [shape] * 2, [(z >> step) & 1])
        pairs = permutation(lambda z, y, x, c, step=step: (z ^ (1 << step), y, x, c))
        terms = [kept, send(sent, pairs)]
    return terms


def spare_lanes(parity):
    lane = lax.broadcasted_iota(jnp.int32, (8, LANES), 1)
    return lane // 64 + parity == 1


def encode(where_ref, kept_ref, got_ref, out_ref):
    own = kept_ref[0] + got_ref[0]
    largest = jnp.max(jnp.max(jnp.abs(own), axis=1, keepdims=True), axis=0, keepdims=True)
    largest = jnp.maximum(jnp.broadcast_to(largest, (8, LANES)), 1e-30)
    exponent = jnp.floor(jnp.log(largest) * (1.0 / math.log(2.0))) - 13.0
    own = own * jnp.concatenate([jnp.exp2(-exponent)] * 5, axis=1)
    squares = jnp.sum(jnp.sum(own * own, axis=1, keepdims=True), axis=0, keepdims=True)
    squares = jnp.broadcast_to(squares, (8, LANES)) * 2.0**-30
    digit = squares.astype(jnp.bfloat16).astype(jnp.float32)
    row = lax.broadcasted_iota(jnp.int32, (8, LANES), 0)
    notes = jnp.where(row == 7, exponent, jnp.where(row == 6, digit, (squares - digit) * 256.0))
    spare = spare_lanes(where_ref[0]) & (row >= 5)
    out_ref[:, :KEY_WIDTH] = own[:, :KEY_WIDTH]
    out_ref[:, KEY_WIDTH:] = jnp.where(spare, notes, own[:, KEY_WIDTH:])


def add_squares(blocks_ref, out_ref):
    totals = [jnp.zeros((1, LANES), jnp.float32)] * 2
    for b in range(64):
        tile = blocks_ref[b, :, KEY_WIDTH:]
        digits = tile[6:7] + tile[5:6] * (1.0 / 256.0)
        totals[b % 2] = totals[b % 2] + digits * jnp.exp2(2.0 * tile[7:8] + 30.0)
    lane = lax.broadcasted_iota(jnp.int32, (1, LANES), 1)
    total = jnp.where(lane == 64, totals[0], 0.0) + jnp.where(lane == 0, totals[1], 0.0)
    out_ref[...] = jnp.broadcast_to(jnp.sum(total, axis=1, keepdims=True), (8, LANES))


def scale_of(tile, z):
    line = tile[7:8]
    turned = jnp.concatenate([line[:, 64:], line[:, :64]], axis=1)
    lane = lax.broadcasted_iota(jnp.int32, (1, LANES), 1)
    line = jnp.where(lane < 64, turned, line) if z % 2 == 0 else jnp.where(lane < 64, line, turned)
    return jnp.exp2(jnp.broadcast_to(line, (8, LANES)))


def gain_line(tile, z):
    first, second = tile[0:1], tile[1:2]
    turned = jnp.concatenate([second[:, 64:], second[:, :64]], axis=1)
    lane = lax.broadcasted_iota(jnp.int32, (1, LANES), 1)
    if z % 2 == 0:
        return jnp.where(lane < 64, turned, first)
    return jnp.where(lane < 64, first, turned)


def clip_factor(squares):
    total = (squares[0][...] + squares[1][...]) + (squares[2][...] + squares[3][...])
    clip_limit = 0.5 * math.sqrt(D * KEY_WIDTH + EXPERTS * D + D)
    return clip_limit / jnp.maximum(jnp.sqrt(total), clip_limit)


def update_rows(t, half, factor, blocks_ref, ins, outs, messages, keys, routers, sems):
    key_ins, router_ins = ins[:3], ins[3:]
    key_outs, router_outs, key_weight, router_weight = outs[:3], outs[3:6], outs[6], outs[7]
    low = lax.broadcasted_iota(jnp.int32, (8, LANES), 1) < 64

    def key_rows(g, base=0):
        return pl.ds(pl.multiple_of(base + t * 512 + g * 64, 64), 64)

    router_rows = pl.ds(pl.multiple_of(t * 32, 32), 32)
    loads = [
        [
            pltpu.make_async_copy(
                key_ins[a].at[key_rows(g)], keys.at[a, pl.ds(g * 64, 64)], sems.at[g * 3 + a]
            )
            for a in range(3)
        ]
        for g in range(8)
    ]
    router_loads = [
        pltpu.make_async_copy(router_ins[a].at[router_rows], routers.at[a], sems.at[24 + a])
        for a in range(3)
    ]
    for copy in loads[0] + router_loads + [c for load in loads[1:] for c in load]:
        copy.start()
    stores = []

    def store(source, target):
        copy = pltpu.make_async_copy(source, target, sems.at[27 + len(stores)])
        copy.start()
        stores.append(copy)

    for copy in router_loads:
        copy.wait()
    for g in range(8):
        for copy in loads[g]:
            copy.wait()
        message, at = messages[g // 4], g % 4
        tiles = []
        for z in range(8):
            tile = blocks_ref[g * 8 + z, :, KEY_WIDTH:]
            scale = scale_of(tile, z) * factor
            tiles.append(tile * scale)
            scaled = blocks_ref[g * 8 + z, :, :KEY_WIDTH] * jnp.concatenate([scale] * 4, axis=1)
            rows = pl.ds(g * 64 + z * 8, 8)
            new = adamw(keys[0, rows], keys[1, rows], keys[2, rows], scaled, 0.1)
            for a in range(3):
                keys[a, rows] = new[a]
            message[pl.ds(at * 64 + z * 8, 8)] = new[0].astype(jnp.bfloat16)
        scaled = jnp.concatenate(
            [jnp.where(low, tiles[2 * i], tiles[2 * i + 1]) for i in range(4)], axis=1
        )
        rows, columns = pl.ds(g // 2 * 8, 8), pl.ds(g % 2 * 512, 512)
        new = adamw(
            routers[0, rows, columns], routers[1, rows, columns], routers[2, rows, columns], scaled, 0.1
        )
        for a in range(3):
            routers[a, rows, columns] = new[a]
        message[pl.ds(256 + at * 8, 8)] = new[0].astype(jnp.bfloat16)
        for a in range(3):
            store(keys.at[a, pl.ds(g * 64, 64)], key_outs[a].at[key_rows(g)])
        if at == 3:
            write_message(t, half, g // 4, message, key_weight, router_weight, store)
    for a in range(3):
        store(routers.at[a], router_outs[a].at[router_rows])
    for copy in stores:
        copy.wait()


def write_message(t, half, which, message, key_weight, router_weight, store):
    rows = pl.ds(pl.multiple_of(half * 1024 + t * 512 + which * 256, 256), 256)
    store(message.at[pl.ds(0, 256)], key_weight.at[rows])
    for i in range(4):
        rows = pl.ds(pl.multiple_of(t * 32 + (which * 2 + i // 2) * 8, 8), 8)
        columns = pl.ds(pl.multiple_of(half * 1024 + i % 2 * 512, 512), 512)
        store(message.at[pl.ds(256 + i * 8, 8)], router_weight.at[rows, columns])


def update_first(where_ref, *refs):
    squares, blocks_ref, ins = refs[:4], refs[4], refs[5:11]
    outs, messages, scratch = refs[11:19], refs[19:21], refs[21:]
    factor = clip_factor(squares)
    update_rows(where_ref[0], where_ref[1], factor, blocks_ref, ins, outs, messages, *scratch)


def update_second(where_ref, *refs):
    squares, blocks_ref, first_ref, ins, gains = refs[:4], refs[4], refs[5], refs[6:12], refs[12:15]
    outs, gain_outs, scratch = refs[23:31], refs[31:35], refs[35:]
    messages, scratch = scratch[:2], scratch[2:]
    factor = clip_factor(squares)
    row = lax.broadcasted_iota(jnp.int32, (8, LANES), 0)
    scaled = jnp.zeros((8, LANES), jnp.float32)
    for z in range(8):
        tile = jnp.where(
            where_ref[0] == 0, blocks_ref[z, :, KEY_WIDTH:], first_ref[z, :, KEY_WIDTH:]
        )
        line = gain_line(tile * (scale_of(tile, z) * factor), z)
        scaled = jnp.where(row == z, line, scaled)
    new = adamw(*[gain[...] for gain in gains], scaled, 0.0)
    for a in range(3):
        gain_outs[a][...] = new[a]
    gain_outs[3][...] = new[0].astype(jnp.bfloat16)
    update_rows(where_ref[0], where_ref[1], factor, blocks_ref, ins, outs, messages, *scratch)


def write_received(where_ref, far0, far1, near0, near1, gain_ref, gain_far_ref, *refs):
    key_weight, router_weight, gain_out, sems = refs[2:]
    t, half = where_ref[0], where_ref[1]
    stores = []

    def store(source, target):
        copy = pltpu.make_async_copy(source, target, sems.at[len(stores)])
        copy.start()
        stores.append(copy)

    write_message(t, 1 - half, 0, far0, key_weight, router_weight, store)
    write_message(t, 1 - half, 1, far1, key_weight, router_weight, store)
    write_message(1 - t, 1 - half, 0, near0, key_weight, router_weight, store)
    write_message(1 - t, 1 - half, 1, near1, key_weight, router_weight, store)
    mine, far = gain_ref[...].astype(jnp.float32), gain_far_ref[...].astype(jnp.float32)
    gain_out[:8] = jnp.where(half == 0, mine, far).astype(jnp.bfloat16)
    gain_out[8:] = jnp.where(half == 0, far, mine).astype(jnp.bfloat16)
    for copy in stores:
        copy.wait()


IN_VMEM = pl.BlockSpec(memory_space=pltpu.VMEM)
IN_HBM = pl.BlockSpec(memory_space=pltpu.HBM)
IN_SMEM = pl.BlockSpec(memory_space=pltpu.SMEM)
MESSAGE = ((288, KEY_WIDTH), jnp.bfloat16)


def in_hbm(arrays):
    return [pltpu.with_memory_space_constraint(a, pltpu.HBM) for a in arrays]


def updated(core, half, squares, parts, other, states, gains):
    shapes = [jax.ShapeDtypeStruct(a.shape, jnp.float32) for a in states]
    shapes += [
        jax.ShapeDtypeStruct((D, KEY_WIDTH), jnp.bfloat16),
        jax.ShapeDtypeStruct((EXPERTS, D), jnp.bfloat16),
    ]
    scratch = [
        pltpu.VMEM((3, 512, KEY_WIDTH), jnp.float32),
        pltpu.VMEM((3, 32, 1024), jnp.float32),
        pltpu.SemaphoreType.DMA((64,)),
    ]
    params = pltpu.CompilerParams(vmem_limit_bytes=24 * 1024 * 1024)
    cost = pl.CostEstimate(flops=7_000_000, bytes_accessed=8_000_000, transcendentals=600_000)
    states = in_hbm(states)
    *outs, sent0, sent1 = pl.pallas_call(
        update_first,
        in_specs=[IN_SMEM] + [IN_VMEM] * 5 + [IN_HBM] * 6,
        out_specs=[IN_HBM] * 8 + [IN_VMEM] * 2,
        out_shape=shapes + [jax.ShapeDtypeStruct(*MESSAGE)] * 2,
        scratch_shapes=scratch,
        compiler_params=params,
        cost_estimate=cost,
    )(jnp.stack([core, half]), *squares, parts, *states)
    far = [send(sent0, PARTNER), send(sent1, OTHER_PARTNER)]
    outs = pl.pallas_call(
        update_second,
        in_specs=[IN_SMEM] + [IN_VMEM] * 6 + [IN_HBM] * 6 + [IN_VMEM] * 3 + [IN_HBM] * 8,
        out_specs=[IN_HBM] * 8 + [IN_VMEM] * 4,
        out_shape=shapes
        + [jax.ShapeDtypeStruct((8, LANES), jnp.float32)] * 3
        + [jax.ShapeDtypeStruct((8, LANES), jnp.bfloat16)],
        input_output_aliases={16 + i: i for i in range(8)},
        scratch_shapes=[pltpu.VMEM(*MESSAGE)] * 2 + scratch,
        compiler_params=params,
        cost_estimate=cost,
    )(jnp.stack([1 - core, half]), *squares, other, parts, *states, *gains, *outs)
    outs, gain_new, gain_low = outs[:8], outs[8:11], outs[11]
    far0, far1, gain_low = lax.optimization_barrier((*far, gain_low))
    far = [far0, far1]
    gain_far = send(gain_low, PARTNER)
    near = [send(a, SIBLING) for a in far]
    key_weight, router_weight, gain_weight = pl.pallas_call(
        write_received,
        in_specs=[IN_SMEM] + [IN_VMEM] * 6 + [IN_HBM] * 2,
        out_specs=[IN_HBM] * 2 + [IN_VMEM],
        out_shape=shapes[6:] + [jax.ShapeDtypeStruct((16, LANES), jnp.bfloat16)],
        input_output_aliases={7: 0, 8: 1},
        scratch_shapes=[pltpu.SemaphoreType.DMA((20,))],
        compiler_params=pltpu.CompilerParams(vmem_limit_bytes=8 * 1024 * 1024),
    )(jnp.stack([core, half]), *far, *near, gain_low, gain_far, *outs[6:])
    return outs[:6], gain_new, key_weight, router_weight, gain_weight


def on_device(
    key_grads,
    router_grads,
    gain_grads,
    key_master,
    key_first,
    key_second,
    router_master,
    router_first,
    router_second,
    gain_master,
    gain_first,
    gain_second,
):
    core = lax.axis_index("c")
    half = lax.axis_index("xl")
    x = lax.axis_index("xh") * 2 + half
    y = lax.axis_index("y")
    z = lax.axis_index("z")
    grads = (key_grads[0, 0], router_grads[0, 0], gain_grads[0, 0])
    first_place = jnp.where(core == 0, x, y)
    second_place = jnp.where(core == 0, y, x)
    got = send(pack(1 - core, second_place, grads), SIBLING)
    kept = pack(core, first_place, grads)
    parts = in_vmem(add_pair, [kept, got], [((4, 8, 8, ROW), jnp.bfloat16)] * 4)
    parts = [parts[0]] + [send(parts[k], along(0, k)) for k in (1, 2, 3)]
    parts = in_vmem(add_rows, parts, [((8, 8, ROW), jnp.float32)] * 4, [second_place])
    parts = [parts[0]] + [send(parts[k], along(1, k)) for k in (1, 2, 3)]
    terms = reduce_along_z(z, parts)
    [code] = in_vmem(encode, terms, [((8, ROW), jnp.float32)], [z & 1])
    parts = lax.all_to_all(
        jnp.broadcast_to(code.astype(jnp.float16)[None], (64, 8, ROW)),
        ("xh", "y", "z"),
        0,
        0,
        tiled=True,
    )
    other = send(parts, SIBLING).astype(jnp.float32)
    parts = parts.astype(jnp.float32)
    [squares] = in_vmem(add_squares, [parts], [((8, LANES), jnp.float32)])
    squares = [squares] + [send(squares, to) for to in (SIBLING, PARTNER, PARTNER_SIBLING)]
    states, gains, key_weight, router_weight, gain_weight = updated(
        core,
        half,
        squares,
        parts,
        other,
        [key_master, key_first, key_second, router_master, router_first, router_second],
        [gain.reshape(8, LANES) for gain in (gain_master, gain_first, gain_second)],
    )
    gains = [gain.reshape(1024) for gain in gains]
    return (*states, *gains, key_weight, router_weight, gain_weight.reshape(D))


def solution(mesh):
    fine = Mesh(np.asarray(mesh.devices).reshape(8, 4, 2, 2, 2), ("z", "y", "xh", "c", "xl"))
    in_specs = (
        P(WIDE, "xl", None, None, None),
        P(WIDE, "xl", None, None, None),
        P(WIDE, "xl", None, None),
        P("xl", None),
        P("xl", None),
        P("xl", None),
        P(None, "xl"),
        P(None, "xl"),
        P(None, "xl"),
        P("xl"),
        P("xl"),
        P("xl"),
    )
    out_specs = (
        P("xl", None),
        P("xl", None),
        P("xl", None),
        P(None, "xl"),
        P(None, "xl"),
        P(None, "xl"),
        P("xl"),
        P("xl"),
        P("xl"),
        P(),
        P(),
        P(),
    )
    return jax.shard_map(
        on_device, mesh=fine, in_specs=in_specs, out_specs=out_specs, check_vma=False
    )
```

```python
import math

import jax
import jax.numpy as jnp
import numpy as np
from jax import lax
from jax.experimental import pallas as pl
from jax.experimental.pallas import tpu as pltpu
from jax.sharding import Mesh
from jax.sharding import PartitionSpec as P

D = 2048
KEY_WIDTH = 512
EXPERTS = 64
LANES = 128
ROW = KEY_WIDTH + LANES

beta_one = 0.9
beta_two = 0.95
step_rate = 0.01
epsilon = 1e-08
bias_one = 1.0 - 0.9**10
bias_two = 1.0 - 0.95**10

WIDE = ("z", "y", "xh", "c")
ALL = ("z", "y", "xh", "c", "xl")


def place(z, y, x, c):
    return (((z * 4 + y) * 2 + x // 2) * 2 + c) * 2 + x % 2


def permutation(target):
    return [
        (place(z, y, x, c), place(*target(z, y, x, c)))
        for z in range(8)
        for y in range(4)
        for x in range(4)
        for c in range(2)
    ]


def along(shift):
    def target(z, y, x, c):
        if c == 0:
            return z, y, (x + shift) % 4, c
        return z, (y + shift) % 4, x, c

    return permutation(target)


SECOND_GROUPS = [
    [place(z, q, p, c) if c == 0 else place(z, p, q, c) for q in range(4) for z in range(8)]
    for c in range(2)
    for p in range(4)
]
SIBLING = permutation(lambda z, y, x, c: (z, y, x, 1 - c))
PARTNER = permutation(lambda z, y, x, c: (z, y, x ^ 1, c))
OTHER_PARTNER = permutation(lambda z, y, x, c: (z, y, x ^ 3, c))
PARTNER_SIBLING = permutation(lambda z, y, x, c: (z, y, x ^ 1, 1 - c))


def send(x, pairs):
    return lax.ppermute(x, ALL, pairs)


def adamw(master, first_moment, second, scaled, decay_rate):
    first_new = beta_one * first_moment + (1.0 - beta_one) * scaled
    second_new = beta_two * second + (1.0 - beta_two) * scaled * scaled
    update = (
        first_new / bias_one / (jnp.sqrt(second_new / bias_two) + epsilon) + decay_rate * master
    )
    master_new = master - step_rate * update
    return (master_new, first_new, second_new)


def group_of(t, p, q):
    x = jnp.where(t == 0, p, q)
    y = jnp.where(t == 0, q, p)
    return x % 2, t * 8 + (x // 2) * 4 + y


def micro_total(stack):
    return (stack[0].astype(jnp.float32) + stack[1].astype(jnp.float32)).astype(jnp.bfloat16)


def pack_local(where_ref, key_ref, router_ref, gain_ref, out_ref, keys, routers, gains, tiles, sems):
    t, p = where_ref[0], where_ref[1]
    copies = []
    for i in range(16):
        half, group = group_of(t, (p + i // 4) % 4, i % 4)
        rows = pl.ds(pl.multiple_of((half * 16 + group) * 64, 64), 64)
        copies.append(pltpu.make_async_copy(key_ref.at[:, rows], keys.at[i], sems.at[i]))
        rows = pl.ds(pl.multiple_of(group // 2 * 8, 8), 8)
        columns = pl.ds(pl.multiple_of((half * 2 + group % 2) * 512, 512), 512)
        copies.append(
            pltpu.make_async_copy(
                router_ref.at[:, rows, columns], routers.at[i], sems.at[16 + i]
            )
        )
    gain_copy = pltpu.make_async_copy(gain_ref, gains, sems.at[32])
    gain_copy.start()
    for copy in copies:
        copy.start()
    lane = lax.broadcasted_iota(jnp.int32, (8, LANES), 1)
    row = lax.broadcasted_iota(jnp.int32, (8, LANES), 0)
    low = lane < 64
    gain_copy.wait()
    gain = gains[...].astype(jnp.float32)
    gain = (gain[0:1] + gain[1:2]).astype(jnp.bfloat16).astype(jnp.float32)
    for half in range(2):
        for z in range(8):
            at = half * 1024 + z * LANES
            line = gain[:, at : at + LANES]
            turned = jnp.concatenate([line[:, 64:], line[:, :64]], axis=1)
            tiles[half, z] = jnp.where(row == 0, line, jnp.where(row == 1, turned, 0.0))
    for i in range(16):
        half, group = group_of(t, (p + i // 4) % 4, i % 4)
        copies[2 * i].wait()
        copies[2 * i + 1].wait()
        key = keys[i, 0].astype(jnp.float32) + keys[i, 1].astype(jnp.float32)
        out_ref[i // 4, i % 4, :, :, :KEY_WIDTH] = key.astype(jnp.bfloat16).reshape(
            8, 8, KEY_WIDTH
        )
        router = routers[i, 0].astype(jnp.float32) + routers[i, 1].astype(jnp.float32)
        for z in range(8):
            tile = router[:, (z // 2) * LANES : (z // 2 + 1) * LANES]
            mine = low if z % 2 == 0 else jnp.logical_not(low)
            kept = jnp.where(group == 0, tiles[half, z], 0.0)
            out_ref[i // 4, i % 4, z, :, KEY_WIDTH:] = jnp.where(mine, tile, kept).astype(
                jnp.bfloat16
            )


def pack(t, p, grads):
    return pl.pallas_call(
        pack_local,
        in_specs=[pl.BlockSpec(memory_space=pltpu.SMEM)]
        + [pl.BlockSpec(memory_space=pltpu.HBM)] * 3,
        out_specs=pl.BlockSpec(memory_space=pltpu.VMEM),
        out_shape=jax.ShapeDtypeStruct((4, 4, 8, 8, ROW), jnp.bfloat16),
        scratch_shapes=[
            pltpu.VMEM((16, 2, 64, KEY_WIDTH), jnp.bfloat16),
            pltpu.VMEM((16, 2, 8, 512), jnp.bfloat16),
            pltpu.VMEM((2, D), jnp.bfloat16),
            pltpu.VMEM((2, 8, 8, LANES), jnp.float32),
            pltpu.SemaphoreType.DMA((33,)),
        ],
        compiler_params=pltpu.CompilerParams(vmem_limit_bytes=4 * 1024 * 1024),
    )(jnp.stack([t, p]), *[pltpu.with_memory_space_constraint(g, pltpu.HBM) for g in grads])


def in_vmem(body, operands, shapes, scalars=()):
    scalars = [jnp.stack(scalars)] if scalars else []
    return pl.pallas_call(
        body,
        in_specs=[pl.BlockSpec(memory_space=pltpu.SMEM)] * len(scalars)
        + [pl.BlockSpec(memory_space=pltpu.VMEM)] * len(operands),
        out_specs=[pl.BlockSpec(memory_space=pltpu.VMEM)] * len(shapes),
        out_shape=[jax.ShapeDtypeStruct(*shape) for shape in shapes],
        compiler_params=pltpu.CompilerParams(vmem_limit_bytes=2 * 1024 * 1024),
    )(*scalars, *operands)


def add_pair(kept_ref, got_ref, *outs):
    for k in range(4):
        for q in range(4):
            total = kept_ref[k, q].astype(jnp.float32) + got_ref[k, q].astype(jnp.float32)
            outs[k][q] = total.astype(jnp.bfloat16)


def spare_lanes(parity):
    lane = lax.broadcasted_iota(jnp.int32, (8, LANES), 1)
    return lane // 64 + parity == 1


def exponent_of(largest):
    largest = jnp.maximum(jnp.broadcast_to(largest, (8, LANES)), 1e-30)
    return jnp.floor(jnp.log(largest) * (1.0 / math.log(2.0))) - 13.0


def largest_of(x):
    return jnp.max(jnp.max(jnp.abs(x), axis=1, keepdims=True), axis=0, keepdims=True)


def sum_encoded(where_ref, *refs):
    terms, out_ref = refs[:4], refs[4]
    largest = jnp.zeros((8, ROW), jnp.float32)
    for q in range(4):
        for z in range(8):
            total = terms[0][q, z].astype(jnp.float32)
            for term in terms[1:]:
                total = total + term[q, z].astype(jnp.float32)
            out_ref[q * 8 + z] = total
            largest = jnp.maximum(largest, jnp.abs(total))
    exponent = exponent_of(largest_of(largest))
    scale = jnp.concatenate([jnp.exp2(-exponent)] * 5, axis=1)
    row = lax.broadcasted_iota(jnp.int32, (8, LANES), 0)
    for b in range(32):
        own = out_ref[b] * scale
        spare = spare_lanes(b % 2) & (row == 7)
        out_ref[b, :, :KEY_WIDTH] = own[:, :KEY_WIDTH]
        out_ref[b, :, KEY_WIDTH:] = jnp.where(spare, exponent, own[:, KEY_WIDTH:])


def encode(where_ref, blocks_ref, out_ref):
    parity = where_ref[0]
    row = lax.broadcasted_iota(jnp.int32, (8, LANES), 0)
    own = jnp.zeros((8, ROW), jnp.float32)
    for b in range(32):
        block = blocks_ref[b]
        scale = scale_of(block[:, KEY_WIDTH:], parity)
        own = own + block * jnp.concatenate([scale] * 5, axis=1)
    spare = spare_lanes(parity) & (row >= 5)
    key, tile = own[:, :KEY_WIDTH], jnp.where(spare, 0.0, own[:, KEY_WIDTH:])
    own = jnp.concatenate([key, tile], axis=1)
    exponent = exponent_of(largest_of(own))
    own = own * jnp.concatenate([jnp.exp2(-exponent)] * 5, axis=1)
    squares = jnp.sum(jnp.sum(own * own, axis=1, keepdims=True), axis=0, keepdims=True)
    squares = jnp.broadcast_to(squares, (8, LANES)) * 2.0**-30
    digit = squares.astype(jnp.bfloat16).astype(jnp.float32)
    notes = jnp.where(row == 7, exponent, jnp.where(row == 6, digit, (squares - digit) * 256.0))
    out_ref[:, :KEY_WIDTH] = own[:, :KEY_WIDTH]
    out_ref[:, KEY_WIDTH:] = jnp.where(spare, notes, own[:, KEY_WIDTH:])


def add_squares(blocks_ref, out_ref):
    totals = [jnp.zeros((1, LANES), jnp.float32)] * 2
    for b in range(64):
        tile = blocks_ref[b, :, KEY_WIDTH:]
        digits = tile[6:7] + tile[5:6] * (1.0 / 256.0)
        totals[b % 2] = totals[b % 2] + digits * jnp.exp2(2.0 * tile[7:8] + 30.0)
    lane = lax.broadcasted_iota(jnp.int32, (1, LANES), 1)
    total = jnp.where(lane == 64, totals[0], 0.0) + jnp.where(lane == 0, totals[1], 0.0)
    out_ref[...] = jnp.broadcast_to(jnp.sum(total, axis=1, keepdims=True), (8, LANES))


def scale_of(tile, parity):
    line = tile[7:8]
    turned = jnp.concatenate([line[:, 64:], line[:, :64]], axis=1)
    lane = lax.broadcasted_iota(jnp.int32, (1, LANES), 1)
    line = jnp.where(lane // 64 + parity == 1, line, turned)
    return jnp.exp2(jnp.broadcast_to(line, (8, LANES)))


def gain_line(tile, z):
    first, second = tile[0:1], tile[1:2]
    turned = jnp.concatenate([second[:, 64:], second[:, :64]], axis=1)
    lane = lax.broadcasted_iota(jnp.int32, (1, LANES), 1)
    if z % 2 == 0:
        return jnp.where(lane < 64, turned, first)
    return jnp.where(lane < 64, first, turned)


def clip_factor(squares):
    total = (squares[0][...] + squares[1][...]) + (squares[2][...] + squares[3][...])
    clip_limit = 0.5 * math.sqrt(D * KEY_WIDTH + EXPERTS * D + D)
    return clip_limit / jnp.maximum(jnp.sqrt(total), clip_limit)


def update_rows(where_ref, squares, blocks_ref, ins, outs, messages, keys, routers, sems):
    t, half = where_ref[0], where_ref[1]
    factor = clip_factor(squares)
    key_ins, router_ins, gain_ins = ins[:3], ins[3:6], ins[6:]
    key_outs, router_outs, key_weight, router_weight = outs[:3], outs[3:6], outs[6], outs[7]
    gain_outs = outs[8:]
    low = lax.broadcasted_iota(jnp.int32, (8, LANES), 1) < 64

    def key_rows(g, base=0):
        return pl.ds(pl.multiple_of(base + t * 512 + g * 64, 64), 64)

    router_rows = pl.ds(pl.multiple_of(t * 32, 32), 32)
    stores = []

    def store(source, target):
        copy = pltpu.make_async_copy(source, target, sems.at[len(stores)])
        copy.start()
        stores.append(copy)

    row = lax.broadcasted_iota(jnp.int32, (8, LANES), 0)
    scaled = jnp.zeros((8, LANES), jnp.float32)
    for z in range(8):
        tile = blocks_ref[z, :, KEY_WIDTH:]
        scaled = jnp.where(row == z, gain_line(tile * (scale_of(tile, z % 2) * factor), z), scaled)
    new = adamw(*[gain[...] for gain in gain_ins], scaled, 0.0)
    for a in range(3):
        gain_outs[a][...] = new[a]
    messages[0][pl.ds(288, 8), :LANES] = new[0].astype(jnp.bfloat16)
    for g in range(8):
        message, at = messages[g // 4], g % 4
        tiles = []
        for z in range(8):
            tile = blocks_ref[g * 8 + z, :, KEY_WIDTH:]
            scale = scale_of(tile, z % 2) * factor
            tiles.append(tile * scale)
            scaled = blocks_ref[g * 8 + z, :, :KEY_WIDTH] * jnp.concatenate([scale] * 4, axis=1)
            rows = pl.ds(g * 64 + z * 8, 8)
            old = pl.ds(pl.multiple_of(t * 512 + g * 64 + z * 8, 8), 8)
            new = adamw(*[key[old] for key in key_ins], scaled, 0.1)
            for a in range(3):
                keys[a, rows] = new[a]
            message[pl.ds(at * 64 + z * 8, 8)] = new[0].astype(jnp.bfloat16)
        scaled = jnp.concatenate(
            [jnp.where(low, tiles[2 * i], tiles[2 * i + 1]) for i in range(4)], axis=1
        )
        rows, columns = pl.ds(g // 2 * 8, 8), pl.ds(g % 2 * 512, 512)
        old = pl.ds(pl.multiple_of(t * 32 + g // 2 * 8, 8), 8)
        new = adamw(*[router[old, columns] for router in router_ins], scaled, 0.1)
        for a in range(3):
            routers[a, rows, columns] = new[a]
        message[pl.ds(256 + at * 8, 8)] = new[0].astype(jnp.bfloat16)
        for a in range(3):
            store(keys.at[a, pl.ds(g * 64, 64)], key_outs[a].at[key_rows(g)])
        if at == 3:
            write_message(t, half, g // 4, message, key_weight, router_weight, store)
    for a in range(3):
        store(routers.at[a], router_outs[a].at[router_rows])
    for copy in stores:
        copy.wait()


def write_message(t, half, which, message, key_weight, router_weight, store):
    rows = pl.ds(pl.multiple_of(half * 1024 + t * 512 + which * 256, 256), 256)
    store(message.at[pl.ds(0, 256)], key_weight.at[rows])
    for i in range(4):
        rows = pl.ds(pl.multiple_of(t * 32 + (which * 2 + i // 2) * 8, 8), 8)
        columns = pl.ds(pl.multiple_of(half * 1024 + i % 2 * 512, 512), 512)
        store(message.at[pl.ds(256 + i * 8, 8)], router_weight.at[rows, columns])


def update_first(where_ref, *refs):
    squares, blocks_ref, ins = refs[:4], refs[4], refs[5:14]
    outs, messages, scratch = refs[14:25], refs[25:27], refs[27:]
    update_rows(where_ref, squares, blocks_ref, ins, outs, messages, *scratch)


def update_second(where_ref, *refs):
    squares, blocks_ref, ins = refs[:4], refs[4], refs[5:14]
    outs, scratch = refs[22:33], refs[33:]
    update_rows(where_ref, squares, blocks_ref, ins, outs, scratch[:2], *scratch[2:])


def write_received(where_ref, far0, far1, near0, near1, *refs):
    first_gains, second_gains = refs[:3], refs[3:6]
    key_weight, router_weight, gain_outs, gain_weight, sems = *refs[8:10], refs[10:13], *refs[13:]
    t, half = where_ref[0], where_ref[1]
    stores = []

    def store(source, target):
        copy = pltpu.make_async_copy(source, target, sems.at[len(stores)])
        copy.start()
        stores.append(copy)

    write_message(t, 1 - half, 0, far0, key_weight, router_weight, store)
    write_message(t, 1 - half, 1, far1, key_weight, router_weight, store)
    write_message(1 - t, 1 - half, 0, near0, key_weight, router_weight, store)
    write_message(1 - t, 1 - half, 1, near1, key_weight, router_weight, store)
    for a in range(3):
        gain_outs[a][...] = jnp.where(t == 0, first_gains[a][...], second_gains[a][...])
    rows = pl.ds(288, 8)
    far, near = far0[rows, :LANES].astype(jnp.float32), near0[rows, :LANES].astype(jnp.float32)
    far, mine = jnp.where(t == 0, far, near), gain_outs[0][...]
    gain_weight[:8] = jnp.where(half == 0, mine, far).astype(jnp.bfloat16)
    gain_weight[8:] = jnp.where(half == 0, far, mine).astype(jnp.bfloat16)
    for copy in stores:
        copy.wait()


IN_VMEM = pl.BlockSpec(memory_space=pltpu.VMEM)
IN_HBM = pl.BlockSpec(memory_space=pltpu.HBM)
IN_SMEM = pl.BlockSpec(memory_space=pltpu.SMEM)
MESSAGES = [((296, KEY_WIDTH), jnp.bfloat16), ((288, KEY_WIDTH), jnp.bfloat16)]


def in_hbm(arrays):
    return [pltpu.with_memory_space_constraint(a, pltpu.HBM) for a in arrays]


def updated(core, half, squares, parts, other, states, gains):
    shapes = [jax.ShapeDtypeStruct(a.shape, jnp.float32) for a in states]
    shapes += [
        jax.ShapeDtypeStruct((D, KEY_WIDTH), jnp.bfloat16),
        jax.ShapeDtypeStruct((EXPERTS, D), jnp.bfloat16),
    ]
    gain_shapes = [jax.ShapeDtypeStruct((8, LANES), jnp.float32)] * 3
    scratch = [
        pltpu.VMEM((3, 512, KEY_WIDTH), jnp.float32),
        pltpu.VMEM((3, 32, 1024), jnp.float32),
        pltpu.SemaphoreType.DMA((37,)),
    ]
    params = pltpu.CompilerParams(vmem_limit_bytes=6 * 1024 * 1024)
    cost = pl.CostEstimate(flops=7_000_000, bytes_accessed=8_000_000, transcendentals=600_000)
    outs = pl.pallas_call(
        update_first,
        in_specs=[IN_SMEM] + [IN_VMEM] * 14,
        out_specs=[IN_HBM] * 8 + [IN_VMEM] * 5,
        out_shape=shapes + gain_shapes + [jax.ShapeDtypeStruct(*m) for m in MESSAGES],
        scratch_shapes=scratch,
        compiler_params=params,
        cost_estimate=cost,
    )(jnp.stack([core, half]), *squares, parts, *states, *gains)
    outs, first_gains, sent = outs[:8], outs[8:11], outs[11:]
    far = [send(sent[0], PARTNER), send(sent[1], OTHER_PARTNER)]
    outs = pl.pallas_call(
        update_second,
        in_specs=[IN_SMEM] + [IN_VMEM] * 14 + [IN_HBM] * 8,
        out_specs=[IN_HBM] * 8 + [IN_VMEM] * 3,
        out_shape=shapes + gain_shapes,
        input_output_aliases={15 + i: i for i in range(8)},
        scratch_shapes=[pltpu.VMEM(*m) for m in MESSAGES] + scratch,
        compiler_params=params,
        cost_estimate=cost,
    )(jnp.stack([1 - core, half]), *squares, other, *states, *gains, *outs)
    outs, second_gains = outs[:8], outs[8:]
    far0, far1, gain_new = lax.optimization_barrier((*far, second_gains[0]))
    far, second_gains = [far0, far1], [gain_new, *second_gains[1:]]
    near = [send(a, SIBLING) for a in far]
    key_weight, router_weight, *gains, gain_weight = pl.pallas_call(
        write_received,
        in_specs=[IN_SMEM] + [IN_VMEM] * 10 + [IN_HBM] * 2,
        out_specs=[IN_HBM] * 2 + [IN_VMEM] * 4,
        out_shape=shapes[6:] + gain_shapes + [jax.ShapeDtypeStruct((16, LANES), jnp.bfloat16)],
        input_output_aliases={11: 0, 12: 1},
        scratch_shapes=[pltpu.SemaphoreType.DMA((20,))],
        compiler_params=pltpu.CompilerParams(vmem_limit_bytes=2 * 1024 * 1024),
    )(jnp.stack([core, half]), *far, *near, *first_gains, *second_gains, *outs[6:])
    return outs[:6], gains, key_weight, router_weight, gain_weight


def on_device(
    key_grads,
    router_grads,
    gain_grads,
    key_master,
    key_first,
    key_second,
    router_master,
    router_first,
    router_second,
    gain_master,
    gain_first,
    gain_second,
):
    core = lax.axis_index("c")
    half = lax.axis_index("xl")
    x = lax.axis_index("xh") * 2 + half
    y = lax.axis_index("y")
    z = lax.axis_index("z")
    grads = (key_grads[0, 0], router_grads[0, 0], gain_grads[0, 0])
    first_place = jnp.where(core == 0, x, y)
    second_place = jnp.where(core == 0, y, x)
    got = send(pack(1 - core, second_place, grads), SIBLING)
    kept = pack(core, first_place, grads)
    parts = in_vmem(add_pair, [kept, got], [((4, 8, 8, ROW), jnp.bfloat16)] * 4)
    states = [key_master, key_first, key_second, router_master, router_first, router_second]
    parts = [parts[0]] + [send(parts[k], along(k)) for k in (1, 2, 3)]
    [code] = in_vmem(sum_encoded, parts, [((32, 8, ROW), jnp.float32)], [z])
    code = lax.all_to_all(
        code.astype(jnp.float16), ALL, 0, 0, axis_index_groups=SECOND_GROUPS, tiled=True
    )
    [code] = in_vmem(encode, [code.astype(jnp.float32)], [((8, ROW), jnp.float32)], [z & 1])
    parts = lax.all_to_all(
        jnp.broadcast_to(code.astype(jnp.float16)[None], (64, 8, ROW)),
        ("xh", "y", "z"),
        0,
        0,
        tiled=True,
    )
    other = send(parts, SIBLING).astype(jnp.float32)
    parts = parts.astype(jnp.float32)
    [squares] = in_vmem(add_squares, [parts], [((8, LANES), jnp.float32)])
    squares = [squares] + [send(squares, to) for to in (SIBLING, PARTNER, PARTNER_SIBLING)]
    states, gains, key_weight, router_weight, gain_weight = updated(
        core,
        half,
        squares,
        parts,
        other,
        states,
        [gain.reshape(8, LANES) for gain in (gain_master, gain_first, gain_second)],
    )
    gains = [gain.reshape(1024) for gain in gains]
    return (*states, *gains, key_weight, router_weight, gain_weight.reshape(D))


def solution(mesh):
    fine = Mesh(np.asarray(mesh.devices).reshape(8, 4, 2, 2, 2), ("z", "y", "xh", "c", "xl"))
    in_specs = (
        P(WIDE, "xl", None, None, None),
        P(WIDE, "xl", None, None, None),
        P(WIDE, "xl", None, None),
        P("xl", None),
        P("xl", None),
        P("xl", None),
        P(None, "xl"),
        P(None, "xl"),
        P(None, "xl"),
        P("xl"),
        P("xl"),
        P("xl"),
    )
    out_specs = (
        P("xl", None),
        P("xl", None),
        P("xl", None),
        P(None, "xl"),
        P(None, "xl"),
        P(None, "xl"),
        P("xl"),
        P("xl"),
        P("xl"),
        P(),
        P(),
        P(),
    )
    return jax.shard_map(
        on_device, mesh=fine, in_specs=in_specs, out_specs=out_specs, check_vma=False
    )
```

```python
import math

import jax
import jax.numpy as jnp
import numpy as np
from jax import lax
from jax.experimental import pallas as pl
from jax.experimental.pallas import tpu as pltpu
from jax.sharding import Mesh
from jax.sharding import PartitionSpec as P

D = 2048
KEY_WIDTH = 512
EXPERTS = 64
LANES = 128
ROW = KEY_WIDTH + LANES

beta_one = 0.9
beta_two = 0.95
step_rate = 0.01
epsilon = 1e-08
bias_one = 1.0 - 0.9**10
bias_two = 1.0 - 0.95**10

WIDE = ("z", "y", "xh", "c")
ALL = ("z", "y", "xh", "c", "xl")


def place(z, y, x, c):
    return (((z * 4 + y) * 2 + x // 2) * 2 + c) * 2 + x % 2


def permutation(target):
    return [
        (place(z, y, x, c), place(*target(z, y, x, c)))
        for z in range(8)
        for y in range(4)
        for x in range(4)
        for c in range(2)
    ]


def along(shift):
    def target(z, y, x, c):
        if c == 0:
            return z, y, (x + shift) % 4, c
        return z, (y + shift) % 4, x, c

    return permutation(target)


SECOND_GROUPS = [
    [place(z, q, p, c) if c == 0 else place(z, p, q, c) for q in range(4) for z in range(8)]
    for c in range(2)
    for p in range(4)
]
SIBLING = permutation(lambda z, y, x, c: (z, y, x, 1 - c))
PARTNER = permutation(lambda z, y, x, c: (z, y, x ^ 1, c))
OTHER_PARTNER = permutation(lambda z, y, x, c: (z, y, x ^ 3, c))
PARTNER_SIBLING = permutation(lambda z, y, x, c: (z, y, x ^ 1, 1 - c))


def send(x, pairs):
    return lax.ppermute(x, ALL, pairs)


def adamw(master, first_moment, second, scaled, decay_rate):
    first_new = beta_one * first_moment + (1.0 - beta_one) * scaled
    second_new = beta_two * second + (1.0 - beta_two) * scaled * scaled
    root = jnp.sqrt(second_new * (1.0 / bias_two)) + epsilon
    kept = master if decay_rate == 0.0 else master * (1.0 - step_rate * decay_rate)
    master_new = kept - first_new * (step_rate / bias_one) / root
    return (master_new, first_new, second_new)


def group_of(t, p, q):
    x = jnp.where(t == 0, p, q)
    y = jnp.where(t == 0, q, p)
    return x % 2, t * 8 + (x // 2) * 4 + y


def micro_total(stack):
    return (stack[0].astype(jnp.float32) + stack[1].astype(jnp.float32)).astype(jnp.bfloat16)


def pack_local(where_ref, key_ref, router_ref, gain_ref, out_ref, keys, routers, gains, tiles, sems):
    t, p = where_ref[0], where_ref[1]
    copies = []
    for i in range(16):
        half, group = group_of(t, (p + i // 4) % 4, i % 4)
        rows = pl.ds(pl.multiple_of((half * 16 + group) * 64, 64), 64)
        copies.append(pltpu.make_async_copy(key_ref.at[:, rows], keys.at[i], sems.at[i]))
        rows = pl.ds(pl.multiple_of(group // 2 * 8, 8), 8)
        columns = pl.ds(pl.multiple_of((half * 2 + group % 2) * 512, 512), 512)
        copies.append(
            pltpu.make_async_copy(
                router_ref.at[:, rows, columns], routers.at[i], sems.at[16 + i]
            )
        )
    gain_copy = pltpu.make_async_copy(gain_ref, gains, sems.at[32])
    gain_copy.start()
    for copy in copies:
        copy.start()
    lane = lax.broadcasted_iota(jnp.int32, (8, LANES), 1)
    row = lax.broadcasted_iota(jnp.int32, (8, LANES), 0)
    low = lane < 64
    gain_copy.wait()
    gain = gains[...].astype(jnp.float32)
    gain = (gain[0:1] + gain[1:2]).astype(jnp.bfloat16).astype(jnp.float32)
    for half in range(2):
        for z in range(8):
            at = half * 1024 + z * LANES
            line = gain[:, at : at + LANES]
            turned = jnp.concatenate([line[:, 64:], line[:, :64]], axis=1)
            tiles[half, z] = jnp.where(row == 0, line, jnp.where(row == 1, turned, 0.0))
    for i in range(16):
        half, group = group_of(t, (p + i // 4) % 4, i % 4)
        copies[2 * i].wait()
        copies[2 * i + 1].wait()
        key = keys[i, 0].astype(jnp.float32) + keys[i, 1].astype(jnp.float32)
        out_ref[i // 4, i % 4, :, :, :KEY_WIDTH] = key.astype(jnp.bfloat16).reshape(
            8, 8, KEY_WIDTH
        )
        router = routers[i, 0].astype(jnp.float32) + routers[i, 1].astype(jnp.float32)
        for z in range(8):
            tile = router[:, (z // 2) * LANES : (z // 2 + 1) * LANES]
            mine = low if z % 2 == 0 else jnp.logical_not(low)
            kept = jnp.where(group == 0, tiles[half, z], 0.0)
            out_ref[i // 4, i % 4, z, :, KEY_WIDTH:] = jnp.where(mine, tile, kept).astype(
                jnp.bfloat16
            )


def pack(t, p, grads):
    return pl.pallas_call(
        pack_local,
        in_specs=[pl.BlockSpec(memory_space=pltpu.SMEM)]
        + [pl.BlockSpec(memory_space=pltpu.HBM)] * 3,
        out_specs=pl.BlockSpec(memory_space=pltpu.VMEM),
        out_shape=jax.ShapeDtypeStruct((4, 4, 8, 8, ROW), jnp.bfloat16),
        scratch_shapes=[
            pltpu.VMEM((16, 2, 64, KEY_WIDTH), jnp.bfloat16),
            pltpu.VMEM((16, 2, 8, 512), jnp.bfloat16),
            pltpu.VMEM((2, D), jnp.bfloat16),
            pltpu.VMEM((2, 8, 8, LANES), jnp.float32),
            pltpu.SemaphoreType.DMA((33,)),
        ],
        compiler_params=pltpu.CompilerParams(vmem_limit_bytes=4 * 1024 * 1024),
    )(jnp.stack([t, p]), *[pltpu.with_memory_space_constraint(g, pltpu.HBM) for g in grads])


def in_vmem(body, operands, shapes, scalars=()):
    scalars = [jnp.stack(scalars)] if scalars else []
    return pl.pallas_call(
        body,
        in_specs=[pl.BlockSpec(memory_space=pltpu.SMEM)] * len(scalars)
        + [pl.BlockSpec(memory_space=pltpu.VMEM)] * len(operands),
        out_specs=[pl.BlockSpec(memory_space=pltpu.VMEM)] * len(shapes),
        out_shape=[jax.ShapeDtypeStruct(*shape) for shape in shapes],
        compiler_params=pltpu.CompilerParams(vmem_limit_bytes=2 * 1024 * 1024),
    )(*scalars, *operands)


def add_pair(kept_ref, got_ref, *outs):
    for k in range(4):
        for q in range(4):
            total = kept_ref[k, q].astype(jnp.float32) + got_ref[k, q].astype(jnp.float32)
            outs[k][q] = total.astype(jnp.bfloat16)


def spare_lanes(parity):
    lane = lax.broadcasted_iota(jnp.int32, (8, LANES), 1)
    return lane // 64 + parity == 1


def exponent_of(largest):
    largest = jnp.maximum(jnp.broadcast_to(largest, (8, LANES)), 1e-30)
    return jnp.floor(jnp.log(largest) * (1.0 / math.log(2.0))) - 13.0


def largest_of(x):
    return jnp.max(jnp.max(jnp.abs(x), axis=1, keepdims=True), axis=0, keepdims=True)


def sum_encoded(where_ref, *refs):
    terms, out_ref = refs[:4], refs[4]
    largest = jnp.zeros((8, ROW), jnp.float32)
    for q in range(4):
        for z in range(8):
            total = terms[0][q, z].astype(jnp.float32)
            for term in terms[1:]:
                total = total + term[q, z].astype(jnp.float32)
            out_ref[q * 8 + z] = total
            largest = jnp.maximum(largest, jnp.abs(total))
    exponent = exponent_of(largest_of(largest))
    scale = jnp.concatenate([jnp.exp2(-exponent)] * 5, axis=1)
    row = lax.broadcasted_iota(jnp.int32, (8, LANES), 0)
    for b in range(32):
        own = out_ref[b] * scale
        spare = spare_lanes(b % 2) & (row == 7)
        out_ref[b, :, :KEY_WIDTH] = own[:, :KEY_WIDTH]
        out_ref[b, :, KEY_WIDTH:] = jnp.where(spare, exponent, own[:, KEY_WIDTH:])


def encode(where_ref, blocks_ref, out_ref):
    parity = where_ref[0]
    row = lax.broadcasted_iota(jnp.int32, (8, LANES), 0)
    own = jnp.zeros((8, ROW), jnp.float32)
    for b in range(32):
        block = blocks_ref[b]
        scale = scale_of(block[:, KEY_WIDTH:], parity)
        own = own + block * jnp.concatenate([scale] * 5, axis=1)
    spare = spare_lanes(parity) & (row >= 5)
    key, tile = own[:, :KEY_WIDTH], jnp.where(spare, 0.0, own[:, KEY_WIDTH:])
    own = jnp.concatenate([key, tile], axis=1)
    exponent = exponent_of(largest_of(own))
    own = own * jnp.concatenate([jnp.exp2(-exponent)] * 5, axis=1)
    squares = jnp.sum(jnp.sum(own * own, axis=1, keepdims=True), axis=0, keepdims=True)
    squares = jnp.broadcast_to(squares, (8, LANES)) * 2.0**-30
    digit = squares.astype(jnp.bfloat16).astype(jnp.float32)
    notes = jnp.where(row == 7, exponent, jnp.where(row == 6, digit, (squares - digit) * 256.0))
    out_ref[:, :KEY_WIDTH] = own[:, :KEY_WIDTH]
    out_ref[:, KEY_WIDTH:] = jnp.where(spare, notes, own[:, KEY_WIDTH:])


def add_squares(blocks_ref, out_ref):
    totals = [jnp.zeros((1, LANES), jnp.float32)] * 2
    for b in range(64):
        tile = blocks_ref[b, :, KEY_WIDTH:]
        digits = tile[6:7] + tile[5:6] * (1.0 / 256.0)
        totals[b % 2] = totals[b % 2] + digits * jnp.exp2(2.0 * tile[7:8] + 30.0)
    lane = lax.broadcasted_iota(jnp.int32, (1, LANES), 1)
    total = jnp.where(lane == 64, totals[0], 0.0) + jnp.where(lane == 0, totals[1], 0.0)
    out_ref[...] = jnp.broadcast_to(jnp.sum(total, axis=1, keepdims=True), (8, LANES))


def scale_of(tile, parity):
    line = tile[7:8]
    turned = jnp.concatenate([line[:, 64:], line[:, :64]], axis=1)
    lane = lax.broadcasted_iota(jnp.int32, (1, LANES), 1)
    line = jnp.where(lane // 64 + parity == 1, line, turned)
    return jnp.exp2(jnp.broadcast_to(line, (8, LANES)))


def gain_line(tile, z):
    first, second = tile[0:1], tile[1:2]
    turned = jnp.concatenate([second[:, 64:], second[:, :64]], axis=1)
    lane = lax.broadcasted_iota(jnp.int32, (1, LANES), 1)
    if z % 2 == 0:
        return jnp.where(lane < 64, turned, first)
    return jnp.where(lane < 64, first, turned)


def clip_factor(squares):
    total = (squares[0][...] + squares[1][...]) + (squares[2][...] + squares[3][...])
    clip_limit = 0.5 * math.sqrt(D * KEY_WIDTH + EXPERTS * D + D)
    return clip_limit / jnp.maximum(jnp.sqrt(total), clip_limit)


def update_rows(where_ref, squares, blocks_ref, ins, outs, messages, keys, routers, sems):
    t, half = where_ref[0], where_ref[1]
    factor = clip_factor(squares)
    key_ins, router_ins, gain_ins = ins[:3], ins[3:6], ins[6:]
    key_outs, router_outs, key_weight, router_weight = outs[:3], outs[3:6], outs[6], outs[7]
    gain_outs = outs[8:]
    low = lax.broadcasted_iota(jnp.int32, (8, LANES), 1) < 64

    def key_rows(g, base=0):
        return pl.ds(pl.multiple_of(base + t * 512 + g * 64, 64), 64)

    router_rows = pl.ds(pl.multiple_of(t * 32, 32), 32)
    stores = []

    def store(source, target):
        copy = pltpu.make_async_copy(source, target, sems.at[len(stores)])
        copy.start()
        stores.append(copy)

    row = lax.broadcasted_iota(jnp.int32, (8, LANES), 0)
    scaled = jnp.zeros((8, LANES), jnp.float32)
    for z in range(8):
        tile = blocks_ref[z, :, KEY_WIDTH:]
        scaled = jnp.where(row == z, gain_line(tile * (scale_of(tile, z % 2) * factor), z), scaled)
    new = adamw(*[gain[...] for gain in gain_ins], scaled, 0.0)
    for a in range(3):
        gain_outs[a][...] = new[a]
    messages[0][pl.ds(288, 8), :LANES] = new[0].astype(jnp.bfloat16)
    for g in range(8):
        message, at = messages[g // 4], g % 4
        tiles = []
        for z in range(8):
            tile = blocks_ref[g * 8 + z, :, KEY_WIDTH:]
            scale = scale_of(tile, z % 2) * factor
            tiles.append(tile * scale)
            scaled = blocks_ref[g * 8 + z, :, :KEY_WIDTH] * jnp.concatenate([scale] * 4, axis=1)
            rows = pl.ds(g * 64 + z * 8, 8)
            old = pl.ds(pl.multiple_of(t * 512 + g * 64 + z * 8, 8), 8)
            new = adamw(*[key[old] for key in key_ins], scaled, 0.1)
            for a in range(3):
                keys[a, rows] = new[a]
            message[pl.ds(at * 64 + z * 8, 8)] = new[0].astype(jnp.bfloat16)
        scaled = jnp.concatenate(
            [jnp.where(low, tiles[2 * i], tiles[2 * i + 1]) for i in range(4)], axis=1
        )
        rows, columns = pl.ds(g // 2 * 8, 8), pl.ds(g % 2 * 512, 512)
        old = pl.ds(pl.multiple_of(t * 32 + g // 2 * 8, 8), 8)
        new = adamw(*[router[old, columns] for router in router_ins], scaled, 0.1)
        for a in range(3):
            routers[a, rows, columns] = new[a]
        message[pl.ds(256 + at * 8, 8)] = new[0].astype(jnp.bfloat16)
        for a in range(3):
            store(keys.at[a, pl.ds(g * 64, 64)], key_outs[a].at[key_rows(g)])
        if at == 3:
            write_message(t, half, g // 4, message, key_weight, router_weight, store)
    for a in range(3):
        store(routers.at[a], router_outs[a].at[router_rows])
    for copy in stores:
        copy.wait()


def write_message(t, half, which, message, key_weight, router_weight, store):
    rows = pl.ds(pl.multiple_of(half * 1024 + t * 512 + which * 256, 256), 256)
    store(message.at[pl.ds(0, 256)], key_weight.at[rows])
    for i in range(4):
        rows = pl.ds(pl.multiple_of(t * 32 + (which * 2 + i // 2) * 8, 8), 8)
        columns = pl.ds(pl.multiple_of(half * 1024 + i % 2 * 512, 512), 512)
        store(message.at[pl.ds(256 + i * 8, 8)], router_weight.at[rows, columns])


def update_first(where_ref, *refs):
    squares, blocks_ref, ins = refs[:4], refs[4], refs[5:14]
    outs, messages, scratch = refs[14:25], refs[25:27], refs[27:]
    update_rows(where_ref, squares, blocks_ref, ins, outs, messages, *scratch)


def update_second(where_ref, *refs):
    squares, blocks_ref, ins = refs[:4], refs[4], refs[5:14]
    outs, scratch = refs[22:33], refs[33:]
    update_rows(where_ref, squares, blocks_ref, ins, outs, scratch[:2], *scratch[2:])


def write_two(t, half, messages, key_weight, router_weight, sems):
    stores = []

    def store(source, target):
        copy = pltpu.make_async_copy(source, target, sems.at[len(stores)])
        copy.start()
        stores.append(copy)

    for i in range(2):
        write_message(t, 1 - half, i, messages[i], key_weight, router_weight, store)
    return stores


def write_far(where_ref, far0, far1, *refs):
    first_gains, second_gains = refs[:3], refs[3:6]
    key_weight, router_weight, gain_outs, sems = *refs[8:10], refs[10:13], refs[13]
    stores = write_two(where_ref[0], where_ref[1], (far0, far1), key_weight, router_weight, sems)
    for a in range(3):
        first, second = first_gains[a][...], second_gains[a][...]
        gain_outs[a][...] = jnp.where(where_ref[0] == 0, first, second)
    for copy in stores:
        copy.wait()


def write_near(where_ref, near0, near1, far0, first_gain, second_gain, *refs):
    key_weight, router_weight, gain_weight, sems = refs[2:]
    t, half = where_ref[0], where_ref[1]
    stores = write_two(1 - t, half, (near0, near1), key_weight, router_weight, sems)
    rows = pl.ds(288, 8)
    far, near = far0[rows, :LANES].astype(jnp.float32), near0[rows, :LANES].astype(jnp.float32)
    far = jnp.where(t == 0, far, near)
    mine = jnp.where(t == 0, first_gain[...], second_gain[...])
    gain_weight[:8] = jnp.where(half == 0, mine, far).astype(jnp.bfloat16)
    gain_weight[8:] = jnp.where(half == 0, far, mine).astype(jnp.bfloat16)
    for copy in stores:
        copy.wait()


IN_VMEM = pl.BlockSpec(memory_space=pltpu.VMEM)
IN_HBM = pl.BlockSpec(memory_space=pltpu.HBM)
IN_SMEM = pl.BlockSpec(memory_space=pltpu.SMEM)
MESSAGES = [((296, KEY_WIDTH), jnp.bfloat16), ((288, KEY_WIDTH), jnp.bfloat16)]


def in_hbm(arrays):
    return [pltpu.with_memory_space_constraint(a, pltpu.HBM) for a in arrays]


def updated(core, half, squares, parts, other, states, gains):
    shapes = [jax.ShapeDtypeStruct(a.shape, jnp.float32) for a in states]
    shapes += [
        jax.ShapeDtypeStruct((D, KEY_WIDTH), jnp.bfloat16),
        jax.ShapeDtypeStruct((EXPERTS, D), jnp.bfloat16),
    ]
    gain_shapes = [jax.ShapeDtypeStruct((8, LANES), jnp.float32)] * 3
    scratch = [
        pltpu.VMEM((3, 512, KEY_WIDTH), jnp.float32),
        pltpu.VMEM((3, 32, 1024), jnp.float32),
        pltpu.SemaphoreType.DMA((37,)),
    ]
    params = pltpu.CompilerParams(vmem_limit_bytes=6 * 1024 * 1024)
    cost = pl.CostEstimate(flops=7_000_000, bytes_accessed=8_000_000, transcendentals=600_000)
    outs = pl.pallas_call(
        update_first,
        in_specs=[IN_SMEM] + [IN_VMEM] * 14,
        out_specs=[IN_HBM] * 8 + [IN_VMEM] * 5,
        out_shape=shapes + gain_shapes + [jax.ShapeDtypeStruct(*m) for m in MESSAGES],
        scratch_shapes=scratch,
        compiler_params=params,
        cost_estimate=cost,
    )(jnp.stack([core, half]), *squares, parts, *states, *gains)
    outs, first_gains, sent = outs[:8], outs[8:11], outs[11:]
    far = [send(sent[0], PARTNER), send(sent[1], OTHER_PARTNER)]
    outs = pl.pallas_call(
        update_second,
        in_specs=[IN_SMEM] + [IN_VMEM] * 14 + [IN_HBM] * 8,
        out_specs=[IN_HBM] * 8 + [IN_VMEM] * 3,
        out_shape=shapes + gain_shapes,
        input_output_aliases={15 + i: i for i in range(8)},
        scratch_shapes=[pltpu.VMEM(*m) for m in MESSAGES] + scratch,
        compiler_params=params,
        cost_estimate=cost,
    )(jnp.stack([1 - core, half]), *squares, other, *states, *gains, *outs)
    outs, second_gains = outs[:8], outs[8:]
    far0, far1, gain_new = lax.optimization_barrier((*far, second_gains[0]))
    far, second_gains = [far0, far1], [gain_new, *second_gains[1:]]
    near = [send(a, SIBLING) for a in far]
    where = jnp.stack([core, half])
    sems = [pltpu.SemaphoreType.DMA((10,))]
    params = pltpu.CompilerParams(vmem_limit_bytes=2 * 1024 * 1024)
    *weights, gain0, gain1, gain2 = pl.pallas_call(
        write_far,
        in_specs=[IN_SMEM] + [IN_VMEM] * 8 + [IN_HBM] * 2,
        out_specs=[IN_HBM] * 2 + [IN_VMEM] * 3,
        out_shape=shapes[6:] + gain_shapes,
        input_output_aliases={9: 0, 10: 1},
        scratch_shapes=sems,
        compiler_params=params,
        cost_estimate=pl.CostEstimate(flops=0, bytes_accessed=2_000_000, transcendentals=0),
    )(where, *far, *first_gains, *second_gains, *outs[6:])
    key_weight, router_weight, gain_weight = pl.pallas_call(
        write_near,
        in_specs=[IN_SMEM] + [IN_VMEM] * 5 + [IN_HBM] * 2,
        out_specs=[IN_HBM] * 2 + [IN_VMEM],
        out_shape=shapes[6:] + [jax.ShapeDtypeStruct((16, LANES), jnp.bfloat16)],
        input_output_aliases={6: 0, 7: 1},
        scratch_shapes=sems,
        compiler_params=params,
    )(where, *near, far[0], first_gains[0], second_gains[0], *weights)
    gains = [gain0, gain1, gain2]
    return outs[:6], gains, key_weight, router_weight, gain_weight


def on_device(
    key_grads,
    router_grads,
    gain_grads,
    key_master,
    key_first,
    key_second,
    router_master,
    router_first,
    router_second,
    gain_master,
    gain_first,
    gain_second,
):
    core = lax.axis_index("c")
    half = lax.axis_index("xl")
    x = lax.axis_index("xh") * 2 + half
    y = lax.axis_index("y")
    z = lax.axis_index("z")
    grads = (key_grads[0, 0], router_grads[0, 0], gain_grads[0, 0])
    first_place = jnp.where(core == 0, x, y)
    second_place = jnp.where(core == 0, y, x)
    got = send(pack(1 - core, second_place, grads), SIBLING)
    kept = pack(core, first_place, grads)
    parts = in_vmem(add_pair, [kept, got], [((4, 8, 8, ROW), jnp.bfloat16)] * 4)
    states = [key_master, key_first, key_second, router_master, router_first, router_second]
    parts = [parts[0]] + [send(parts[k], along(k)) for k in (1, 2, 3)]
    [code] = in_vmem(sum_encoded, parts, [((32, 8, ROW), jnp.float32)], [z])
    code = lax.all_to_all(
        code.astype(jnp.float16), ALL, 0, 0, axis_index_groups=SECOND_GROUPS, tiled=True
    )
    [code] = in_vmem(encode, [code.astype(jnp.float32)], [((8, ROW), jnp.float32)], [z & 1])
    parts = lax.all_to_all(
        jnp.broadcast_to(code.astype(jnp.float16)[None], (64, 8, ROW)),
        ("xh", "y", "z"),
        0,
        0,
        tiled=True,
    )
    wide_parts = parts.astype(jnp.float32)
    [squares] = in_vmem(add_squares, [wide_parts], [((8, LANES), jnp.float32)])
    squares = [squares] + [send(squares, to) for to in (SIBLING, PARTNER, PARTNER_SIBLING)]
    parts, *squares = lax.optimization_barrier((parts, *squares))
    other = send(parts, SIBLING).astype(jnp.float32)
    states, gains, key_weight, router_weight, gain_weight = updated(
        core,
        half,
        squares,
        wide_parts,
        other,
        states,
        [gain.reshape(8, LANES) for gain in (gain_master, gain_first, gain_second)],
    )
    gains = [gain.reshape(1024) for gain in gains]
    return (*states, *gains, key_weight, router_weight, gain_weight.reshape(D))


def solution(mesh):
    fine = Mesh(np.asarray(mesh.devices).reshape(8, 4, 2, 2, 2), ("z", "y", "xh", "c", "xl"))
    in_specs = (
        P(WIDE, "xl", None, None, None),
        P(WIDE, "xl", None, None, None),
        P(WIDE, "xl", None, None),
        P("xl", None),
        P("xl", None),
        P("xl", None),
        P(None, "xl"),
        P(None, "xl"),
        P(None, "xl"),
        P("xl"),
        P("xl"),
        P("xl"),
    )
    out_specs = (
        P("xl", None),
        P("xl", None),
        P("xl", None),
        P(None, "xl"),
        P(None, "xl"),
        P(None, "xl"),
        P("xl"),
        P("xl"),
        P("xl"),
        P(),
        P(),
        P(),
    )
    return jax.shard_map(
        on_device, mesh=fine, in_specs=in_specs, out_specs=out_specs, check_vma=False
    )
```

```python
import math

import jax
import jax.numpy as jnp
import numpy as np
from jax import lax
from jax.experimental import pallas as pl
from jax.experimental.pallas import tpu as pltpu
from jax.sharding import Mesh
from jax.sharding import PartitionSpec as P

D = 2048
KEY_WIDTH = 512
EXPERTS = 64
LANES = 128
ROW = KEY_WIDTH + LANES

beta_one = 0.9
beta_two = 0.95
step_rate = 0.01
epsilon = 1e-08
bias_one = 1.0 - 0.9**10
bias_two = 1.0 - 0.95**10

WIDE = ("z", "y", "xh", "c")
ALL = ("z", "y", "xh", "c", "xl")


def place(z, y, x, c):
    return (((z * 4 + y) * 2 + x // 2) * 2 + c) * 2 + x % 2


def permutation(target):
    return [
        (place(z, y, x, c), place(*target(z, y, x, c)))
        for z in range(8)
        for y in range(4)
        for x in range(4)
        for c in range(2)
    ]


def along(shift):
    def target(z, y, x, c):
        if c == 0:
            return z, y, (x + shift) % 4, c
        return z, (y + shift) % 4, x, c

    return permutation(target)


SECOND_GROUPS = [
    [place(z, q, p, c) if c == 0 else place(z, p, q, c) for q in range(4) for z in range(8)]
    for c in range(2)
    for p in range(4)
]
SIBLING = permutation(lambda z, y, x, c: (z, y, x, 1 - c))
PARTNER = permutation(lambda z, y, x, c: (z, y, x ^ 1, c))
OTHER_PARTNER = permutation(lambda z, y, x, c: (z, y, x ^ 3, c))
PARTNER_SIBLING = permutation(lambda z, y, x, c: (z, y, x ^ 1, 1 - c))


def send(x, pairs):
    return lax.ppermute(x, ALL, pairs)


def adamw(master, first_moment, second, scaled, decay_rate):
    first_new = beta_one * first_moment + (1.0 - beta_one) * scaled
    second_new = beta_two * second + (1.0 - beta_two) * scaled * scaled
    root = jnp.sqrt(second_new * (1.0 / bias_two)) + epsilon
    kept = master if decay_rate == 0.0 else master * (1.0 - step_rate * decay_rate)
    master_new = kept - first_new * (step_rate / bias_one) / root
    return (master_new, first_new, second_new)


def group_of(t, p, q):
    x = jnp.where(t == 0, p, q)
    y = jnp.where(t == 0, q, p)
    return x % 2, t * 8 + (x // 2) * 4 + y


def micro_total(stack):
    return (stack[0].astype(jnp.float32) + stack[1].astype(jnp.float32)).astype(jnp.bfloat16)


def pack_local(where_ref, key_ref, router_ref, gain_ref, out_ref, keys, routers, gains, tiles, sems):
    t, p = where_ref[0], where_ref[1]
    copies = []
    for i in range(16):
        half, group = group_of(t, (p + i // 4) % 4, i % 4)
        rows = pl.ds(pl.multiple_of((half * 16 + group) * 64, 64), 64)
        copies.append(pltpu.make_async_copy(key_ref.at[:, rows], keys.at[i], sems.at[i]))
        rows = pl.ds(pl.multiple_of(group // 2 * 8, 8), 8)
        columns = pl.ds(pl.multiple_of((half * 2 + group % 2) * 512, 512), 512)
        copies.append(
            pltpu.make_async_copy(
                router_ref.at[:, rows, columns], routers.at[i], sems.at[16 + i]
            )
        )
    gain_copy = pltpu.make_async_copy(gain_ref, gains, sems.at[32])
    gain_copy.start()
    for copy in copies:
        copy.start()
    lane = lax.broadcasted_iota(jnp.int32, (8, LANES), 1)
    row = lax.broadcasted_iota(jnp.int32, (8, LANES), 0)
    low = lane < 64
    gain_copy.wait()
    gain = gains[...].astype(jnp.float32)
    gain = (gain[0:1] + gain[1:2]).astype(jnp.bfloat16).astype(jnp.float32)
    for half in range(2):
        for z in range(8):
            at = half * 1024 + z * LANES
            line = gain[:, at : at + LANES]
            turned = jnp.concatenate([line[:, 64:], line[:, :64]], axis=1)
            tiles[half, z] = jnp.where(row == 0, line, jnp.where(row == 1, turned, 0.0))
    for i in range(16):
        half, group = group_of(t, (p + i // 4) % 4, i % 4)
        copies[2 * i].wait()
        copies[2 * i + 1].wait()
        key = keys[i, 0].astype(jnp.float32) + keys[i, 1].astype(jnp.float32)
        out_ref[i // 4, i % 4, :, :, :KEY_WIDTH] = key.astype(jnp.bfloat16).reshape(
            8, 8, KEY_WIDTH
        )
        router = routers[i, 0].astype(jnp.float32) + routers[i, 1].astype(jnp.float32)
        for z in range(8):
            tile = router[:, (z // 2) * LANES : (z // 2 + 1) * LANES]
            mine = low if z % 2 == 0 else jnp.logical_not(low)
            kept = jnp.where(group == 0, tiles[half, z], 0.0)
            out_ref[i // 4, i % 4, z, :, KEY_WIDTH:] = jnp.where(mine, tile, kept).astype(
                jnp.bfloat16
            )


def pack(t, p, grads):
    return pl.pallas_call(
        pack_local,
        in_specs=[pl.BlockSpec(memory_space=pltpu.SMEM)]
        + [pl.BlockSpec(memory_space=pltpu.HBM)] * 3,
        out_specs=pl.BlockSpec(memory_space=pltpu.VMEM),
        out_shape=jax.ShapeDtypeStruct((4, 4, 8, 8, ROW), jnp.bfloat16),
        scratch_shapes=[
            pltpu.VMEM((16, 2, 64, KEY_WIDTH), jnp.bfloat16),
            pltpu.VMEM((16, 2, 8, 512), jnp.bfloat16),
            pltpu.VMEM((2, D), jnp.bfloat16),
            pltpu.VMEM((2, 8, 8, LANES), jnp.float32),
            pltpu.SemaphoreType.DMA((33,)),
        ],
        compiler_params=pltpu.CompilerParams(vmem_limit_bytes=4 * 1024 * 1024),
    )(jnp.stack([t, p]), *[pltpu.with_memory_space_constraint(g, pltpu.HBM) for g in grads])


def in_vmem(body, operands, shapes, scalars=()):
    scalars = [jnp.stack(scalars)] if scalars else []
    return pl.pallas_call(
        body,
        in_specs=[pl.BlockSpec(memory_space=pltpu.SMEM)] * len(scalars)
        + [pl.BlockSpec(memory_space=pltpu.VMEM)] * len(operands),
        out_specs=[pl.BlockSpec(memory_space=pltpu.VMEM)] * len(shapes),
        out_shape=[jax.ShapeDtypeStruct(*shape) for shape in shapes],
        compiler_params=pltpu.CompilerParams(vmem_limit_bytes=2 * 1024 * 1024),
    )(*scalars, *operands)


def add_pair(kept_ref, got_ref, *outs):
    for k in range(4):
        for q in range(4):
            total = kept_ref[k, q].astype(jnp.float32) + got_ref[k, q].astype(jnp.float32)
            outs[k][q] = total.astype(jnp.bfloat16)


def spare_lanes(parity):
    lane = lax.broadcasted_iota(jnp.int32, (8, LANES), 1)
    return lane // 64 + parity == 1


def exponent_of(largest):
    largest = jnp.maximum(jnp.broadcast_to(largest, (8, LANES)), 1e-30)
    return jnp.floor(jnp.log(largest) * (1.0 / math.log(2.0))) - 13.0


def largest_of(x):
    return jnp.max(jnp.max(jnp.abs(x), axis=1, keepdims=True), axis=0, keepdims=True)


def sum_encoded(where_ref, *refs):
    terms, out_ref = refs[:4], refs[4]
    largest = jnp.zeros((8, ROW), jnp.float32)
    for q in range(4):
        for z in range(8):
            total = terms[0][q, z].astype(jnp.float32)
            for term in terms[1:]:
                total = total + term[q, z].astype(jnp.float32)
            out_ref[q * 8 + z] = total
            largest = jnp.maximum(largest, jnp.abs(total))
    exponent = exponent_of(largest_of(largest))
    scale = jnp.concatenate([jnp.exp2(-exponent)] * 5, axis=1)
    row = lax.broadcasted_iota(jnp.int32, (8, LANES), 0)
    for b in range(32):
        own = out_ref[b] * scale
        spare = spare_lanes(b % 2) & (row == 7)
        out_ref[b, :, :KEY_WIDTH] = own[:, :KEY_WIDTH]
        out_ref[b, :, KEY_WIDTH:] = jnp.where(spare, exponent, own[:, KEY_WIDTH:])


def encode(where_ref, blocks_ref, out_ref):
    parity = where_ref[0]
    row = lax.broadcasted_iota(jnp.int32, (8, LANES), 0)
    own = jnp.zeros((8, ROW), jnp.float32)
    for b in range(32):
        block = blocks_ref[b]
        scale = scale_of(block[:, KEY_WIDTH:], parity)
        own = own + block * jnp.concatenate([scale] * 5, axis=1)
    spare = spare_lanes(parity) & (row >= 5)
    key, tile = own[:, :KEY_WIDTH], jnp.where(spare, 0.0, own[:, KEY_WIDTH:])
    own = jnp.concatenate([key, tile], axis=1)
    exponent = exponent_of(largest_of(own))
    own = own * jnp.concatenate([jnp.exp2(-exponent)] * 5, axis=1)
    squares = jnp.sum(jnp.sum(own * own, axis=1, keepdims=True), axis=0, keepdims=True)
    squares = jnp.broadcast_to(squares, (8, LANES)) * 2.0**-30
    digit = squares.astype(jnp.bfloat16).astype(jnp.float32)
    notes = jnp.where(row == 7, exponent, jnp.where(row == 6, digit, (squares - digit) * 256.0))
    out_ref[:, :KEY_WIDTH] = own[:, :KEY_WIDTH]
    out_ref[:, KEY_WIDTH:] = jnp.where(spare, notes, own[:, KEY_WIDTH:])


def add_squares(blocks_ref, out_ref):
    totals = [jnp.zeros((1, LANES), jnp.float32)] * 2
    for b in range(64):
        tile = blocks_ref[b, :, KEY_WIDTH:]
        digits = tile[6:7] + tile[5:6] * (1.0 / 256.0)
        totals[b % 2] = totals[b % 2] + digits * jnp.exp2(2.0 * tile[7:8] + 30.0)
    lane = lax.broadcasted_iota(jnp.int32, (1, LANES), 1)
    total = jnp.where(lane == 64, totals[0], 0.0) + jnp.where(lane == 0, totals[1], 0.0)
    out_ref[...] = jnp.broadcast_to(jnp.sum(total, axis=1, keepdims=True), (8, LANES))


def scale_of(tile, parity):
    line = tile[7:8]
    turned = jnp.concatenate([line[:, 64:], line[:, :64]], axis=1)
    lane = lax.broadcasted_iota(jnp.int32, (1, LANES), 1)
    line = jnp.where(lane // 64 + parity == 1, line, turned)
    return jnp.exp2(jnp.broadcast_to(line, (8, LANES)))


def gain_line(tile, z):
    first, second = tile[0:1], tile[1:2]
    turned = jnp.concatenate([second[:, 64:], second[:, :64]], axis=1)
    lane = lax.broadcasted_iota(jnp.int32, (1, LANES), 1)
    if z % 2 == 0:
        return jnp.where(lane < 64, turned, first)
    return jnp.where(lane < 64, first, turned)


def clip_factor(squares):
    total = (squares[0][...] + squares[1][...]) + (squares[2][...] + squares[3][...])
    clip_limit = 0.5 * math.sqrt(D * KEY_WIDTH + EXPERTS * D + D)
    return clip_limit / jnp.maximum(jnp.sqrt(total), clip_limit)


def update_rows(where_ref, squares, blocks_ref, ins, outs, after_group=None):
    t = where_ref[0]
    factor = clip_factor(squares)
    key_ins, router_ins, gain_ins = ins[:3], ins[3:6], ins[6:]
    keys, routers, gain_outs, messages = outs[0], outs[1], outs[2:5], outs[5:]
    low = lax.broadcasted_iota(jnp.int32, (8, LANES), 1) < 64
    row = lax.broadcasted_iota(jnp.int32, (8, LANES), 0)
    scaled = jnp.zeros((8, LANES), jnp.float32)
    for z in range(8):
        tile = blocks_ref[z, :, KEY_WIDTH:]
        scaled = jnp.where(row == z, gain_line(tile * (scale_of(tile, z % 2) * factor), z), scaled)
    new = adamw(*[gain[...] for gain in gain_ins], scaled, 0.0)
    for a in range(3):
        gain_outs[a][...] = new[a]
    messages[0][pl.ds(288, 8), :LANES] = new[0].astype(jnp.bfloat16)
    for g in range(8):
        message, at = messages[g // 4], g % 4
        tiles = []
        for z in range(8):
            tile = blocks_ref[g * 8 + z, :, KEY_WIDTH:]
            scale = scale_of(tile, z % 2) * factor
            tiles.append(tile * scale)
            scaled = blocks_ref[g * 8 + z, :, :KEY_WIDTH] * jnp.concatenate([scale] * 4, axis=1)
            rows = pl.ds(g * 64 + z * 8, 8)
            old = pl.ds(pl.multiple_of(t * 512 + g * 64 + z * 8, 8), 8)
            new = adamw(*[key[old] for key in key_ins], scaled, 0.1)
            for a in range(3):
                keys[a, rows] = new[a]
            message[pl.ds(at * 64 + z * 8, 8)] = new[0].astype(jnp.bfloat16)
        scaled = jnp.concatenate(
            [jnp.where(low, tiles[2 * i], tiles[2 * i + 1]) for i in range(4)], axis=1
        )
        rows, columns = pl.ds(g // 2 * 8, 8), pl.ds(g % 2 * 512, 512)
        old = pl.ds(pl.multiple_of(t * 32 + g // 2 * 8, 8), 8)
        new = adamw(*[router[old, columns] for router in router_ins], scaled, 0.1)
        for a in range(3):
            routers[a, rows, columns] = new[a]
        message[pl.ds(256 + at * 8, 8)] = new[0].astype(jnp.bfloat16)
        if after_group is not None:
            after_group(g)


class Stores:
    def __init__(self, sems):
        self.sems, self.copies = sems, []

    def __call__(self, source, target):
        copy = pltpu.make_async_copy(source, target, self.sems.at[len(self.copies)])
        copy.start()
        self.copies.append(copy)

    def wait(self):
        for copy in self.copies:
            copy.wait()


def store_weights(store, t, half, g, message, key_weight, router_weight):
    rows = pl.ds(pl.multiple_of(half * 1024 + t * 512 + g * 64, 64), 64)
    store(message.at[pl.ds(g % 4 * 64, 64)], key_weight.at[rows])
    rows = pl.ds(pl.multiple_of(t * 32 + g // 2 * 8, 8), 8)
    columns = pl.ds(pl.multiple_of(half * 1024 + g % 2 * 512, 512), 512)
    store(message.at[pl.ds(256 + g % 4 * 8, 8)], router_weight.at[rows, columns])


def store_group(store, t, half, g, keys, message, outs):
    rows = pl.ds(pl.multiple_of(t * 512 + g * 64, 64), 64)
    for a in range(3):
        store(keys.at[a, pl.ds(g * 64, 64)], outs[a].at[rows])
    store_weights(store, t, half, g, message, outs[6], outs[7])


def store_routers(store, t, routers, outs):
    rows = pl.ds(pl.multiple_of(t * 32, 32), 32)
    for a in range(3):
        store(routers.at[a], outs[3 + a].at[rows])


def update_first(where_ref, *refs):
    update_rows(where_ref, refs[:4], refs[4], refs[5:14], refs[14:])


def update_second(where_ref, *refs):
    squares, blocks_ref, ins, first = refs[:4], refs[4], refs[5:14], refs[14:18]
    outs, gains, scratch = refs[18:26], refs[26:29], refs[29:]
    keys, routers, messages, sems = scratch[0], scratch[1], scratch[2:4], scratch[4]
    t, half = where_ref[0], where_ref[1]
    store = Stores(sems)
    for g in range(8):
        store_group(store, 1 - t, half, g, first[0], first[2 + g // 4], outs)
    store_routers(store, 1 - t, first[1], outs)
    update_rows(
        where_ref,
        squares,
        blocks_ref,
        ins,
        (keys, routers, *gains, *messages),
        lambda g: store_group(store, t, half, g, keys, messages[g // 4], outs),
    )
    store_routers(store, t, routers, outs)
    store.wait()


def write_received(where_ref, far0, far1, near0, near1, *refs):
    first_gains, second_gains = refs[:3], refs[3:6]
    key_weight, router_weight, gain_outs, gain_weight, sems = *refs[8:10], refs[10:13], *refs[13:]
    t, half = where_ref[0], where_ref[1]
    store = Stores(sems)
    for g in range(8):
        store_weights(store, t, 1 - half, g, (far0, far1)[g // 4], key_weight, router_weight)
        store_weights(store, 1 - t, 1 - half, g, (near0, near1)[g // 4], key_weight, router_weight)
    for a in range(3):
        gain_outs[a][...] = jnp.where(t == 0, first_gains[a][...], second_gains[a][...])
    rows = pl.ds(288, 8)
    far, near = far0[rows, :LANES].astype(jnp.float32), near0[rows, :LANES].astype(jnp.float32)
    far = jnp.where(t == 0, far, near)
    mine = jnp.where(t == 0, first_gains[0][...], second_gains[0][...])
    gain_weight[:8] = jnp.where(half == 0, mine, far).astype(jnp.bfloat16)
    gain_weight[8:] = jnp.where(half == 0, far, mine).astype(jnp.bfloat16)
    store.wait()


IN_VMEM = pl.BlockSpec(memory_space=pltpu.VMEM)
IN_HBM = pl.BlockSpec(memory_space=pltpu.HBM)
IN_SMEM = pl.BlockSpec(memory_space=pltpu.SMEM)
MESSAGES = [((296, KEY_WIDTH), jnp.bfloat16), ((288, KEY_WIDTH), jnp.bfloat16)]


def in_hbm(arrays):
    return [pltpu.with_memory_space_constraint(a, pltpu.HBM) for a in arrays]


def updated(core, half, squares, parts, other, states, gains):
    shapes = [jax.ShapeDtypeStruct(a.shape, jnp.float32) for a in states]
    shapes += [
        jax.ShapeDtypeStruct((D, KEY_WIDTH), jnp.bfloat16),
        jax.ShapeDtypeStruct((EXPERTS, D), jnp.bfloat16),
    ]
    gain_shapes = [jax.ShapeDtypeStruct((8, LANES), jnp.float32)] * 3
    rows = [((3, 512, KEY_WIDTH), jnp.float32), ((3, 32, 1024), jnp.float32)]
    cost = pl.CostEstimate(flops=7_000_000, bytes_accessed=8_000_000, transcendentals=600_000)
    keys, routers, *outs = pl.pallas_call(
        update_first,
        in_specs=[IN_SMEM] + [IN_VMEM] * 14,
        out_specs=[IN_VMEM] * 7,
        out_shape=[jax.ShapeDtypeStruct(*r) for r in rows]
        + gain_shapes
        + [jax.ShapeDtypeStruct(*m) for m in MESSAGES],
        compiler_params=pltpu.CompilerParams(vmem_limit_bytes=2 * 1024 * 1024),
        cost_estimate=cost,
    )(jnp.stack([core, half]), *squares, parts, *states, *gains)
    first_gains, sent = outs[:3], outs[3:]
    far = [send(sent[0], PARTNER), send(sent[1], OTHER_PARTNER)]
    outs = pl.pallas_call(
        update_second,
        in_specs=[IN_SMEM] + [IN_VMEM] * 18,
        out_specs=[IN_HBM] * 8 + [IN_VMEM] * 3,
        out_shape=shapes + gain_shapes,
        scratch_shapes=[pltpu.VMEM(*r) for r in rows + MESSAGES]
        + [pltpu.SemaphoreType.DMA((86,))],
        compiler_params=pltpu.CompilerParams(vmem_limit_bytes=8 * 1024 * 1024),
        cost_estimate=cost,
    )(jnp.stack([1 - core, half]), *squares, other, *states, *gains, keys, routers, *sent)
    outs, second_gains = outs[:8], outs[8:]
    far0, far1, gain_new = lax.optimization_barrier((*far, second_gains[0]))
    far, second_gains = [far0, far1], [gain_new, *second_gains[1:]]
    near = [send(a, SIBLING) for a in far]
    key_weight, router_weight, *gains, gain_weight = pl.pallas_call(
        write_received,
        in_specs=[IN_SMEM] + [IN_VMEM] * 10 + [IN_HBM] * 2,
        out_specs=[IN_HBM] * 2 + [IN_VMEM] * 4,
        out_shape=shapes[6:] + gain_shapes + [jax.ShapeDtypeStruct((16, LANES), jnp.bfloat16)],
        input_output_aliases={11: 0, 12: 1},
        scratch_shapes=[pltpu.SemaphoreType.DMA((32,))],
        compiler_params=pltpu.CompilerParams(vmem_limit_bytes=2 * 1024 * 1024),
    )(jnp.stack([core, half]), *far, *near, *first_gains, *second_gains, *outs[6:])
    return outs[:6], gains, key_weight, router_weight, gain_weight


def on_device(
    key_grads,
    router_grads,
    gain_grads,
    key_master,
    key_first,
    key_second,
    router_master,
    router_first,
    router_second,
    gain_master,
    gain_first,
    gain_second,
):
    core = lax.axis_index("c")
    half = lax.axis_index("xl")
    x = lax.axis_index("xh") * 2 + half
    y = lax.axis_index("y")
    z = lax.axis_index("z")
    grads = (key_grads[0, 0], router_grads[0, 0], gain_grads[0, 0])
    first_place = jnp.where(core == 0, x, y)
    second_place = jnp.where(core == 0, y, x)
    got = send(pack(1 - core, second_place, grads), SIBLING)
    kept = pack(core, first_place, grads)
    parts = in_vmem(add_pair, [kept, got], [((4, 8, 8, ROW), jnp.bfloat16)] * 4)
    states = [key_master, key_first, key_second, router_master, router_first, router_second]
    parts = [parts[0]] + [send(parts[k], along(k)) for k in (1, 2, 3)]
    [code] = in_vmem(sum_encoded, parts, [((32, 8, ROW), jnp.float32)], [z])
    code = lax.all_to_all(
        code.astype(jnp.float16), ALL, 0, 0, axis_index_groups=SECOND_GROUPS, tiled=True
    )
    [code] = in_vmem(encode, [code.astype(jnp.float32)], [((8, ROW), jnp.float32)], [z & 1])
    parts = lax.all_to_all(
        jnp.broadcast_to(code.astype(jnp.float16)[None], (64, 8, ROW)),
        ("xh", "y", "z"),
        0,
        0,
        tiled=True,
    )
    wide_parts = parts.astype(jnp.float32)
    [squares] = in_vmem(add_squares, [wide_parts], [((8, LANES), jnp.float32)])
    squares = [squares] + [send(squares, to) for to in (SIBLING, PARTNER, PARTNER_SIBLING)]
    parts, *squares = lax.optimization_barrier((parts, *squares))
    other = send(parts, SIBLING).astype(jnp.float32)
    states, gains, key_weight, router_weight, gain_weight = updated(
        core,
        half,
        squares,
        wide_parts,
        other,
        states,
        [gain.reshape(8, LANES) for gain in (gain_master, gain_first, gain_second)],
    )
    gains = [gain.reshape(1024) for gain in gains]
    return (*states, *gains, key_weight, router_weight, gain_weight.reshape(D))


def solution(mesh):
    fine = Mesh(np.asarray(mesh.devices).reshape(8, 4, 2, 2, 2), ("z", "y", "xh", "c", "xl"))
    in_specs = (
        P(WIDE, "xl", None, None, None),
        P(WIDE, "xl", None, None, None),
        P(WIDE, "xl", None, None),
        P("xl", None),
        P("xl", None),
        P("xl", None),
        P(None, "xl"),
        P(None, "xl"),
        P(None, "xl"),
        P("xl"),
        P("xl"),
        P("xl"),
    )
    out_specs = (
        P("xl", None),
        P("xl", None),
        P("xl", None),
        P(None, "xl"),
        P(None, "xl"),
        P(None, "xl"),
        P("xl"),
        P("xl"),
        P("xl"),
        P(),
        P(),
        P(),
    )
    return jax.shard_map(
        on_device, mesh=fine, in_specs=in_specs, out_specs=out_specs, check_vma=False
    )
```

```python
import math

import jax
import jax.numpy as jnp
import numpy as np
from jax import lax
from jax.experimental import pallas as pl
from jax.experimental.pallas import tpu as pltpu
from jax.sharding import Mesh
from jax.sharding import PartitionSpec as P

D = 2048
KEY_WIDTH = 512
EXPERTS = 64
LANES = 128
ROW = KEY_WIDTH + LANES

beta_one = 0.9
beta_two = 0.95
step_rate = 0.01
epsilon = 1e-08
bias_one = 1.0 - 0.9**10
bias_two = 1.0 - 0.95**10

WIDE = ("z", "y", "xh", "c")
ALL = ("z", "y", "xh", "c", "xl")


def place(z, y, x, c):
    return (((z * 4 + y) * 2 + x // 2) * 2 + c) * 2 + x % 2


def permutation(target):
    return [
        (place(z, y, x, c), place(*target(z, y, x, c)))
        for z in range(8)
        for y in range(4)
        for x in range(4)
        for c in range(2)
    ]


def along(shift):
    def target(z, y, x, c):
        if c == 0:
            return z, y, x ^ shift, c
        return z, y ^ shift, x, c

    return permutation(target)


SECOND_GROUPS = [
    [place(z, q, p, c) if c == 0 else place(z, p, q, c) for q in range(4) for z in range(8)]
    for c in range(2)
    for p in range(4)
]
SIBLING = permutation(lambda z, y, x, c: (z, y, x, 1 - c))
PARTNER = permutation(lambda z, y, x, c: (z, y, x ^ 1, c))
OTHER_PARTNER = permutation(lambda z, y, x, c: (z, y, x ^ 3, c))
PARTNER_SIBLING = permutation(lambda z, y, x, c: (z, y, x ^ 1, 1 - c))


def send(x, pairs):
    return lax.ppermute(x, ALL, pairs)


def adamw(master, first_moment, second, scaled, decay_rate):
    first_new = beta_one * first_moment + (1.0 - beta_one) * scaled
    second_new = beta_two * second + (1.0 - beta_two) * scaled * scaled
    root = jnp.sqrt(second_new * (1.0 / bias_two)) + epsilon
    kept = master if decay_rate == 0.0 else master * (1.0 - step_rate * decay_rate)
    master_new = kept - first_new * (step_rate / bias_one) / root
    return (master_new, first_new, second_new)


def group_of(t, p, q):
    x = jnp.where(t == 0, p, q)
    y = jnp.where(t == 0, q, p)
    return x % 2, t * 8 + (x // 2) * 4 + y


def micro_total(stack):
    return (stack[0].astype(jnp.float32) + stack[1].astype(jnp.float32)).astype(jnp.bfloat16)


def pack_local(where_ref, key_ref, router_ref, gain_ref, out_ref, keys, routers, gains, tiles, sems):
    t, p = where_ref[0], where_ref[1]
    copies = []
    for i in range(16):
        half, group = group_of(t, p ^ (i // 4), i % 4)
        rows = pl.ds(pl.multiple_of((half * 16 + group) * 64, 64), 64)
        copies.append(pltpu.make_async_copy(key_ref.at[:, rows], keys.at[i], sems.at[i]))
        rows = pl.ds(pl.multiple_of(group // 2 * 8, 8), 8)
        columns = pl.ds(pl.multiple_of((half * 2 + group % 2) * 512, 512), 512)
        copies.append(
            pltpu.make_async_copy(
                router_ref.at[:, rows, columns], routers.at[i], sems.at[16 + i]
            )
        )
    gain_copy = pltpu.make_async_copy(gain_ref, gains, sems.at[32])
    gain_copy.start()
    for copy in copies:
        copy.start()
    lane = lax.broadcasted_iota(jnp.int32, (8, LANES), 1)
    row = lax.broadcasted_iota(jnp.int32, (8, LANES), 0)
    low = lane < 64
    gain_copy.wait()
    gain = gains[...].astype(jnp.float32)
    gain = (gain[0:1] + gain[1:2]).astype(jnp.bfloat16).astype(jnp.float32)
    for half in range(2):
        for z in range(8):
            at = half * 1024 + z * LANES
            line = gain[:, at : at + LANES]
            turned = jnp.concatenate([line[:, 64:], line[:, :64]], axis=1)
            tiles[half, z] = jnp.where(row == 0, line, jnp.where(row == 1, turned, 0.0))
    for i in range(16):
        half, group = group_of(t, p ^ (i // 4), i % 4)
        copies[2 * i].wait()
        copies[2 * i + 1].wait()
        key = keys[i, 0].astype(jnp.float32) + keys[i, 1].astype(jnp.float32)
        out_ref[i // 4, i % 4, :, :, :KEY_WIDTH] = key.astype(jnp.bfloat16).reshape(
            8, 8, KEY_WIDTH
        )
        router = routers[i, 0].astype(jnp.float32) + routers[i, 1].astype(jnp.float32)
        for z in range(8):
            tile = router[:, (z // 2) * LANES : (z // 2 + 1) * LANES]
            mine = low if z % 2 == 0 else jnp.logical_not(low)
            kept = jnp.where(group == 0, tiles[half, z], 0.0)
            out_ref[i // 4, i % 4, z, :, KEY_WIDTH:] = jnp.where(mine, tile, kept).astype(
                jnp.bfloat16
            )


def pack(t, p, grads):
    return pl.pallas_call(
        pack_local,
        in_specs=[pl.BlockSpec(memory_space=pltpu.SMEM)]
        + [pl.BlockSpec(memory_space=pltpu.HBM)] * 3,
        out_specs=pl.BlockSpec(memory_space=pltpu.VMEM),
        out_shape=jax.ShapeDtypeStruct((4, 4, 8, 8, ROW), jnp.bfloat16),
        scratch_shapes=[
            pltpu.VMEM((16, 2, 64, KEY_WIDTH), jnp.bfloat16),
            pltpu.VMEM((16, 2, 8, 512), jnp.bfloat16),
            pltpu.VMEM((2, D), jnp.bfloat16),
            pltpu.VMEM((2, 8, 8, LANES), jnp.float32),
            pltpu.SemaphoreType.DMA((33,)),
        ],
        compiler_params=pltpu.CompilerParams(vmem_limit_bytes=4 * 1024 * 1024),
    )(jnp.stack([t, p]), *[pltpu.with_memory_space_constraint(g, pltpu.HBM) for g in grads])


def in_vmem(body, operands, shapes, scalars=()):
    scalars = [jnp.stack(scalars)] if scalars else []
    return pl.pallas_call(
        body,
        in_specs=[pl.BlockSpec(memory_space=pltpu.SMEM)] * len(scalars)
        + [pl.BlockSpec(memory_space=pltpu.VMEM)] * len(operands),
        out_specs=[pl.BlockSpec(memory_space=pltpu.VMEM)] * len(shapes),
        out_shape=[jax.ShapeDtypeStruct(*shape) for shape in shapes],
        compiler_params=pltpu.CompilerParams(vmem_limit_bytes=2 * 1024 * 1024),
    )(*scalars, *operands)


def add_pair(kept_ref, got_ref, *outs):
    for k in range(4):
        for q in range(4):
            total = kept_ref[k, q].astype(jnp.float32) + got_ref[k, q].astype(jnp.float32)
            outs[k][q] = total.astype(jnp.bfloat16)


def spare_lanes(parity):
    lane = lax.broadcasted_iota(jnp.int32, (8, LANES), 1)
    return lane // 64 + parity == 1


def exponent_of(largest):
    largest = jnp.maximum(jnp.broadcast_to(largest, (8, LANES)), 1e-30)
    return jnp.floor(jnp.log(largest) * (1.0 / math.log(2.0))) - 13.0


def largest_of(x):
    return jnp.max(jnp.max(jnp.abs(x), axis=1, keepdims=True), axis=0, keepdims=True)


def sum_encoded(where_ref, *refs):
    terms, out_ref = refs[:4], refs[4]
    largest = jnp.zeros((8, ROW), jnp.float32)
    for q in range(4):
        for z in range(8):
            total = terms[0][q, z].astype(jnp.float32)
            for term in terms[1:]:
                total = total + term[q, z].astype(jnp.float32)
            out_ref[q * 8 + z] = total
            largest = jnp.maximum(largest, jnp.abs(total))
    exponent = exponent_of(largest_of(largest))
    scale = jnp.concatenate([jnp.exp2(-exponent)] * 5, axis=1)
    row = lax.broadcasted_iota(jnp.int32, (8, LANES), 0)
    for b in range(32):
        own = out_ref[b] * scale
        spare = spare_lanes(b % 2) & (row == 7)
        out_ref[b, :, :KEY_WIDTH] = own[:, :KEY_WIDTH]
        out_ref[b, :, KEY_WIDTH:] = jnp.where(spare, exponent, own[:, KEY_WIDTH:])


def encode(where_ref, blocks_ref, out_ref):
    parity = where_ref[0]
    row = lax.broadcasted_iota(jnp.int32, (8, LANES), 0)
    own = jnp.zeros((8, ROW), jnp.float32)
    for b in range(32):
        block = blocks_ref[b]
        scale = scale_of(block[:, KEY_WIDTH:], parity)
        own = own + block * jnp.concatenate([scale] * 5, axis=1)
    spare = spare_lanes(parity) & (row >= 5)
    key, tile = own[:, :KEY_WIDTH], jnp.where(spare, 0.0, own[:, KEY_WIDTH:])
    own = jnp.concatenate([key, tile], axis=1)
    exponent = exponent_of(largest_of(own))
    own = own * jnp.concatenate([jnp.exp2(-exponent)] * 5, axis=1)
    squares = jnp.sum(jnp.sum(own * own, axis=1, keepdims=True), axis=0, keepdims=True)
    squares = jnp.broadcast_to(squares, (8, LANES)) * 2.0**-30
    digit = squares.astype(jnp.bfloat16).astype(jnp.float32)
    notes = jnp.where(row == 7, exponent, jnp.where(row == 6, digit, (squares - digit) * 256.0))
    out_ref[:, :KEY_WIDTH] = own[:, :KEY_WIDTH]
    out_ref[:, KEY_WIDTH:] = jnp.where(spare, notes, own[:, KEY_WIDTH:])


def add_squares(blocks_ref, out_ref):
    totals = [jnp.zeros((1, LANES), jnp.float32)] * 2
    for b in range(64):
        tile = blocks_ref[b, :, KEY_WIDTH:]
        digits = tile[6:7] + tile[5:6] * (1.0 / 256.0)
        totals[b // 8 % 2] = totals[b // 8 % 2] + digits * jnp.exp2(2.0 * tile[7:8] + 30.0)
    lane = lax.broadcasted_iota(jnp.int32, (1, LANES), 1)
    total = jnp.where(lane == 64, totals[0], 0.0) + jnp.where(lane == 0, totals[1], 0.0)
    out_ref[...] = jnp.broadcast_to(jnp.sum(total, axis=1, keepdims=True), (8, LANES))


def scale_of(tile, parity):
    line = tile[7:8]
    turned = jnp.concatenate([line[:, 64:], line[:, :64]], axis=1)
    lane = lax.broadcasted_iota(jnp.int32, (1, LANES), 1)
    line = jnp.where(lane // 64 + parity == 1, line, turned)
    return jnp.exp2(jnp.broadcast_to(line, (8, LANES)))


def gain_line(tile, z):
    first, second = tile[0:1], tile[1:2]
    turned = jnp.concatenate([second[:, 64:], second[:, :64]], axis=1)
    lane = lax.broadcasted_iota(jnp.int32, (1, LANES), 1)
    if z % 2 == 0:
        return jnp.where(lane < 64, turned, first)
    return jnp.where(lane < 64, first, turned)


def clip_factor(squares):
    total = (squares[0][...] + squares[1][...]) + (squares[2][...] + squares[3][...])
    clip_limit = 0.5 * math.sqrt(D * KEY_WIDTH + EXPERTS * D + D)
    return clip_limit / jnp.maximum(jnp.sqrt(total), clip_limit)


def update_rows(where_ref, squares, blocks_ref, ins, outs, after_group=None):
    t = where_ref[0]
    factor = clip_factor(squares)
    key_ins, router_ins, gain_ins = ins[:3], ins[3:6], ins[6:]
    keys, routers, gain_outs, messages = outs[0], outs[1], outs[2:5], outs[5:]
    low = lax.broadcasted_iota(jnp.int32, (8, LANES), 1) < 64
    row = lax.broadcasted_iota(jnp.int32, (8, LANES), 0)
    scaled = jnp.zeros((8, LANES), jnp.float32)
    for z in range(8):
        tile = blocks_ref[z * 8, :, KEY_WIDTH:]
        scaled = jnp.where(row == z, gain_line(tile * (scale_of(tile, z % 2) * factor), z), scaled)
    new = adamw(*[gain[...] for gain in gain_ins], scaled, 0.0)
    for a in range(3):
        gain_outs[a][...] = new[a]
    messages[0][pl.ds(288, 8), :LANES] = new[0].astype(jnp.bfloat16)
    for g in range(8):
        message, at = messages[g // 4], g % 4
        tiles = []
        for z in range(8):
            b = z * 8 + g % 4 * 2 + g // 4
            tile = blocks_ref[b, :, KEY_WIDTH:]
            scale = scale_of(tile, z % 2) * factor
            tiles.append(tile * scale)
            scaled = blocks_ref[b, :, :KEY_WIDTH] * jnp.concatenate([scale] * 4, axis=1)
            rows = pl.ds(g * 64 + z * 8, 8)
            old = pl.ds(pl.multiple_of(t * 512 + g * 64 + z * 8, 8), 8)
            new = adamw(*[key[old] for key in key_ins], scaled, 0.1)
            for a in range(3):
                keys[a, rows] = new[a]
            message[pl.ds(at * 64 + z * 8, 8)] = new[0].astype(jnp.bfloat16)
        scaled = jnp.concatenate(
            [jnp.where(low, tiles[2 * i], tiles[2 * i + 1]) for i in range(4)], axis=1
        )
        rows, columns = pl.ds(g // 2 * 8, 8), pl.ds(g % 2 * 512, 512)
        old = pl.ds(pl.multiple_of(t * 32 + g // 2 * 8, 8), 8)
        new = adamw(*[router[old, columns] for router in router_ins], scaled, 0.1)
        for a in range(3):
            routers[a, rows, columns] = new[a]
        message[pl.ds(256 + at * 8, 8)] = new[0].astype(jnp.bfloat16)
        if after_group is not None:
            after_group(g)


class Stores:
    def __init__(self, sems):
        self.sems, self.copies = sems, []

    def __call__(self, source, target):
        copy = pltpu.make_async_copy(source, target, self.sems.at[len(self.copies)])
        copy.start()
        self.copies.append(copy)

    def wait(self):
        for copy in self.copies:
            copy.wait()


def store_weights(store, t, half, g, message, key_weight, router_weight):
    rows = pl.ds(pl.multiple_of(half * 1024 + t * 512 + g * 64, 64), 64)
    store(message.at[pl.ds(g % 4 * 64, 64)], key_weight.at[rows])
    rows = pl.ds(pl.multiple_of(t * 32 + g // 2 * 8, 8), 8)
    columns = pl.ds(pl.multiple_of(half * 1024 + g % 2 * 512, 512), 512)
    store(message.at[pl.ds(256 + g % 4 * 8, 8)], router_weight.at[rows, columns])


def store_group(store, t, half, g, keys, message, outs):
    rows = pl.ds(pl.multiple_of(t * 512 + g * 64, 64), 64)
    for a in range(3):
        store(keys.at[a, pl.ds(g * 64, 64)], outs[a].at[rows])
    store_weights(store, t, half, g, message, outs[6], outs[7])


def store_routers(store, t, routers, outs):
    rows = pl.ds(pl.multiple_of(t * 32, 32), 32)
    for a in range(3):
        store(routers.at[a], outs[3 + a].at[rows])


def update_first(where_ref, *refs):
    update_rows(where_ref, refs[:4], refs[4], refs[5:14], refs[14:])


def update_second(where_ref, *refs):
    squares, blocks_ref, ins, first = refs[:4], refs[4], refs[5:14], refs[14:18]
    outs, gains, scratch = refs[18:26], refs[26:29], refs[29:]
    keys, routers, messages, sems = scratch[0], scratch[1], scratch[2:4], scratch[4]
    t, half = where_ref[0], where_ref[1]
    store = Stores(sems)
    for g in range(8):
        store_group(store, 1 - t, half, g, first[0], first[2 + g // 4], outs)
    store_routers(store, 1 - t, first[1], outs)
    update_rows(
        where_ref,
        squares,
        blocks_ref,
        ins,
        (keys, routers, *gains, *messages),
        lambda g: store_group(store, t, half, g, keys, messages[g // 4], outs),
    )
    store_routers(store, t, routers, outs)
    store.wait()


def write_received(where_ref, far0, far1, near0, near1, *refs):
    first_gains, second_gains = refs[:3], refs[3:6]
    key_weight, router_weight, gain_outs, gain_weight, sems = *refs[8:10], refs[10:13], *refs[13:]
    t, half = where_ref[0], where_ref[1]
    store = Stores(sems)
    for g in range(8):
        store_weights(store, t, 1 - half, g, (far0, far1)[g // 4], key_weight, router_weight)
        store_weights(store, 1 - t, 1 - half, g, (near0, near1)[g // 4], key_weight, router_weight)
    for a in range(3):
        gain_outs[a][...] = jnp.where(t == 0, first_gains[a][...], second_gains[a][...])
    rows = pl.ds(288, 8)
    far, near = far0[rows, :LANES].astype(jnp.float32), near0[rows, :LANES].astype(jnp.float32)
    far = jnp.where(t == 0, far, near)
    mine = jnp.where(t == 0, first_gains[0][...], second_gains[0][...])
    gain_weight[:8] = jnp.where(half == 0, mine, far).astype(jnp.bfloat16)
    gain_weight[8:] = jnp.where(half == 0, far, mine).astype(jnp.bfloat16)
    store.wait()


IN_VMEM = pl.BlockSpec(memory_space=pltpu.VMEM)
IN_HBM = pl.BlockSpec(memory_space=pltpu.HBM)
IN_SMEM = pl.BlockSpec(memory_space=pltpu.SMEM)
MESSAGES = [((296, KEY_WIDTH), jnp.bfloat16), ((288, KEY_WIDTH), jnp.bfloat16)]


def in_hbm(arrays):
    return [pltpu.with_memory_space_constraint(a, pltpu.HBM) for a in arrays]


def updated(core, half, squares, parts, other, states, gains):
    shapes = [jax.ShapeDtypeStruct(a.shape, jnp.float32) for a in states]
    shapes += [
        jax.ShapeDtypeStruct((D, KEY_WIDTH), jnp.bfloat16),
        jax.ShapeDtypeStruct((EXPERTS, D), jnp.bfloat16),
    ]
    gain_shapes = [jax.ShapeDtypeStruct((8, LANES), jnp.float32)] * 3
    rows = [((3, 512, KEY_WIDTH), jnp.float32), ((3, 32, 1024), jnp.float32)]
    cost = pl.CostEstimate(flops=7_000_000, bytes_accessed=8_000_000, transcendentals=600_000)
    keys, routers, *outs = pl.pallas_call(
        update_first,
        in_specs=[IN_SMEM] + [IN_VMEM] * 14,
        out_specs=[IN_VMEM] * 7,
        out_shape=[jax.ShapeDtypeStruct(*r) for r in rows]
        + gain_shapes
        + [jax.ShapeDtypeStruct(*m) for m in MESSAGES],
        compiler_params=pltpu.CompilerParams(vmem_limit_bytes=2 * 1024 * 1024),
        cost_estimate=cost,
    )(jnp.stack([core, half]), *squares, parts, *states, *gains)
    first_gains, sent = outs[:3], outs[3:]
    far = [send(sent[0], PARTNER), send(sent[1], OTHER_PARTNER)]
    outs = pl.pallas_call(
        update_second,
        in_specs=[IN_SMEM] + [IN_VMEM] * 18,
        out_specs=[IN_HBM] * 8 + [IN_VMEM] * 3,
        out_shape=shapes + gain_shapes,
        scratch_shapes=[pltpu.VMEM(*r) for r in rows + MESSAGES]
        + [pltpu.SemaphoreType.DMA((86,))],
        compiler_params=pltpu.CompilerParams(vmem_limit_bytes=8 * 1024 * 1024),
        cost_estimate=cost,
    )(jnp.stack([1 - core, half]), *squares, other, *states, *gains, keys, routers, *sent)
    outs, second_gains = outs[:8], outs[8:]
    far0, far1, gain_new = lax.optimization_barrier((*far, second_gains[0]))
    far, second_gains = [far0, far1], [gain_new, *second_gains[1:]]
    near = [send(a, SIBLING) for a in far]
    key_weight, router_weight, *gains, gain_weight = pl.pallas_call(
        write_received,
        in_specs=[IN_SMEM] + [IN_VMEM] * 10 + [IN_HBM] * 2,
        out_specs=[IN_HBM] * 2 + [IN_VMEM] * 4,
        out_shape=shapes[6:] + gain_shapes + [jax.ShapeDtypeStruct((16, LANES), jnp.bfloat16)],
        input_output_aliases={11: 0, 12: 1},
        scratch_shapes=[pltpu.SemaphoreType.DMA((32,))],
        compiler_params=pltpu.CompilerParams(vmem_limit_bytes=2 * 1024 * 1024),
    )(jnp.stack([core, half]), *far, *near, *first_gains, *second_gains, *outs[6:])
    return outs[:6], gains, key_weight, router_weight, gain_weight


def on_device(
    key_grads,
    router_grads,
    gain_grads,
    key_master,
    key_first,
    key_second,
    router_master,
    router_first,
    router_second,
    gain_master,
    gain_first,
    gain_second,
):
    core = lax.axis_index("c")
    half = lax.axis_index("xl")
    x = lax.axis_index("xh") * 2 + half
    y = lax.axis_index("y")
    z = lax.axis_index("z")
    grads = (key_grads[0, 0], router_grads[0, 0], gain_grads[0, 0])
    first_place = jnp.where(core == 0, x, y)
    second_place = jnp.where(core == 0, y, x)
    got = send(pack(1 - core, second_place, grads), SIBLING)
    kept = pack(core, first_place, grads)
    parts = in_vmem(add_pair, [kept, got], [((4, 8, 8, ROW), jnp.bfloat16)] * 4)
    states = [key_master, key_first, key_second, router_master, router_first, router_second]
    parts = [parts[0]] + [send(parts[k], along(k)) for k in (2, 1, 3)]
    [code] = in_vmem(sum_encoded, parts, [((32, 8, ROW), jnp.float32)], [z])
    code = lax.all_to_all(
        code.astype(jnp.float16), ALL, 0, 0, axis_index_groups=SECOND_GROUPS, tiled=True
    )
    [code] = in_vmem(encode, [code.astype(jnp.float32)], [((8, ROW), jnp.float32)], [z & 1])
    parts = lax.all_to_all(
        jnp.broadcast_to(code.astype(jnp.float16)[None], (64, 8, ROW)),
        ("z", "y", "xh"),
        0,
        0,
        tiled=True,
    )
    wide_parts = parts.astype(jnp.float32)
    [squares] = in_vmem(add_squares, [wide_parts], [((8, LANES), jnp.float32)])
    squares = [squares] + [send(squares, to) for to in (SIBLING, PARTNER, PARTNER_SIBLING)]
    parts, *squares = lax.optimization_barrier((parts, *squares))
    other = send(parts, SIBLING).astype(jnp.float32)
    states, gains, key_weight, router_weight, gain_weight = updated(
        core,
        half,
        squares,
        wide_parts,
        other,
        states,
        [gain.reshape(8, LANES) for gain in (gain_master, gain_first, gain_second)],
    )
    gains = [gain.reshape(1024) for gain in gains]
    return (*states, *gains, key_weight, router_weight, gain_weight.reshape(D))


def solution(mesh):
    fine = Mesh(np.asarray(mesh.devices).reshape(8, 4, 2, 2, 2), ("z", "y", "xh", "c", "xl"))
    in_specs = (
        P(WIDE, "xl", None, None, None),
        P(WIDE, "xl", None, None, None),
        P(WIDE, "xl", None, None),
        P("xl", None),
        P("xl", None),
        P("xl", None),
        P(None, "xl"),
        P(None, "xl"),
        P(None, "xl"),
        P("xl"),
        P("xl"),
        P("xl"),
    )
    out_specs = (
        P("xl", None),
        P("xl", None),
        P("xl", None),
        P(None, "xl"),
        P(None, "xl"),
        P(None, "xl"),
        P("xl"),
        P("xl"),
        P("xl"),
        P(),
        P(),
        P(),
    )
    return jax.shard_map(
        on_device, mesh=fine, in_specs=in_specs, out_specs=out_specs, check_vma=False
    )
```

```python
import math

import jax
import jax.numpy as jnp
import numpy as np
from jax import lax
from jax.experimental import pallas as pl
from jax.experimental.pallas import tpu as pltpu
from jax.sharding import Mesh
from jax.sharding import PartitionSpec as P

D = 2048
KEY_WIDTH = 512
EXPERTS = 64
LANES = 128
ROW = KEY_WIDTH + LANES

beta_one = 0.9
beta_two = 0.95
step_rate = 0.01
epsilon = 1e-08
bias_one = 1.0 - 0.9**10
bias_two = 1.0 - 0.95**10

WIDE = ("z", "y", "xh", "c")
ALL = ("z", "y", "xh", "c", "xl")


def place(z, y, x, c):
    return (((z * 4 + y) * 2 + x // 2) * 2 + c) * 2 + x % 2


def permutation(target):
    return [
        (place(z, y, x, c), place(*target(z, y, x, c)))
        for z in range(8)
        for y in range(4)
        for x in range(4)
        for c in range(2)
    ]


def along(shift):
    def target(z, y, x, c):
        if c == 0:
            return z, y, x ^ shift, c
        return z, y ^ shift, x, c

    return permutation(target)


SECOND_GROUPS = [
    [place(z, q, p, c) if c == 0 else place(z, p, q, c) for q in range(4) for z in range(8)]
    for c in range(2)
    for p in range(4)
]
SIBLING = permutation(lambda z, y, x, c: (z, y, x, 1 - c))
PARTNER = permutation(lambda z, y, x, c: (z, y, x ^ 1, c))
OTHER_PARTNER = permutation(lambda z, y, x, c: (z, y, x ^ 3, c))
PARTNER_SIBLING = permutation(lambda z, y, x, c: (z, y, x ^ 1, 1 - c))


def send(x, pairs):
    return lax.ppermute(x, ALL, pairs)


def adamw(master, first_moment, second, scaled, decay_rate):
    first_new = beta_one * first_moment + (1.0 - beta_one) * scaled
    second_new = beta_two * second + (1.0 - beta_two) * scaled * scaled
    root = jnp.sqrt(second_new * (1.0 / bias_two)) + epsilon
    kept = master if decay_rate == 0.0 else master * (1.0 - step_rate * decay_rate)
    master_new = kept - first_new * (step_rate / bias_one) / root
    return (master_new, first_new, second_new)


def group_of(t, p, q):
    x = jnp.where(t == 0, p, q)
    y = jnp.where(t == 0, q, p)
    return x % 2, t * 8 + (x // 2) * 4 + y


def micro_total(stack):
    return (stack[0].astype(jnp.float32) + stack[1].astype(jnp.float32)).astype(jnp.bfloat16)


def pack_local(where_ref, key_ref, router_ref, gain_ref, out_ref, keys, routers, gains, tiles, sems):
    t, p = where_ref[0], where_ref[1]
    copies = []
    for i in range(16):
        half, group = group_of(t, p ^ (i // 4), i % 4)
        rows = pl.ds(pl.multiple_of((half * 16 + group) * 64, 64), 64)
        copies.append(pltpu.make_async_copy(key_ref.at[:, rows], keys.at[i], sems.at[i]))
        rows = pl.ds(pl.multiple_of(group // 2 * 8, 8), 8)
        columns = pl.ds(pl.multiple_of((half * 2 + group % 2) * 512, 512), 512)
        copies.append(
            pltpu.make_async_copy(
                router_ref.at[:, rows, columns], routers.at[i], sems.at[16 + i]
            )
        )
    gain_copy = pltpu.make_async_copy(gain_ref, gains, sems.at[32])
    gain_copy.start()
    for copy in copies:
        copy.start()
    lane = lax.broadcasted_iota(jnp.int32, (8, LANES), 1)
    row = lax.broadcasted_iota(jnp.int32, (8, LANES), 0)
    low = lane < 64
    gain_copy.wait()
    gain = gains[...].astype(jnp.float32)
    gain = (gain[0:1] + gain[1:2]).astype(jnp.bfloat16).astype(jnp.float32)
    for half in range(2):
        for z in range(8):
            at = half * 1024 + z * LANES
            line = gain[:, at : at + LANES]
            turned = jnp.concatenate([line[:, 64:], line[:, :64]], axis=1)
            tiles[half, z] = jnp.where(row == 0, line, jnp.where(row == 1, turned, 0.0))
    for i in range(16):
        half, group = group_of(t, p ^ (i // 4), i % 4)
        copies[2 * i].wait()
        copies[2 * i + 1].wait()
        key = keys[i, 0].astype(jnp.float32) + keys[i, 1].astype(jnp.float32)
        out_ref[i // 4, i % 4, :, :, :KEY_WIDTH] = key.astype(jnp.bfloat16).reshape(
            8, 8, KEY_WIDTH
        )
        router = routers[i, 0].astype(jnp.float32) + routers[i, 1].astype(jnp.float32)
        for z in range(8):
            tile = router[:, (z // 2) * LANES : (z // 2 + 1) * LANES]
            mine = low if z % 2 == 0 else jnp.logical_not(low)
            kept = jnp.where(group == 0, tiles[half, z], 0.0)
            out_ref[i // 4, i % 4, z, :, KEY_WIDTH:] = jnp.where(mine, tile, kept).astype(
                jnp.bfloat16
            )


def pack(t, p, grads):
    return pl.pallas_call(
        pack_local,
        in_specs=[pl.BlockSpec(memory_space=pltpu.SMEM)]
        + [pl.BlockSpec(memory_space=pltpu.HBM)] * 3,
        out_specs=pl.BlockSpec(memory_space=pltpu.VMEM),
        out_shape=jax.ShapeDtypeStruct((4, 4, 8, 8, ROW), jnp.bfloat16),
        scratch_shapes=[
            pltpu.VMEM((16, 2, 64, KEY_WIDTH), jnp.bfloat16),
            pltpu.VMEM((16, 2, 8, 512), jnp.bfloat16),
            pltpu.VMEM((2, D), jnp.bfloat16),
            pltpu.VMEM((2, 8, 8, LANES), jnp.float32),
            pltpu.SemaphoreType.DMA((33,)),
        ],
        compiler_params=pltpu.CompilerParams(vmem_limit_bytes=4 * 1024 * 1024),
    )(jnp.stack([t, p]), *[pltpu.with_memory_space_constraint(g, pltpu.HBM) for g in grads])


def in_vmem(body, operands, shapes, scalars=()):
    scalars = [jnp.stack(scalars)] if scalars else []
    return pl.pallas_call(
        body,
        in_specs=[pl.BlockSpec(memory_space=pltpu.SMEM)] * len(scalars)
        + [pl.BlockSpec(memory_space=pltpu.VMEM)] * len(operands),
        out_specs=[pl.BlockSpec(memory_space=pltpu.VMEM)] * len(shapes),
        out_shape=[jax.ShapeDtypeStruct(*shape) for shape in shapes],
        compiler_params=pltpu.CompilerParams(vmem_limit_bytes=2 * 1024 * 1024),
    )(*scalars, *operands)


def add_pair(kept_ref, got_ref, *outs):
    for k in range(4):
        for q in range(4):
            total = kept_ref[k, q].astype(jnp.float32) + got_ref[k, q].astype(jnp.float32)
            outs[k][q] = total.astype(jnp.bfloat16)


def spare_lanes(parity):
    lane = lax.broadcasted_iota(jnp.int32, (8, LANES), 1)
    return lane // 64 + parity == 1


def exponent_of(largest):
    largest = jnp.maximum(jnp.broadcast_to(largest, (8, LANES)), 1e-30)
    return jnp.floor(jnp.log(largest) * (1.0 / math.log(2.0))) - 13.0


def largest_of(x):
    return jnp.max(jnp.max(jnp.abs(x), axis=1, keepdims=True), axis=0, keepdims=True)


def sum_encoded(where_ref, *refs):
    terms, out_ref = refs[:4], refs[4]
    largest = jnp.zeros((8, ROW), jnp.float32)
    for q in range(4):
        for z in range(8):
            total = terms[0][q, z].astype(jnp.float32)
            for term in terms[1:]:
                total = total + term[q, z].astype(jnp.float32)
            out_ref[q * 8 + z] = total
            largest = jnp.maximum(largest, jnp.abs(total))
    exponent = exponent_of(largest_of(largest))
    scale = jnp.concatenate([jnp.exp2(-exponent)] * 5, axis=1)
    row = lax.broadcasted_iota(jnp.int32, (8, LANES), 0)
    for b in range(32):
        own = out_ref[b] * scale
        spare = spare_lanes(b % 2) & (row == 7)
        out_ref[b, :, :KEY_WIDTH] = own[:, :KEY_WIDTH]
        out_ref[b, :, KEY_WIDTH:] = jnp.where(spare, exponent, own[:, KEY_WIDTH:])


def encode(where_ref, blocks_ref, out_ref):
    parity = where_ref[0]
    row = lax.broadcasted_iota(jnp.int32, (8, LANES), 0)
    own = jnp.zeros((8, ROW), jnp.float32)
    for b in range(32):
        block = blocks_ref[b]
        scale = scale_of(block[:, KEY_WIDTH:], parity)
        own = own + block * jnp.concatenate([scale] * 5, axis=1)
    spare = spare_lanes(parity) & (row >= 5)
    key, tile = own[:, :KEY_WIDTH], jnp.where(spare, 0.0, own[:, KEY_WIDTH:])
    own = jnp.concatenate([key, tile], axis=1)
    exponent = exponent_of(largest_of(own))
    own = own * jnp.concatenate([jnp.exp2(-exponent)] * 5, axis=1)
    squares = jnp.sum(jnp.sum(own * own, axis=1, keepdims=True), axis=0, keepdims=True)
    squares = jnp.broadcast_to(squares, (8, LANES)) * 2.0**-30
    digit = squares.astype(jnp.bfloat16).astype(jnp.float32)
    notes = jnp.where(row == 7, exponent, jnp.where(row == 6, digit, (squares - digit) * 256.0))
    out_ref[:, :KEY_WIDTH] = own[:, :KEY_WIDTH]
    out_ref[:, KEY_WIDTH:] = jnp.where(spare, notes, own[:, KEY_WIDTH:])


def add_squares(blocks_ref, out_ref):
    totals = [jnp.zeros((1, LANES), jnp.float32)] * 2
    for b in range(64):
        tile = blocks_ref[b, :, KEY_WIDTH:]
        digits = tile[6:7] + tile[5:6] * (1.0 / 256.0)
        totals[b % 2] = totals[b % 2] + digits * jnp.exp2(2.0 * tile[7:8] + 30.0)
    lane = lax.broadcasted_iota(jnp.int32, (1, LANES), 1)
    total = jnp.where(lane == 64, totals[0], 0.0) + jnp.where(lane == 0, totals[1], 0.0)
    out_ref[...] = jnp.broadcast_to(jnp.sum(total, axis=1, keepdims=True), (8, LANES))


def scale_of(tile, parity):
    line = tile[7:8]
    turned = jnp.concatenate([line[:, 64:], line[:, :64]], axis=1)
    lane = lax.broadcasted_iota(jnp.int32, (1, LANES), 1)
    line = jnp.where(lane // 64 + parity == 1, line, turned)
    return jnp.exp2(jnp.broadcast_to(line, (8, LANES)))


def gain_line(tile, z):
    first, second = tile[0:1], tile[1:2]
    turned = jnp.concatenate([second[:, 64:], second[:, :64]], axis=1)
    lane = lax.broadcasted_iota(jnp.int32, (1, LANES), 1)
    if z % 2 == 0:
        return jnp.where(lane < 64, turned, first)
    return jnp.where(lane < 64, first, turned)


def clip_factor(squares):
    total = (squares[0][...] + squares[1][...]) + (squares[2][...] + squares[3][...])
    clip_limit = 0.5 * math.sqrt(D * KEY_WIDTH + EXPERTS * D + D)
    return clip_limit / jnp.maximum(jnp.sqrt(total), clip_limit)


def update_rows(where_ref, squares, blocks_ref, ins, outs, after_group=None):
    t = where_ref[0]
    factor = clip_factor(squares)
    key_ins, router_ins, gain_ins = ins[:3], ins[3:6], ins[6:]
    keys, routers, gain_outs, messages = outs[0], outs[1], outs[2:5], outs[5:]
    low = lax.broadcasted_iota(jnp.int32, (8, LANES), 1) < 64
    row = lax.broadcasted_iota(jnp.int32, (8, LANES), 0)
    scaled = jnp.zeros((8, LANES), jnp.float32)
    for z in range(8):
        tile = blocks_ref[z, :, KEY_WIDTH:]
        scaled = jnp.where(row == z, gain_line(tile * (scale_of(tile, z % 2) * factor), z), scaled)
    new = adamw(*[gain[...] for gain in gain_ins], scaled, 0.0)
    for a in range(3):
        gain_outs[a][...] = new[a]
    messages[0][pl.ds(288, 8), :LANES] = new[0].astype(jnp.bfloat16)
    for g in range(8):
        message, at = messages[g // 4], g % 4
        tiles = []
        for z in range(8):
            b = (g % 4 * 2 + g // 4) * 8 + z
            tile = blocks_ref[b, :, KEY_WIDTH:]
            scale = scale_of(tile, z % 2) * factor
            tiles.append(tile * scale)
            scaled = blocks_ref[b, :, :KEY_WIDTH] * jnp.concatenate([scale] * 4, axis=1)
            rows = pl.ds(g * 64 + z * 8, 8)
            old = pl.ds(pl.multiple_of(t * 512 + g * 64 + z * 8, 8), 8)
            new = adamw(*[key[old] for key in key_ins], scaled, 0.1)
            for a in range(3):
                keys[a, rows] = new[a]
            message[pl.ds(at * 64 + z * 8, 8)] = new[0].astype(jnp.bfloat16)
        scaled = jnp.concatenate(
            [jnp.where(low, tiles[2 * i], tiles[2 * i + 1]) for i in range(4)], axis=1
        )
        rows, columns = pl.ds(g // 2 * 8, 8), pl.ds(g % 2 * 512, 512)
        old = pl.ds(pl.multiple_of(t * 32 + g // 2 * 8, 8), 8)
        new = adamw(*[router[old, columns] for router in router_ins], scaled, 0.1)
        for a in range(3):
            routers[a, rows, columns] = new[a]
        message[pl.ds(256 + at * 8, 8)] = new[0].astype(jnp.bfloat16)
        if after_group is not None:
            after_group(g)


class Stores:
    def __init__(self, sems):
        self.sems, self.copies = sems, []

    def __call__(self, source, target):
        copy = pltpu.make_async_copy(source, target, self.sems.at[len(self.copies)])
        copy.start()
        self.copies.append(copy)

    def wait(self):
        for copy in self.copies:
            copy.wait()


def store_weights(store, t, half, g, message, key_weight, router_weight):
    rows = pl.ds(pl.multiple_of(half * 1024 + t * 512 + g * 64, 64), 64)
    store(message.at[pl.ds(g % 4 * 64, 64)], key_weight.at[rows])
    rows = pl.ds(pl.multiple_of(t * 32 + g // 2 * 8, 8), 8)
    columns = pl.ds(pl.multiple_of(half * 1024 + g % 2 * 512, 512), 512)
    store(message.at[pl.ds(256 + g % 4 * 8, 8)], router_weight.at[rows, columns])


def store_group(store, t, half, g, keys, message, outs):
    rows = pl.ds(pl.multiple_of(t * 512 + g * 64, 64), 64)
    for a in range(3):
        store(keys.at[a, pl.ds(g * 64, 64)], outs[a].at[rows])
    store_weights(store, t, half, g, message, outs[6], outs[7])


def store_routers(store, t, routers, outs):
    rows = pl.ds(pl.multiple_of(t * 32, 32), 32)
    for a in range(3):
        store(routers.at[a], outs[3 + a].at[rows])


def update_first(where_ref, *refs):
    update_rows(where_ref, refs[:4], refs[4], refs[5:14], refs[14:])


def update_second(where_ref, *refs):
    squares, blocks_ref, ins, first = refs[:4], refs[4], refs[5:14], refs[14:18]
    outs, gains, scratch = refs[18:26], refs[26:29], refs[29:]
    keys, routers, messages, sems = scratch[0], scratch[1], scratch[2:4], scratch[4]
    t, half = where_ref[0], where_ref[1]
    store = Stores(sems)
    for g in range(8):
        store_group(store, 1 - t, half, g, first[0], first[2 + g // 4], outs)
    store_routers(store, 1 - t, first[1], outs)
    update_rows(
        where_ref,
        squares,
        blocks_ref,
        ins,
        (keys, routers, *gains, *messages),
        lambda g: store_group(store, t, half, g, keys, messages[g // 4], outs),
    )
    store_routers(store, t, routers, outs)
    store.wait()


def write_received(where_ref, far0, far1, near0, near1, *refs):
    first_gains, second_gains = refs[:3], refs[3:6]
    key_weight, router_weight, gain_outs, gain_weight, sems = *refs[8:10], refs[10:13], *refs[13:]
    t, half = where_ref[0], where_ref[1]
    store = Stores(sems)
    for g in range(8):
        store_weights(store, t, 1 - half, g, (far0, far1)[g // 4], key_weight, router_weight)
        store_weights(store, 1 - t, 1 - half, g, (near0, near1)[g // 4], key_weight, router_weight)
    for a in range(3):
        gain_outs[a][...] = jnp.where(t == 0, first_gains[a][...], second_gains[a][...])
    rows = pl.ds(288, 8)
    far, near = far0[rows, :LANES].astype(jnp.float32), near0[rows, :LANES].astype(jnp.float32)
    far = jnp.where(t == 0, far, near)
    mine = jnp.where(t == 0, first_gains[0][...], second_gains[0][...])
    gain_weight[:8] = jnp.where(half == 0, mine, far).astype(jnp.bfloat16)
    gain_weight[8:] = jnp.where(half == 0, far, mine).astype(jnp.bfloat16)
    store.wait()


IN_VMEM = pl.BlockSpec(memory_space=pltpu.VMEM)
IN_HBM = pl.BlockSpec(memory_space=pltpu.HBM)
IN_SMEM = pl.BlockSpec(memory_space=pltpu.SMEM)
MESSAGES = [((296, KEY_WIDTH), jnp.bfloat16), ((288, KEY_WIDTH), jnp.bfloat16)]


def in_hbm(arrays):
    return [pltpu.with_memory_space_constraint(a, pltpu.HBM) for a in arrays]


def updated(core, half, squares, parts, other, states, gains):
    shapes = [jax.ShapeDtypeStruct(a.shape, jnp.float32) for a in states]
    shapes += [
        jax.ShapeDtypeStruct((D, KEY_WIDTH), jnp.bfloat16),
        jax.ShapeDtypeStruct((EXPERTS, D), jnp.bfloat16),
    ]
    gain_shapes = [jax.ShapeDtypeStruct((8, LANES), jnp.float32)] * 3
    rows = [((3, 512, KEY_WIDTH), jnp.float32), ((3, 32, 1024), jnp.float32)]
    cost = pl.CostEstimate(flops=7_000_000, bytes_accessed=8_000_000, transcendentals=600_000)
    keys, routers, *outs = pl.pallas_call(
        update_first,
        in_specs=[IN_SMEM] + [IN_VMEM] * 14,
        out_specs=[IN_VMEM] * 7,
        out_shape=[jax.ShapeDtypeStruct(*r) for r in rows]
        + gain_shapes
        + [jax.ShapeDtypeStruct(*m) for m in MESSAGES],
        compiler_params=pltpu.CompilerParams(vmem_limit_bytes=2 * 1024 * 1024),
        cost_estimate=cost,
    )(jnp.stack([core, half]), *squares, parts, *states, *gains)
    first_gains, sent = outs[:3], outs[3:]
    far = [send(sent[0], PARTNER), send(sent[1], OTHER_PARTNER)]
    outs = pl.pallas_call(
        update_second,
        in_specs=[IN_SMEM] + [IN_VMEM] * 18,
        out_specs=[IN_HBM] * 8 + [IN_VMEM] * 3,
        out_shape=shapes + gain_shapes,
        scratch_shapes=[pltpu.VMEM(*r) for r in rows + MESSAGES]
        + [pltpu.SemaphoreType.DMA((86,))],
        compiler_params=pltpu.CompilerParams(vmem_limit_bytes=8 * 1024 * 1024),
        cost_estimate=cost,
    )(jnp.stack([1 - core, half]), *squares, other, *states, *gains, keys, routers, *sent)
    outs, second_gains = outs[:8], outs[8:]
    far0, far1, gain_new = lax.optimization_barrier((*far, second_gains[0]))
    far, second_gains = [far0, far1], [gain_new, *second_gains[1:]]
    near = [send(a, SIBLING) for a in far]
    key_weight, router_weight, *gains, gain_weight = pl.pallas_call(
        write_received,
        in_specs=[IN_SMEM] + [IN_VMEM] * 10 + [IN_HBM] * 2,
        out_specs=[IN_HBM] * 2 + [IN_VMEM] * 4,
        out_shape=shapes[6:] + gain_shapes + [jax.ShapeDtypeStruct((16, LANES), jnp.bfloat16)],
        input_output_aliases={11: 0, 12: 1},
        scratch_shapes=[pltpu.SemaphoreType.DMA((32,))],
        compiler_params=pltpu.CompilerParams(vmem_limit_bytes=2 * 1024 * 1024),
    )(jnp.stack([core, half]), *far, *near, *first_gains, *second_gains, *outs[6:])
    return outs[:6], gains, key_weight, router_weight, gain_weight


def on_device(
    key_grads,
    router_grads,
    gain_grads,
    key_master,
    key_first,
    key_second,
    router_master,
    router_first,
    router_second,
    gain_master,
    gain_first,
    gain_second,
):
    core = lax.axis_index("c")
    half = lax.axis_index("xl")
    x = lax.axis_index("xh") * 2 + half
    y = lax.axis_index("y")
    z = lax.axis_index("z")
    grads = (key_grads[0, 0], router_grads[0, 0], gain_grads[0, 0])
    first_place = jnp.where(core == 0, x, y)
    second_place = jnp.where(core == 0, y, x)
    got = send(pack(1 - core, second_place, grads), SIBLING)
    kept = pack(core, first_place, grads)
    parts = in_vmem(add_pair, [kept, got], [((4, 8, 8, ROW), jnp.bfloat16)] * 4)
    states = [key_master, key_first, key_second, router_master, router_first, router_second]
    parts = [parts[0]] + [send(parts[k], along(k)) for k in (2, 1, 3)]
    [code] = in_vmem(sum_encoded, parts, [((32, 8, ROW), jnp.float32)], [z])
    code = lax.all_to_all(
        code.astype(jnp.float16), ALL, 0, 0, axis_index_groups=SECOND_GROUPS, tiled=True
    )
    [code] = in_vmem(encode, [code.astype(jnp.float32)], [((8, ROW), jnp.float32)], [z & 1])
    line = lax.all_to_all(
        jnp.broadcast_to(code.astype(jnp.float16)[None], (8, 8, ROW)), "z", 0, 0, tiled=True
    )
    line = jnp.broadcast_to(line[None], (8, 8, 8, ROW)).reshape(64, 8, ROW)
    parts = lax.all_to_all(line, ("y", "xh"), 0, 0, tiled=True)
    wide_parts = parts.astype(jnp.float32)
    [squares] = in_vmem(add_squares, [wide_parts], [((8, LANES), jnp.float32)])
    squares = [squares] + [send(squares, to) for to in (SIBLING, PARTNER, PARTNER_SIBLING)]
    parts, *squares = lax.optimization_barrier((parts, *squares))
    other = send(parts, SIBLING).astype(jnp.float32)
    states, gains, key_weight, router_weight, gain_weight = updated(
        core,
        half,
        squares,
        wide_parts,
        other,
        states,
        [gain.reshape(8, LANES) for gain in (gain_master, gain_first, gain_second)],
    )
    gains = [gain.reshape(1024) for gain in gains]
    return (*states, *gains, key_weight, router_weight, gain_weight.reshape(D))


def solution(mesh):
    fine = Mesh(np.asarray(mesh.devices).reshape(8, 4, 2, 2, 2), ("z", "y", "xh", "c", "xl"))
    in_specs = (
        P(WIDE, "xl", None, None, None),
        P(WIDE, "xl", None, None, None),
        P(WIDE, "xl", None, None),
        P("xl", None),
        P("xl", None),
        P("xl", None),
        P(None, "xl"),
        P(None, "xl"),
        P(None, "xl"),
        P("xl"),
        P("xl"),
        P("xl"),
    )
    out_specs = (
        P("xl", None),
        P("xl", None),
        P("xl", None),
        P(None, "xl"),
        P(None, "xl"),
        P(None, "xl"),
        P("xl"),
        P("xl"),
        P("xl"),
        P(),
        P(),
        P(),
    )
    return jax.shard_map(
        on_device, mesh=fine, in_specs=in_specs, out_specs=out_specs, check_vma=False
    )
```

```python
import math

import jax
import jax.numpy as jnp
import numpy as np
from jax import lax
from jax.experimental import pallas as pl
from jax.experimental.pallas import tpu as pltpu
from jax.sharding import Mesh
from jax.sharding import PartitionSpec as P

D = 2048
KEY_WIDTH = 512
EXPERTS = 64
LANES = 128
ROW = KEY_WIDTH + LANES

beta_one = 0.9
beta_two = 0.95
step_rate = 0.01
epsilon = 1e-08
bias_one = 1.0 - 0.9**10
bias_two = 1.0 - 0.95**10

WIDE = ("z", "y", "xh", "c")
ALL = ("z", "y", "xh", "c", "xl")


def place(z, y, x, c):
    return (((z * 4 + y) * 2 + x // 2) * 2 + c) * 2 + x % 2


def permutation(target):
    return [
        (place(z, y, x, c), place(*target(z, y, x, c)))
        for z in range(8)
        for y in range(4)
        for x in range(4)
        for c in range(2)
    ]


def along(stage, shift):
    def target(z, y, x, c):
        if c == stage:
            return z, y, x ^ shift, c
        return z, y ^ shift, x, c

    return permutation(target)


SIBLING = permutation(lambda z, y, x, c: (z, y, x, 1 - c))
PARTNER = permutation(lambda z, y, x, c: (z, y, x ^ 1, c))
OTHER_PARTNER = permutation(lambda z, y, x, c: (z, y, x ^ 3, c))
PARTNER_SIBLING = permutation(lambda z, y, x, c: (z, y, x ^ 1, 1 - c))


def send(x, pairs):
    return lax.ppermute(x, ALL, pairs)


def adamw(master, first_moment, second, scaled, decay_rate):
    first_new = beta_one * first_moment + (1.0 - beta_one) * scaled
    second_new = beta_two * second + (1.0 - beta_two) * scaled * scaled
    root = jnp.sqrt(second_new * (1.0 / bias_two)) + epsilon
    kept = master if decay_rate == 0.0 else master * (1.0 - step_rate * decay_rate)
    master_new = kept - first_new * (step_rate / bias_one) / root
    return (master_new, first_new, second_new)


def group_of(t, p, q):
    x = jnp.where(t == 0, p, q)
    y = jnp.where(t == 0, q, p)
    return x % 2, t * 8 + (x // 2) * 4 + y


def micro_total(stack):
    return (stack[0].astype(jnp.float32) + stack[1].astype(jnp.float32)).astype(jnp.bfloat16)


def pack_local(where_ref, key_ref, router_ref, gain_ref, out_ref, keys, routers, gains, tiles, sems):
    t, p = where_ref[0], where_ref[1]
    copies = []
    for i in range(16):
        half, group = group_of(t, p ^ (i // 4), i % 4)
        rows = pl.ds(pl.multiple_of((half * 16 + group) * 64, 64), 64)
        copies.append(pltpu.make_async_copy(key_ref.at[:, rows], keys.at[i], sems.at[i]))
        rows = pl.ds(pl.multiple_of(group // 2 * 8, 8), 8)
        columns = pl.ds(pl.multiple_of((half * 2 + group % 2) * 512, 512), 512)
        copies.append(
            pltpu.make_async_copy(
                router_ref.at[:, rows, columns], routers.at[i], sems.at[16 + i]
            )
        )
    gain_copy = pltpu.make_async_copy(gain_ref, gains, sems.at[32])
    gain_copy.start()
    for copy in copies:
        copy.start()
    lane = lax.broadcasted_iota(jnp.int32, (8, LANES), 1)
    row = lax.broadcasted_iota(jnp.int32, (8, LANES), 0)
    low = lane < 64
    gain_copy.wait()
    gain = gains[...].astype(jnp.float32)
    gain = (gain[0:1] + gain[1:2]).astype(jnp.bfloat16).astype(jnp.float32)
    for half in range(2):
        for z in range(8):
            at = half * 1024 + z * LANES
            line = gain[:, at : at + LANES]
            turned = jnp.concatenate([line[:, 64:], line[:, :64]], axis=1)
            tiles[half, z] = jnp.where(row == 0, line, jnp.where(row == 1, turned, 0.0))
    for i in range(16):
        half, group = group_of(t, p ^ (i // 4), i % 4)
        copies[2 * i].wait()
        copies[2 * i + 1].wait()
        key = keys[i, 0].astype(jnp.float32) + keys[i, 1].astype(jnp.float32)
        out_ref[i // 4, i % 4, :, :, :KEY_WIDTH] = key.astype(jnp.bfloat16).reshape(
            8, 8, KEY_WIDTH
        )
        router = routers[i, 0].astype(jnp.float32) + routers[i, 1].astype(jnp.float32)
        for z in range(8):
            tile = router[:, (z // 2) * LANES : (z // 2 + 1) * LANES]
            mine = low if z % 2 == 0 else jnp.logical_not(low)
            kept = jnp.where(group == 0, tiles[half, z], 0.0)
            out_ref[i // 4, i % 4, z, :, KEY_WIDTH:] = jnp.where(mine, tile, kept).astype(
                jnp.bfloat16
            )


def pack(t, p, grads):
    return pl.pallas_call(
        pack_local,
        in_specs=[pl.BlockSpec(memory_space=pltpu.SMEM)]
        + [pl.BlockSpec(memory_space=pltpu.HBM)] * 3,
        out_specs=pl.BlockSpec(memory_space=pltpu.VMEM),
        out_shape=jax.ShapeDtypeStruct((4, 4, 8, 8, ROW), jnp.bfloat16),
        scratch_shapes=[
            pltpu.VMEM((16, 2, 64, KEY_WIDTH), jnp.bfloat16),
            pltpu.VMEM((16, 2, 8, 512), jnp.bfloat16),
            pltpu.VMEM((2, D), jnp.bfloat16),
            pltpu.VMEM((2, 8, 8, LANES), jnp.float32),
            pltpu.SemaphoreType.DMA((33,)),
        ],
        compiler_params=pltpu.CompilerParams(vmem_limit_bytes=4 * 1024 * 1024),
    )(jnp.stack([t, p]), *[pltpu.with_memory_space_constraint(g, pltpu.HBM) for g in grads])


def in_vmem(body, operands, shapes, scalars=()):
    scalars = [jnp.stack(scalars)] if scalars else []
    return pl.pallas_call(
        body,
        in_specs=[pl.BlockSpec(memory_space=pltpu.SMEM)] * len(scalars)
        + [pl.BlockSpec(memory_space=pltpu.VMEM)] * len(operands),
        out_specs=[pl.BlockSpec(memory_space=pltpu.VMEM)] * len(shapes),
        out_shape=[jax.ShapeDtypeStruct(*shape) for shape in shapes],
        compiler_params=pltpu.CompilerParams(vmem_limit_bytes=2 * 1024 * 1024),
    )(*scalars, *operands)


def add_pair(kept_ref, got_ref, *outs):
    for k in range(4):
        for q in range(4):
            total = kept_ref[k, q].astype(jnp.float32) + got_ref[k, q].astype(jnp.float32)
            outs[k][q] = total.astype(jnp.bfloat16)


def spare_lanes(parity):
    lane = lax.broadcasted_iota(jnp.int32, (8, LANES), 1)
    return lane // 64 + parity == 1


def exponent_of(largest):
    largest = jnp.maximum(jnp.broadcast_to(largest, (8, LANES)), 1e-30)
    return jnp.floor(jnp.log(largest) * (1.0 / math.log(2.0))) - 13.0


def largest_of(x):
    return jnp.max(jnp.max(jnp.abs(x), axis=1, keepdims=True), axis=0, keepdims=True)


def add_rows(where_ref, *refs):
    terms, outs = refs[:4], refs[4:]
    for k in range(4):
        at = where_ref[0] ^ k
        total = terms[0][at].astype(jnp.float32)
        for term in terms[1:]:
            total = total + term[at].astype(jnp.float32)
        outs[k][...] = total


def sum_encoded(*refs):
    terms, out_ref = refs[:4], refs[4]
    largest = jnp.zeros((8, ROW), jnp.float32)
    for b in range(8):
        total = (terms[0][b] + terms[1][b]) + (terms[2][b] + terms[3][b])
        out_ref[b] = total
        largest = jnp.maximum(largest, jnp.abs(total))
    exponent = exponent_of(largest_of(largest))
    scale = jnp.concatenate([jnp.exp2(-exponent)] * 5, axis=1)
    row = lax.broadcasted_iota(jnp.int32, (8, LANES), 0)
    for b in range(8):
        own = out_ref[b] * scale
        spare = spare_lanes(b % 2) & (row == 7)
        out_ref[b, :, :KEY_WIDTH] = own[:, :KEY_WIDTH]
        out_ref[b, :, KEY_WIDTH:] = jnp.where(spare, exponent, own[:, KEY_WIDTH:])


def encode(where_ref, blocks_ref, out_ref):
    parity = where_ref[0]
    row = lax.broadcasted_iota(jnp.int32, (8, LANES), 0)
    own = jnp.zeros((8, ROW), jnp.float32)
    for b in range(8):
        block = blocks_ref[b]
        scale = scale_of(block[:, KEY_WIDTH:], parity)
        own = own + block * jnp.concatenate([scale] * 5, axis=1)
    spare = spare_lanes(parity) & (row >= 5)
    key, tile = own[:, :KEY_WIDTH], jnp.where(spare, 0.0, own[:, KEY_WIDTH:])
    own = jnp.concatenate([key, tile], axis=1)
    exponent = exponent_of(largest_of(own))
    own = own * jnp.concatenate([jnp.exp2(-exponent)] * 5, axis=1)
    squares = jnp.sum(jnp.sum(own * own, axis=1, keepdims=True), axis=0, keepdims=True)
    squares = jnp.broadcast_to(squares, (8, LANES)) * 2.0**-30
    digit = squares.astype(jnp.bfloat16).astype(jnp.float32)
    notes = jnp.where(row == 7, exponent, jnp.where(row == 6, digit, (squares - digit) * 256.0))
    out_ref[:, :KEY_WIDTH] = own[:, :KEY_WIDTH]
    out_ref[:, KEY_WIDTH:] = jnp.where(spare, notes, own[:, KEY_WIDTH:])


def add_squares(blocks_ref, out_ref):
    totals = [jnp.zeros((1, LANES), jnp.float32)] * 2
    for b in range(64):
        tile = blocks_ref[b, :, KEY_WIDTH:]
        digits = tile[6:7] + tile[5:6] * (1.0 / 256.0)
        totals[b % 2] = totals[b % 2] + digits * jnp.exp2(2.0 * tile[7:8] + 30.0)
    lane = lax.broadcasted_iota(jnp.int32, (1, LANES), 1)
    total = jnp.where(lane == 64, totals[0], 0.0) + jnp.where(lane == 0, totals[1], 0.0)
    out_ref[...] = jnp.broadcast_to(jnp.sum(total, axis=1, keepdims=True), (8, LANES))


def scale_of(tile, parity):
    line = tile[7:8]
    turned = jnp.concatenate([line[:, 64:], line[:, :64]], axis=1)
    lane = lax.broadcasted_iota(jnp.int32, (1, LANES), 1)
    line = jnp.where(lane // 64 + parity == 1, line, turned)
    return jnp.exp2(jnp.broadcast_to(line, (8, LANES)))


def gain_line(tile, z):
    first, second = tile[0:1], tile[1:2]
    turned = jnp.concatenate([second[:, 64:], second[:, :64]], axis=1)
    lane = lax.broadcasted_iota(jnp.int32, (1, LANES), 1)
    if z % 2 == 0:
        return jnp.where(lane < 64, turned, first)
    return jnp.where(lane < 64, first, turned)


def clip_factor(squares):
    total = (squares[0][...] + squares[1][...]) + (squares[2][...] + squares[3][...])
    clip_limit = 0.5 * math.sqrt(D * KEY_WIDTH + EXPERTS * D + D)
    return clip_limit / jnp.maximum(jnp.sqrt(total), clip_limit)


def update_rows(where_ref, squares, blocks_ref, ins, outs, after_group=None):
    t = where_ref[0]
    factor = clip_factor(squares)
    key_ins, router_ins, gain_ins = ins[:3], ins[3:6], ins[6:]
    keys, routers, gain_outs, messages = outs[0], outs[1], outs[2:5], outs[5:]
    low = lax.broadcasted_iota(jnp.int32, (8, LANES), 1) < 64
    row = lax.broadcasted_iota(jnp.int32, (8, LANES), 0)
    scaled = jnp.zeros((8, LANES), jnp.float32)
    for z in range(8):
        tile = blocks_ref[z, :, KEY_WIDTH:]
        scaled = jnp.where(row == z, gain_line(tile * (scale_of(tile, z % 2) * factor), z), scaled)
    new = adamw(*[gain[...] for gain in gain_ins], scaled, 0.0)
    for a in range(3):
        gain_outs[a][...] = new[a]
    messages[0][pl.ds(288, 8), :LANES] = new[0].astype(jnp.bfloat16)
    for g in range(8):
        message, at = messages[g // 4], g % 4
        tiles = []
        for z in range(8):
            b = (g % 4 * 2 + g // 4) * 8 + z
            tile = blocks_ref[b, :, KEY_WIDTH:]
            scale = scale_of(tile, z % 2) * factor
            tiles.append(tile * scale)
            scaled = blocks_ref[b, :, :KEY_WIDTH] * jnp.concatenate([scale] * 4, axis=1)
            rows = pl.ds(g * 64 + z * 8, 8)
            old = pl.ds(pl.multiple_of(t * 512 + g * 64 + z * 8, 8), 8)
            new = adamw(*[key[old] for key in key_ins], scaled, 0.1)
            for a in range(3):
                keys[a, rows] = new[a]
            message[pl.ds(at * 64 + z * 8, 8)] = new[0].astype(jnp.bfloat16)
        scaled = jnp.concatenate(
            [jnp.where(low, tiles[2 * i], tiles[2 * i + 1]) for i in range(4)], axis=1
        )
        rows, columns = pl.ds(g // 2 * 8, 8), pl.ds(g % 2 * 512, 512)
        old = pl.ds(pl.multiple_of(t * 32 + g // 2 * 8, 8), 8)
        new = adamw(*[router[old, columns] for router in router_ins], scaled, 0.1)
        for a in range(3):
            routers[a, rows, columns] = new[a]
        message[pl.ds(256 + at * 8, 8)] = new[0].astype(jnp.bfloat16)
        if after_group is not None:
            after_group(g)


class Stores:
    def __init__(self, sems):
        self.sems, self.copies = sems, []

    def __call__(self, source, target):
        copy = pltpu.make_async_copy(source, target, self.sems.at[len(self.copies)])
        copy.start()
        self.copies.append(copy)

    def wait(self):
        for copy in self.copies:
            copy.wait()


def store_weights(store, t, half, g, message, key_weight, router_weight):
    rows = pl.ds(pl.multiple_of(half * 1024 + t * 512 + g * 64, 64), 64)
    store(message.at[pl.ds(g % 4 * 64, 64)], key_weight.at[rows])
    rows = pl.ds(pl.multiple_of(t * 32 + g // 2 * 8, 8), 8)
    columns = pl.ds(pl.multiple_of(half * 1024 + g % 2 * 512, 512), 512)
    store(message.at[pl.ds(256 + g % 4 * 8, 8)], router_weight.at[rows, columns])


def store_group(store, t, half, g, keys, message, outs):
    rows = pl.ds(pl.multiple_of(t * 512 + g * 64, 64), 64)
    for a in range(3):
        store(keys.at[a, pl.ds(g * 64, 64)], outs[a].at[rows])
    store_weights(store, t, half, g, message, outs[6], outs[7])


def store_routers(store, t, routers, outs):
    rows = pl.ds(pl.multiple_of(t * 32, 32), 32)
    for a in range(3):
        store(routers.at[a], outs[3 + a].at[rows])


def update_first(where_ref, *refs):
    update_rows(where_ref, refs[:4], refs[4], refs[5:14], refs[14:])


def update_second(where_ref, *refs):
    squares, blocks_ref, ins, first = refs[:4], refs[4], refs[5:14], refs[14:18]
    outs, gains, scratch = refs[18:26], refs[26:29], refs[29:]
    keys, routers, messages, sems = scratch[0], scratch[1], scratch[2:4], scratch[4]
    t, half = where_ref[0], where_ref[1]
    store = Stores(sems)
    for g in range(8):
        store_group(store, 1 - t, half, g, first[0], first[2 + g // 4], outs)
    store_routers(store, 1 - t, first[1], outs)
    update_rows(
        where_ref,
        squares,
        blocks_ref,
        ins,
        (keys, routers, *gains, *messages),
        lambda g: store_group(store, t, half, g, keys, messages[g // 4], outs),
    )
    store_routers(store, t, routers, outs)
    store.wait()


def write_received(where_ref, far0, far1, near0, near1, *refs):
    first_gains, second_gains = refs[:3], refs[3:6]
    key_weight, router_weight, gain_outs, gain_weight, sems = *refs[8:10], refs[10:13], *refs[13:]
    t, half = where_ref[0], where_ref[1]
    store = Stores(sems)
    for g in range(8):
        store_weights(store, t, 1 - half, g, (far0, far1)[g // 4], key_weight, router_weight)
        store_weights(store, 1 - t, 1 - half, g, (near0, near1)[g // 4], key_weight, router_weight)
    for a in range(3):
        gain_outs[a][...] = jnp.where(t == 0, first_gains[a][...], second_gains[a][...])
    rows = pl.ds(288, 8)
    far, near = far0[rows, :LANES].astype(jnp.float32), near0[rows, :LANES].astype(jnp.float32)
    far = jnp.where(t == 0, far, near)
    mine = jnp.where(t == 0, first_gains[0][...], second_gains[0][...])
    gain_weight[:8] = jnp.where(half == 0, mine, far).astype(jnp.bfloat16)
    gain_weight[8:] = jnp.where(half == 0, far, mine).astype(jnp.bfloat16)
    store.wait()


IN_VMEM = pl.BlockSpec(memory_space=pltpu.VMEM)
IN_HBM = pl.BlockSpec(memory_space=pltpu.HBM)
IN_SMEM = pl.BlockSpec(memory_space=pltpu.SMEM)
MESSAGES = [((296, KEY_WIDTH), jnp.bfloat16), ((288, KEY_WIDTH), jnp.bfloat16)]


def in_hbm(arrays):
    return [pltpu.with_memory_space_constraint(a, pltpu.HBM) for a in arrays]


def updated(core, half, squares, parts, other, states, gains):
    shapes = [jax.ShapeDtypeStruct(a.shape, jnp.float32) for a in states]
    shapes += [
        jax.ShapeDtypeStruct((D, KEY_WIDTH), jnp.bfloat16),
        jax.ShapeDtypeStruct((EXPERTS, D), jnp.bfloat16),
    ]
    gain_shapes = [jax.ShapeDtypeStruct((8, LANES), jnp.float32)] * 3
    rows = [((3, 512, KEY_WIDTH), jnp.float32), ((3, 32, 1024), jnp.float32)]
    cost = pl.CostEstimate(flops=7_000_000, bytes_accessed=8_000_000, transcendentals=600_000)
    keys, routers, *outs = pl.pallas_call(
        update_first,
        in_specs=[IN_SMEM] + [IN_VMEM] * 14,
        out_specs=[IN_VMEM] * 7,
        out_shape=[jax.ShapeDtypeStruct(*r) for r in rows]
        + gain_shapes
        + [jax.ShapeDtypeStruct(*m) for m in MESSAGES],
        compiler_params=pltpu.CompilerParams(vmem_limit_bytes=2 * 1024 * 1024),
        cost_estimate=cost,
    )(jnp.stack([core, half]), *squares, parts, *states, *gains)
    first_gains, sent = outs[:3], outs[3:]
    far = [send(sent[0], PARTNER), send(sent[1], OTHER_PARTNER)]
    outs = pl.pallas_call(
        update_second,
        in_specs=[IN_SMEM] + [IN_VMEM] * 18,
        out_specs=[IN_HBM] * 8 + [IN_VMEM] * 3,
        out_shape=shapes + gain_shapes,
        scratch_shapes=[pltpu.VMEM(*r) for r in rows + MESSAGES]
        + [pltpu.SemaphoreType.DMA((86,))],
        compiler_params=pltpu.CompilerParams(vmem_limit_bytes=8 * 1024 * 1024),
        cost_estimate=cost,
    )(jnp.stack([1 - core, half]), *squares, other, *states, *gains, keys, routers, *sent)
    outs, second_gains = outs[:8], outs[8:]
    far0, far1, gain_new = lax.optimization_barrier((*far, second_gains[0]))
    far, second_gains = [far0, far1], [gain_new, *second_gains[1:]]
    near = [send(a, SIBLING) for a in far]
    key_weight, router_weight, *gains, gain_weight = pl.pallas_call(
        write_received,
        in_specs=[IN_SMEM] + [IN_VMEM] * 10 + [IN_HBM] * 2,
        out_specs=[IN_HBM] * 2 + [IN_VMEM] * 4,
        out_shape=shapes[6:] + gain_shapes + [jax.ShapeDtypeStruct((16, LANES), jnp.bfloat16)],
        input_output_aliases={11: 0, 12: 1},
        scratch_shapes=[pltpu.SemaphoreType.DMA((32,))],
        compiler_params=pltpu.CompilerParams(vmem_limit_bytes=2 * 1024 * 1024),
    )(jnp.stack([core, half]), *far, *near, *first_gains, *second_gains, *outs[6:])
    return outs[:6], gains, key_weight, router_weight, gain_weight


def on_device(
    key_grads,
    router_grads,
    gain_grads,
    key_master,
    key_first,
    key_second,
    router_master,
    router_first,
    router_second,
    gain_master,
    gain_first,
    gain_second,
):
    core = lax.axis_index("c")
    half = lax.axis_index("xl")
    x = lax.axis_index("xh") * 2 + half
    y = lax.axis_index("y")
    z = lax.axis_index("z")
    grads = (key_grads[0, 0], router_grads[0, 0], gain_grads[0, 0])
    first_place = jnp.where(core == 0, x, y)
    second_place = jnp.where(core == 0, y, x)
    got = send(pack(1 - core, second_place, grads), SIBLING)
    kept = pack(core, first_place, grads)
    parts = in_vmem(add_pair, [kept, got], [((4, 8, 8, ROW), jnp.bfloat16)] * 4)
    states = [key_master, key_first, key_second, router_master, router_first, router_second]
    parts = [parts[0]] + [send(parts[k], along(0, k)) for k in (2, 1, 3)]
    parts = in_vmem(add_rows, parts, [((8, 8, ROW), jnp.float32)] * 4, [second_place])
    parts = [parts[0]] + [send(parts[k], along(1, k)) for k in (2, 1, 3)]
    [code] = in_vmem(sum_encoded, parts, [((8, 8, ROW), jnp.float32)])
    code = lax.all_to_all(code.astype(jnp.float16), "z", 0, 0, tiled=True)
    [code] = in_vmem(encode, [code.astype(jnp.float32)], [((8, ROW), jnp.float32)], [z & 1])
    line = lax.all_to_all(
        jnp.broadcast_to(code.astype(jnp.float16)[None], (8, 8, ROW)), "z", 0, 0, tiled=True
    )
    line = jnp.broadcast_to(line[None], (8, 8, 8, ROW)).reshape(64, 8, ROW)
    parts = lax.all_to_all(line, ("y", "xh"), 0, 0, tiled=True)
    wide_parts = parts.astype(jnp.float32)
    [squares] = in_vmem(add_squares, [wide_parts], [((8, LANES), jnp.float32)])
    squares = [squares] + [send(squares, to) for to in (SIBLING, PARTNER, PARTNER_SIBLING)]
    parts, *squares = lax.optimization_barrier((parts, *squares))
    other = send(parts, SIBLING).astype(jnp.float32)
    states, gains, key_weight, router_weight, gain_weight = updated(
        core,
        half,
        squares,
        wide_parts,
        other,
        states,
        [gain.reshape(8, LANES) for gain in (gain_master, gain_first, gain_second)],
    )
    gains = [gain.reshape(1024) for gain in gains]
    return (*states, *gains, key_weight, router_weight, gain_weight.reshape(D))


def solution(mesh):
    fine = Mesh(np.asarray(mesh.devices).reshape(8, 4, 2, 2, 2), ("z", "y", "xh", "c", "xl"))
    in_specs = (
        P(WIDE, "xl", None, None, None),
        P(WIDE, "xl", None, None, None),
        P(WIDE, "xl", None, None),
        P("xl", None),
        P("xl", None),
        P("xl", None),
        P(None, "xl"),
        P(None, "xl"),
        P(None, "xl"),
        P("xl"),
        P("xl"),
        P("xl"),
    )
    out_specs = (
        P("xl", None),
        P("xl", None),
        P("xl", None),
        P(None, "xl"),
        P(None, "xl"),
        P(None, "xl"),
        P("xl"),
        P("xl"),
        P("xl"),
        P(),
        P(),
        P(),
    )
    return jax.shard_map(
        on_device, mesh=fine, in_specs=in_specs, out_specs=out_specs, check_vma=False
    )
```
